256 devices in a mesh: dp: 2 (over x_hi), tm: 16 (over z, x_lo), mp: 8 (over y, core).
Axes of the slice: x: 4 (x_hi: 2, x_lo: 2; x = x_hi * 2 + x_lo), y: 4, z: 8, core: 2. Of those that a mesh axis runs over, the one named last changes fastest.
Arguments:
- features: bfloat16 [128, 576, 1024], P(('dp', 'tm'), 'mp'), parts along dimension 0, may hold values from -6 to 6
- queries: bfloat16 [8192, 1024], P(('dp', 'tm')), parts along dimension 0, may hold values from -6 to 6
- anchor_frame: int32 [8192], P(('dp', 'tm')), parts along dimension 0, may hold values from 0 to 63, as said below
- anchor_patch: int32 [8192], P(('dp', 'tm')), parts along dimension 0, may hold values from 0 to 575
- time_offset: float32 [8192, 8, 4], P(('dp', 'tm')), parts along dimension 0, may hold values from -1.99 to 1.99
- space_offset: float32 [2, 8192, 8, 4], P(None, ('dp', 'tm')), parts along dimension 1, may hold values from -3 to 3
- value_weight: bfloat16 [1024, 1024], replicated, may hold values from -0.1875 to 0.1875
- point_weight: bfloat16 [1024, 32], replicated, may hold values from -0.1875 to 0.1875
- point_bias: float32 [32], replicated, may hold values from -6 to 260
- output_weight: bfloat16 [1024, 1024], P('mp'), may hold values from -0.1875 to 0.1875
- project_weight: bfloat16 [1024, 3584], P(None, 'mp'), may hold values from -2 to 2
- norm_gain: float32 [3584], P('mp'), may hold values from 0.1 to 1.9
- query_weight: bfloat16 [3584, 3072], P(None, 'mp'), may hold values from -0.09375 to 0.09375
- query_bias: float32 [3072], P('mp'), may hold values from -6 to 40
- cache_weight: bfloat16 [3584, 1024], P(None, 'mp'), may hold values from -0.09375 to 0.09375
- cache_bias: float32 [1024], P('mp'), may hold values from -6 to 40
Outputs:
- attention: bfloat16 [8192, 3072], P(('dp', 'tm'), 'mp'), parts along dimension 0
- key_value: bfloat16 [8192, 1024], P(('dp', 'tm'), 'mp'), parts along dimension 0
The draws below stay inside these ranges and needn't reach their ends.
There are 2 independent parts, one for each index of `dp`. The reference program is written for one: setup_inputs(seed, part) draws one part's arguments, and reference() takes and returns one part's arrays. A program takes and returns all parts, laid end to end along the dimension named above; an argument that names none is the same for every part. Nothing has to cross between parts.
Inputs may be any that keep to these rules, and one draw needn't show every extreme that they name: `anchor_frame`: the anchor frame of query q lies among the 4 frames that begin at (q // 256) * 4.
All inputs are finite; a program needn't handle non-finite values.
Results may differ from the reference program's by a relative error of at most 0.04.
Values may be sent and summed in bfloat16 or wider, within the bound.
No kernel may reach another device: no remote copies, remote signals or barrier semaphores. Data moves between devices by JAX's collectives and lax.ppermute only.
A program may use at most 64 MiB of HBM per device.

```python
import math
import jax
import jax.numpy as jnp
from jax import lax

C = 1024
AH = 8
AHD = 128
POINTS = 4
GRID = 24
PATCH = 576
D = 3584
HEADS = 24
KVH = 4
HD = 128
GROUP = 7
FR_DEV = 4
Q_DEV = 256
FRAMES = 64
QUERIES = 4096


def draw_queries(key, part):
    normal_part = jnp.clip(jax.random.normal(key, (QUERIES, C), jnp.float32), -6.0, 6.0)
    normal_part = normal_part * 0.3
    return normal_part.astype(jnp.bfloat16)


def draw_anchor_frame(key, part):
    position = jnp.arange(QUERIES, dtype=jnp.int32)
    within = jax.random.randint(key, (QUERIES,), 0, FR_DEV, dtype=jnp.int32)
    return position // Q_DEV * FR_DEV + within


def draw_point_bias(key, part):
    normal_part = jnp.clip(jax.random.normal(key, (AH, POINTS), jnp.float32), -6.0, 6.0)
    return normal_part.reshape(AH * POINTS)


def draw_project_weight(key, part):
    normal_part = jnp.clip(jax.random.normal(key, (C, D), jnp.float32), -6.0, 6.0) / math.sqrt(C)
    column_scale = 1.0 + 4.0 * jnp.arange(D, dtype=jnp.float32) / D
    return jnp.clip(normal_part * column_scale[None, :], -2.0, 2.0).astype(jnp.bfloat16)


def draw_query_bias(key, part):
    normal_part = jnp.clip(jax.random.normal(jax.random.fold_in(key, 1), (HEADS, HD), jnp.float32), -6.0, 6.0)
    return normal_part.reshape(HEADS * HD)


def draw_cache_bias(key, part):
    normal_part = jnp.clip(jax.random.normal(jax.random.fold_in(key, 2), (2 * KVH, HD), jnp.float32), -6.0, 6.0)
    return normal_part.reshape(2 * KVH * HD)


def touch_ends(entries, rng, least, largest):
    place = [jax.random.randint(jax.random.fold_in(rng, axis), (), 0, length) for axis, length in enumerate(entries.shape)]
    longest = entries.shape.index(max(entries.shape))
    beside = place[:longest] + [(place[longest] + 1) % entries.shape[longest]] + place[longest + 1:]
    return entries.at[tuple(place)].set(least).at[tuple(beside)].set(largest)


def block_levels(own_key, extent, shards, low, top_value):
    loudness, own = 1.0, jax.random.fold_in(own_key, 6)
    for dim, blocks in shards:
        steps = jnp.exp(jax.random.uniform(jax.random.fold_in(own, dim), (blocks,), jnp.float32, low / len(shards), top_value / len(shards)))
        loudness = loudness * jnp.repeat(steps, extent[dim] // blocks).reshape([-1 if axis == dim else 1 for axis in range(len(extent))])
    return loudness


def gaussian(key, shape, width, most, split=(), kind=jnp.bfloat16):
    values = jax.random.normal(key, shape, jnp.float32) * width
    if len(split) > 0:
        values = block_levels(key, shape, split, -0.22, 0.18) * values
    return jnp.clip(values, min=-most, max=most).astype(kind)


def setup_inputs(seed: int = 0, part: int = 0) -> dict:
    seeds = jax.random.split(jax.random.key(seed), 17)
    part_splits = jax.random.split(jax.random.fold_in(seeds[16], part), 17)
    return {
        "features": gaussian(part_splits[0], (FRAMES, PATCH, C), 1.0, 6.0, ((0, 16), (1, 8))),
        "queries": draw_queries(jax.random.fold_in(jax.random.fold_in(seeds[16], part), 71), part),
        "anchor_frame": draw_anchor_frame(jax.random.fold_in(jax.random.fold_in(seeds[16], part), 71), part),
        "anchor_patch": touch_ends(jax.random.randint(part_splits[3], (QUERIES,), 0, PATCH), jax.random.fold_in(part_splits[3], 1), 0, PATCH - 1).astype(jnp.int32),
        "time_offset": jnp.clip(jax.random.uniform(part_splits[4], (QUERIES, AH, POINTS), jnp.float32, -1.99, 1.99) * block_levels(part_splits[4], (QUERIES, AH, POINTS), ((0, 16),), -0.4, 0.0), -1.99, 1.99),
        "space_offset": jnp.clip(jax.random.uniform(part_splits[5], (2, QUERIES, AH, POINTS), jnp.float32, -3.0, 3.0) * block_levels(part_splits[5], (2, QUERIES, AH, POINTS), ((1, 16),), -0.4, 0.0), -3.0, 3.0),
        "value_weight": gaussian(seeds[6], (C, C), C ** -0.5, 0.1875),
        "point_weight": gaussian(seeds[7], (C, AH * POINTS), C ** -0.5, 0.1875),
        "point_bias": draw_point_bias(jax.random.fold_in(seeds[16], 71), part),
        "output_weight": gaussian(seeds[9], (C, C), C ** -0.5, 0.1875, ((0, 8),)),
        "project_weight": draw_project_weight(jax.random.fold_in(seeds[16], 71), part),
        "norm_gain": jnp.clip(1.0 + 0.18 * jax.random.normal(seeds[11], (D,), jnp.float32), 0.1, 1.9),
        "query_weight": gaussian(seeds[12], (D, HEADS * HD), D ** -0.5, 0.09375, ((1, 8),)),
        "query_bias": draw_query_bias(jax.random.fold_in(seeds[16], 71), part),
        "cache_weight": gaussian(seeds[14], (D, 2 * KVH * HD), D ** -0.5, 0.09375, ((1, 8),)),
        "cache_bias": draw_cache_bias(jax.random.fold_in(seeds[16], 71), part),
    }


rope_base = 1000000.0
epsilon = 1e-06
masked = -1e+30

def rotate(vectors, positions):
    half_width = vectors.shape[-1] // 2
    frequency = rope_base ** (-2.0 * jnp.arange(half_width, dtype=jnp.float32) / vectors.shape[-1])
    angles = positions.astype(jnp.float32)[:, None] * frequency[None, :]
    cosine = jnp.cos(angles)[:, None, :]
    sine_part = jnp.sin(angles)[:, None, :]
    first_half = vectors[..., :half_width]
    second_half = vectors[..., half_width:]
    return jnp.concatenate([first_half * cosine - second_half * sine_part, second_half * cosine + first_half * sine_part], axis=-1)

def trilinear_corners(frame_pos, row_pos, column_pos, weight, frame_total, side):
    floor_frame = jnp.floor(frame_pos)
    floor_row = jnp.floor(row_pos)
    floor_column = jnp.floor(column_pos)
    frame_part = frame_pos - floor_frame
    row_part = row_pos - floor_row
    column_part = column_pos - floor_column
    frame_start = floor_frame.astype(jnp.int32)
    row_start = floor_row.astype(jnp.int32)
    column_start = floor_column.astype(jnp.int32)
    listing = []
    for frame_step in (0, 1):
        for row_step in (0, 1):
            for column_step in (0, 1):
                frame_cell = frame_start + frame_step
                row_cell = row_start + row_step
                column_cell = column_start + column_step
                portion = weight * (frame_part if frame_step else 1.0 - frame_part)
                portion = portion * (row_part if row_step else 1.0 - row_part)
                portion = portion * (column_part if column_step else 1.0 - column_part)
                inside = (frame_cell >= 0) & (frame_cell < frame_total) & (row_cell >= 0) & (row_cell < side)
                inside = inside & (column_cell >= 0) & (column_cell < side)
                portion = jnp.where(inside, portion, 0.0)
                patch_id = jnp.clip(row_cell, 0, side - 1) * side + jnp.clip(column_cell, 0, side - 1)
                listing.append((frame_cell, patch_id.astype(jnp.int32), portion))
    return listing

def reference(features, queries, anchor_frame, anchor_patch, time_offset, space_offset, value_weight, point_weight, point_bias, output_weight, project_weight, norm_gain, query_weight, query_bias, cache_weight, cache_bias):
    patch_values = jnp.dot(features.reshape(FRAMES * PATCH, C), value_weight, preferred_element_type=jnp.float32).astype(jnp.bfloat16)
    by_head = patch_values.reshape(FRAMES * PATCH, AH, AHD).transpose(1, 0, 2)
    logits = jnp.dot(queries, point_weight, preferred_element_type=jnp.float32) + point_bias
    point_share = jax.nn.softmax(logits.reshape(QUERIES, AH, POINTS), axis=-1)
    frame_pos = anchor_frame.astype(jnp.float32)[:, None, None] + time_offset
    row_pos = (anchor_patch // GRID).astype(jnp.float32)[:, None, None] + space_offset[0]
    column_pos = (anchor_patch % GRID).astype(jnp.float32)[:, None, None] + space_offset[1]

    def sample_head(inputs):
        lookup, frame_head, row_head, column_head, share_head = inputs
        running = jnp.zeros((QUERIES, AHD), jnp.float32)
        for frame_cell, patch_id, portion in trilinear_corners(frame_head, row_head, column_head, share_head, FRAMES, GRID):
            picked = lookup[jnp.clip(frame_cell, 0, FRAMES - 1) * PATCH + patch_id]
            running = running + lax.optimization_barrier(jnp.sum(portion[..., None] * picked.astype(jnp.float32), axis=1))
        return running
    sampled = lax.map(sample_head, (by_head, frame_pos.transpose(1, 0, 2), row_pos.transpose(1, 0, 2), column_pos.transpose(1, 0, 2), point_share.transpose(1, 0, 2)))
    sampled = sampled.transpose(1, 0, 2).reshape(QUERIES, C).astype(jnp.bfloat16)
    abstract = (queries.astype(jnp.float32) + jnp.dot(sampled, output_weight, preferred_element_type=jnp.float32)).astype(jnp.bfloat16)
    visual = jnp.dot(abstract, project_weight, preferred_element_type=jnp.float32)
    normed = (visual * lax.rsqrt(lax.optimization_barrier(jnp.mean(visual * visual, axis=1, keepdims=True)) + epsilon) * norm_gain).astype(jnp.bfloat16)
    positions = jnp.arange(QUERIES, dtype=jnp.int32)
    query_state = (jnp.dot(normed, query_weight, preferred_element_type=jnp.float32) + query_bias).reshape(QUERIES, HEADS, HD)
    query_state = rotate(query_state, positions).astype(jnp.bfloat16)
    cache_state = (jnp.dot(normed, cache_weight, preferred_element_type=jnp.float32) + cache_bias).reshape(QUERIES, 2 * KVH, HD)
    cache_state = jnp.concatenate([rotate(cache_state[:, :KVH], positions), cache_state[:, KVH:]], axis=1)
    key_value = cache_state.reshape(QUERIES, 2 * KVH * HD).astype(jnp.bfloat16)
    key_heads = key_value.reshape(QUERIES, 2 * KVH, HD).transpose(1, 0, 2)
    query_heads = query_state.transpose(1, 0, 2)
    allowed = positions[None, :] <= positions[:, None]

    def attend_head(head_id):
        group_id = head_id // GROUP
        scores = jnp.dot(query_heads[head_id], key_heads[group_id].T, preferred_element_type=jnp.float32) * HD ** (-0.5)
        scores = jnp.where(allowed, scores, masked)
        row_peak = lax.optimization_barrier(jnp.max(scores, axis=1, keepdims=True))
        weights = jnp.where(allowed, jnp.exp(scores - row_peak), 0.0)
        weighted = jnp.dot(weights.astype(jnp.bfloat16), key_heads[KVH + group_id], preferred_element_type=jnp.float32)
        return weighted / lax.optimization_barrier(jnp.sum(weights, axis=1, keepdims=True))
    attention = lax.map(attend_head, jnp.arange(HEADS, dtype=jnp.int32))
    attention = attention.transpose(1, 0, 2).reshape(QUERIES, HEADS * HD).astype(jnp.bfloat16)
    return (attention, key_value)
```

```python
import jax
import jax.numpy as jnp
from jax import lax
from jax.experimental import pallas as pl
from jax.experimental.pallas import tpu as pltpu
from jax.sharding import Mesh
from jax.sharding import PartitionSpec as P

AH = 8
AHD = 128
POINTS = 4
GRID = 24
KVH = 4
HD = 128
GROUP = 7
PARTS = 8
RING = 8
TM = ("tz", "tx")
MP = ("my", "mc")

rope_base = 1000000.0
epsilon = 1e-06
masked = -1e30
MIB = 1 << 20

f32 = jnp.float32
bf16 = jnp.bfloat16


def part_index():
    return lax.axis_index("my") * 2 + lax.axis_index("mc")


def time_index():
    return lax.axis_index("tz") * 2 + lax.axis_index("tx")


def gathered_source(place):
    step, other = place // 2, place % 2
    row = lax.rem(lax.axis_index("my") - step + 4, 4)
    core = lax.axis_index("mc")
    return row * 2 + (1 - core if other else core)


def turned(size, step):
    return [(i, (i + step) % size) for i in range(size)]


def gather_blocks(x):
    columns = [x] + [lax.ppermute(x, "my", turned(4, step)) for step in (1, 2, 3)]
    blocks = []
    for block in columns:
        blocks += [block, lax.ppermute(block, "mc", turned(2, 1))]
    return blocks


def dot(a, b):
    return jnp.dot(a, b, preferred_element_type=f32)


def params(mib, flops=0, read=0):
    return dict(
        compiler_params=pltpu.CompilerParams(vmem_limit_bytes=mib * MIB),
        cost_estimate=pl.CostEstimate(flops=flops, bytes_accessed=read, transcendentals=0),
    )


def vmem(count):
    return [pl.BlockSpec(memory_space=pltpu.VMEM)] * count


def project_kernel(features_ref, weight_ref, *refs):
    outs, held = refs[:PARTS], refs[PARTS]
    features = features_ref[...]
    for pair in range(PARTS // 2):
        both = dot(features, weight_ref[:, pair * 256 : pair * 256 + 256]).astype(bf16)
        held[2 * pair] = both[:, :AHD]
        held[2 * pair + 1] = both[:, AHD:]
    part = part_index()
    for step in range(PARTS):
        outs[step][...] = held[lax.rem(part + step, PARTS)]


def project_values(features, weight):
    rows = features.shape[0]
    return pl.pallas_call(
        project_kernel,
        out_shape=[jax.ShapeDtypeStruct((rows, AHD), bf16)] * PARTS,
        in_specs=vmem(2),
        out_specs=vmem(PARTS),
        scratch_shapes=[pltpu.VMEM((PARTS, rows, AHD), bf16)],
        name="project_values",
        **params(16, 2 * rows * weight.size, 2 * (features.size * 2 + weight.size)),
    )(features, weight)


def hat(distance):
    return jnp.maximum(1.0 - jnp.abs(distance), 0.0)


def sample_kernel(frames, rows_each, place_ref, *refs):
    values, out_ref, spread, stacked = refs[:PARTS], refs[PARTS], refs[PARTS + 1], refs[PARTS + 2]
    count = place_ref.shape[1]
    block = frames * rows_each * GRID
    part = part_index()
    first = (time_index() * frames).astype(f32)
    cell = lax.broadcasted_iota(jnp.int32, (GRID, count), 0).astype(f32)
    frame_at = [place_ref[k : k + 1, :] for k in range(POINTS)]
    row_at = [place_ref[POINTS + k : POINTS + k + 1, :] for k in range(POINTS)]
    share = [place_ref[3 * POINTS + k : 3 * POINTS + k + 1, :] for k in range(POINTS)]
    column_hat = [
        hat(cell - place_ref[2 * POINTS + k : 2 * POINTS + k + 1, :]) for k in range(POINTS)
    ]
    frame_hat = [
        [share[k] * hat(first + float(f) - frame_at[k]) for k in range(POINTS)]
        for f in range(frames)
    ]
    for step in range(PARTS):
        source = lax.rem(part - step + PARTS, PARTS)
        top = source * rows_each
        row_hat = [
            [hat((top + r).astype(f32) - row_at[k]) for k in range(POINTS)]
            for r in range(rows_each)
        ]
        pieces = []
        for f in range(frames):
            for r in range(rows_each):
                total = (frame_hat[f][0] * row_hat[r][0]) * column_hat[0]
                for k in range(1, POINTS):
                    total = total + (frame_hat[f][k] * row_hat[r][k]) * column_hat[k]
                pieces.append(total)
        spread[step * block : (step + 1) * block, :] = jnp.concatenate(pieces, axis=0).astype(bf16)
        stacked[step * block : (step + 1) * block, :] = values[step][...]
    turned_values = stacked[...].T
    for lo in range(0, count, 256):
        out = dot(turned_values, spread[:, lo : lo + 256])
        out_ref[lo : lo + 256, :] = out.T.astype(out_ref.dtype)


def sample(values, place, frames, kind):
    rows, width = values[0].shape
    count = place.shape[1]
    rows_each = GRID // PARTS
    return pl.pallas_call(
        lambda *refs: sample_kernel(frames, rows_each, *refs),
        out_shape=jax.ShapeDtypeStruct((count, width), kind),
        in_specs=vmem(1 + PARTS),
        out_specs=pl.BlockSpec(memory_space=pltpu.VMEM),
        scratch_shapes=[
            pltpu.VMEM((PARTS * rows, count), bf16),
            pltpu.VMEM((PARTS * rows, width), bf16),
        ],
        name="sample_values",
        **params(32, 2 * PARTS * rows * width * count, 4 * PARTS * rows * width),
    )(place, *values)


def model_kernel(*refs):
    samples, weights = refs[:PARTS], refs[PARTS : 2 * PARTS]
    queries_ref, project_ref, gain_ref, out_ref = refs[2 * PARTS :]
    width = project_ref.shape[1]
    mixed = queries_ref[...].astype(f32)
    for a, b in zip(samples, weights):
        mixed = mixed + dot(a[...], b[...])
    visual = dot(mixed.astype(bf16), project_ref[...])
    squares = jnp.sum(visual * visual, axis=1, keepdims=True)
    high = squares.astype(bf16).astype(f32)
    middle = (squares - high).astype(bf16).astype(f32)
    low = squares - high - middle
    scaled = visual * gain_ref[...]
    out_ref[:, :width] = scaled.astype(bf16)
    extra = out_ref.shape[1] - width
    lane = lax.broadcasted_iota(jnp.int32, (scaled.shape[0], extra), 1)
    terms = jnp.where(lane == 0, high, jnp.where(lane == 1, middle, jnp.where(lane == 2, low, 0.0)))
    out_ref[:, width:] = terms.astype(bf16)


def model_columns(samples, weights, queries, project_weight, gain):
    rows, width = queries.shape[0], project_weight.shape[1]
    return pl.pallas_call(
        model_kernel,
        out_shape=jax.ShapeDtypeStruct((rows, width + 64), bf16),
        in_specs=vmem(2 * PARTS + 3),
        out_specs=pl.BlockSpec(memory_space=pltpu.VMEM),
        name="model_columns",
        **params(24, 2 * rows * queries.shape[1] * (queries.shape[1] + width), 4 * MIB),
    )(*samples, *weights, queries, project_weight, gain)


def turn(vectors, cosine, sine):
    return vectors * cosine + pltpu.roll(vectors, HD // 2, 1) * sine


def heads_kernel(width, *refs):
    blocks = refs[:PARTS]
    (query_ref, cache_ref, query_bias, cache_bias, cosine, sine, own_cosine, own_sine) = refs[
        PARTS : PARTS + 8
    ]
    query_out, cache_out = refs[PARTS + 8 :]
    rows = blocks[0].shape[0]
    queries = jnp.zeros((rows, query_ref.shape[1]), f32)
    cached = jnp.zeros((rows, cache_ref.shape[1]), f32)
    squares = jnp.zeros((rows, 1), f32)
    for place in range(PARTS):
        lines = pl.ds(pl.multiple_of(gathered_source(place) * width, 64), width)
        block = blocks[place][:, :width]
        queries = queries + dot(block, query_ref[lines, :])
        cached = cached + dot(block, cache_ref[lines, :])
        terms = blocks[place][:, width:].astype(f32)
        squares = squares + jnp.sum(terms, axis=1, keepdims=True)
    scale = lax.rsqrt(squares / float(PARTS * width) + epsilon)
    queries = queries * scale + query_bias[...]
    for head in range(query_ref.shape[1] // HD):
        query_out[head] = turn(
            queries[:, head * HD : (head + 1) * HD], cosine[...], sine[...]
        ).astype(bf16)
    cached = cached * scale + cache_bias[...]
    cache_out[...] = turn(cached, own_cosine[...], own_sine[...]).astype(bf16)


def head_states(blocks, width, query_weight, cache_weight, query_bias, cache_bias, tables):
    rows = blocks[0].shape[0]
    heads = query_weight.shape[1] // HD
    return pl.pallas_call(
        lambda *refs: heads_kernel(width, *refs),
        out_shape=[
            jax.ShapeDtypeStruct((heads, rows, HD), bf16),
            jax.ShapeDtypeStruct((rows, cache_weight.shape[1]), bf16),
        ],
        in_specs=vmem(PARTS + 8),
        out_specs=vmem(2),
        name="head_states",
        **params(24, 2 * rows * (query_weight.size + cache_weight.size), 6 * MIB),
    )(*blocks, query_weight, cache_weight, query_bias, cache_bias, *tables)


def attend_kernel(heads, query_ref, *refs):
    first, second = refs[:RING], refs[RING : 2 * RING]
    out_ref, peak, total, mix = refs[2 * RING :]
    rows = query_ref.shape[1]
    part, here, half = part_index(), lax.axis_index("tz"), lax.axis_index("tx")
    factor = HD ** (-0.5) * 1.4426950408889634
    lowest = lax.div(part * heads, GROUP)
    peak[...] = jnp.full_like(peak, masked)
    total[...] = jnp.zeros_like(total)
    mix[...] = jnp.zeros_like(mix)

    def update(head, pair_ref, own):
        key, value = pair_ref[:, :HD], pair_ref[:, HD:]
        scores = (
            lax.dot_general(
                query_ref[head], key, (((1,), (1,)), ((), ())), preferred_element_type=f32
            )
            * factor
        )
        if own:
            row = lax.broadcasted_iota(jnp.int32, scores.shape, 0) + half * rows
            column = lax.broadcasted_iota(jnp.int32, scores.shape, 1)
            column = jnp.where(column < rows, column + half * rows, column - half * rows)
            scores = jnp.where(column <= row, scores, masked)
        old = peak[head]
        new = jnp.maximum(old, jnp.max(scores, axis=1, keepdims=True))
        weights = jnp.exp2(scores - new[:, :1])
        shrink = jnp.exp2(old - new)
        peak[head] = new
        total[head] = total[head] * shrink + jnp.sum(weights, axis=1, keepdims=True)
        mix[head] = mix[head] * shrink + dot(weights.astype(bf16), value)

    for place in range(RING):
        if place == 0:
            needed = here >= 0
        elif place <= RING // 2:
            needed = here - place >= 0
        else:
            needed = here + place - RING // 2 >= RING
        for head in range(heads):
            same = lax.div(part * heads + head, GROUP) == lowest

            @pl.when(needed & same)
            def _():
                update(head, first[place], place == 0)

            @pl.when(needed & jnp.logical_not(same))
            def _():
                update(head, second[place], place == 0)

    for head in range(heads):
        out_ref[:, head * HD : (head + 1) * HD] = (mix[head] / total[head]).astype(bf16)


def attend(queries, first, second):
    heads, rows, _ = queries.shape
    return pl.pallas_call(
        lambda *refs: attend_kernel(heads, *refs),
        out_shape=jax.ShapeDtypeStruct((rows, heads * HD), bf16),
        in_specs=vmem(1 + 2 * RING),
        out_specs=pl.BlockSpec(memory_space=pltpu.VMEM),
        scratch_shapes=[pltpu.VMEM((heads, rows, HD), f32)] * 3,
        name="attend",
        **params(32, 4 * heads * rows * 4096 * HD, 5 * MIB),
    )(queries, *first, *second)


def by_group(x, low):
    sent = [
        [(0, 0), (1, 3), (2, 5), (3, 7)],
        [(0, 1), (1, 4), (2, 6)],
        [(0, 2)],
    ]
    pieces = [
        lax.ppermute(x, MP, [(low + source, target) for source, target in pairs])
        for pairs in sent
    ]
    return pieces[0] + pieces[1] + pieces[2]


def local(
    features,
    queries,
    anchor_frame,
    anchor_patch,
    time_offset,
    space_offset,
    value_weight,
    point_weight,
    point_bias,
    output_weight,
    project_weight,
    norm_gain,
    query_weight,
    query_bias,
    cache_weight,
    cache_bias,
):
    part = part_index()
    frames, patches, feature_width = features.shape
    rows = queries.shape[0]
    model_width = project_weight.shape[1]

    def own_head(array):
        return lax.dynamic_slice_in_dim(array, part, 1, 1)[:, 0].T

    logits = lax.dot_general(
        point_weight, queries, (((0,), (1,)), ((), ())), preferred_element_type=f32
    )
    logits = lax.dynamic_slice_in_dim(logits + point_bias[:, None], part * POINTS, POINTS, 0)
    share = jax.nn.softmax(logits, axis=0)
    frame_pos = anchor_frame.astype(f32)[None] + own_head(time_offset)
    row_pos = (anchor_patch // GRID).astype(f32)[None] + own_head(space_offset[0])
    column_pos = (anchor_patch % GRID).astype(f32)[None] + own_head(space_offset[1])
    place = jnp.concatenate([frame_pos, row_pos, column_pos, share], axis=0)
    forward = [(i, i + 1) for i in range(15)]
    backward = [(i + 1, i) for i in range(15)]
    nearby = jnp.concatenate(
        [lax.ppermute(place, TM, forward), lax.ppermute(place, TM, backward)], axis=1
    )

    projected = project_values(features.reshape(frames * patches, feature_width), value_weight)
    values = [projected[0]] + [
        lax.ppermute(projected[step], MP, turned(PARTS, step)) for step in range(1, PARTS)
    ]
    weights = gather_blocks(output_weight)

    theirs = sample(values, nearby, frames, bf16)
    mine = sample(values, place, frames, f32)
    below = lax.ppermute(theirs[:rows], TM, backward)
    above = lax.ppermute(theirs[rows:], TM, forward)
    sampled = (mine + below.astype(f32) + above.astype(f32)).astype(bf16)
    samples = gather_blocks(sampled)

    columns = model_columns(samples, weights, queries, project_weight, norm_gain[None])
    blocks = gather_blocks(columns)

    positions = (time_index() * rows + jnp.arange(rows, dtype=jnp.int32)).astype(f32)
    frequency = rope_base ** (-2.0 * jnp.arange(HD // 2, dtype=f32) / HD)
    angles = positions[:, None] * frequency[None, :]
    cosine, sine = jnp.cos(angles), jnp.sin(angles)
    cosine = jnp.concatenate([cosine, cosine], axis=1)
    sine = jnp.concatenate([-sine, sine], axis=1)
    is_key = part < KVH
    own_cosine = jnp.where(is_key, cosine, 1.0)
    own_sine = jnp.where(is_key, sine, 0.0)
    turned_queries, key_value = head_states(
        blocks,
        model_width,
        query_weight,
        cache_weight,
        query_bias[None],
        cache_bias[None],
        (cosine, sine, own_cosine, own_sine),
    )

    own = jnp.concatenate([by_group(key_value, 0), by_group(key_value, KVH)], axis=1)
    other = lax.ppermute(own, "tx", turned(2, 1))
    pair = jnp.concatenate([own, other], axis=0)
    first = [pair]
    for step in range(1, RING // 2 + 1):
        pairs = [(i, i + 1) for i in range(step - 1, RING - 1)]
        first.append(lax.ppermute(first[-1], "tz", pairs))
    down = pair
    for step in range(1, RING // 2):
        down = lax.ppermute(down, "tz", turned(RING, -1))
        first.append(down)
    second = [lax.ppermute(x, MP, [(3, 2), (5, 4)]) for x in first]
    attention = attend(turned_queries, first, second)
    return (attention, key_value)


def solution(mesh):
    finer = Mesh(
        mesh.devices.reshape(mesh.shape["dp"], RING, 2, 4, 2), ("dp", "tz", "tx", "my", "mc")
    )
    time = ("dp", *TM)
    placed = (
        P(time, MP, None),
        P(time, None),
        P(time),
        P(time),
        P(time, None, None),
        P(None, time, None, None),
        P(),
        P(),
        P(),
        P(MP, None),
        P(None, MP),
        P(MP),
        P(None, MP),
        P(MP),
        P(None, MP),
        P(MP),
    )
    return jax.shard_map(
        local,
        mesh=finer,
        in_specs=placed,
        out_specs=(P(time, MP), P(time, MP)),
        check_vma=False,
    )
```

```python
import jax
import jax.numpy as jnp
from jax import lax
from jax.experimental import pallas as pl
from jax.experimental.pallas import tpu as pltpu
from jax.sharding import Mesh
from jax.sharding import PartitionSpec as P

AH = 8
AHD = 128
POINTS = 4
GRID = 24
KVH = 4
HD = 128
GROUP = 7
PARTS = 8
RING = 8
TM = ("tz", "tx")
MP = ("my", "mc")

rope_base = 1000000.0
epsilon = 1e-06
masked = -1e30
MIB = 1 << 20

f32 = jnp.float32
bf16 = jnp.bfloat16


def part_index():
    return lax.axis_index("my") * 2 + lax.axis_index("mc")


def time_index():
    return lax.axis_index("tz") * 2 + lax.axis_index("tx")


def gathered_source(place):
    step, other = place // 2, place % 2
    row = lax.rem(lax.axis_index("my") - step + 4, 4)
    core = lax.axis_index("mc")
    return row * 2 + (1 - core if other else core)


def turned(size, step):
    return [(i, (i + step) % size) for i in range(size)]


def gather_blocks(x):
    columns = [x] + [lax.ppermute(x, "my", turned(4, step)) for step in (1, 2, 3)]
    blocks = []
    for block in columns:
        blocks += [block, lax.ppermute(block, "mc", turned(2, 1))]
    return blocks


def dot(a, b):
    return jnp.dot(a, b, preferred_element_type=f32)


def params(mib, flops=0, read=0):
    return dict(
        compiler_params=pltpu.CompilerParams(vmem_limit_bytes=mib * MIB),
        cost_estimate=pl.CostEstimate(flops=flops, bytes_accessed=read, transcendentals=0),
    )


def vmem(count):
    return [pl.BlockSpec(memory_space=pltpu.VMEM)] * count


def begin_kernel(*refs):
    inputs, place_ref, outs = refs[:8], refs[8], refs[9 : 9 + PARTS]
    arrived, (held, arriving) = refs[9 + PARTS : 17 + PARTS], refs[17 + PARTS :]
    part = part_index()
    copies = []
    for k, (source, target) in enumerate(zip(inputs, arrived)):
        if k == 4:
            source = source.at[part]
        if k == 5:
            source = source.at[:, part]
        copies.append(pltpu.make_async_copy(source, target, arriving.at[k]))
    for copy in copies:
        copy.start()
    queries, point_weight, bias, anchors, time, space, features, value_weight = arrived
    for copy in copies[:6]:
        copy.wait()
    logits = lax.dot_general(
        point_weight[...], queries[...], (((1,), (1,)), ((), ())), preferred_element_type=f32
    )
    columns = AH * POINTS
    on_diagonal = lax.broadcasted_iota(jnp.int32, (columns, columns), 0) == (
        lax.broadcasted_iota(jnp.int32, (columns, columns), 1)
    )
    logits = logits + jnp.sum(jnp.where(on_diagonal, bias[...], 0.0), axis=1, keepdims=True)
    own = logits[:POINTS]
    for head in range(1, AH):
        own = jnp.where(part == head, logits[head * POINTS : (head + 1) * POINTS], own)
    share = jnp.exp(own - jnp.max(own, axis=0, keepdims=True))
    share = share / jnp.sum(share, axis=0, keepdims=True)
    patch = anchors[1:2, :].astype(f32)
    row = jnp.floor((patch + 0.5) * (1.0 / GRID))
    place_ref[0:POINTS] = anchors[0:1, :].astype(f32) + time[...]
    place_ref[POINTS : 2 * POINTS] = row + space[0]
    place_ref[2 * POINTS : 3 * POINTS] = (patch - row * GRID) + space[1]
    place_ref[3 * POINTS :] = share
    for copy in copies[6:]:
        copy.wait()
    for pair in range(PARTS // 2):
        both = dot(features[...], value_weight[:, pair * 256 : pair * 256 + 256]).astype(bf16)
        held[2 * pair] = both[:, :AHD]
        held[2 * pair + 1] = both[:, AHD:]
    for step in range(PARTS):
        outs[step][...] = held[lax.rem(part + step, PARTS)]


def begin(queries, weight, bias, frame, patch, time_offset, space_offset, features, value_weight):
    rows, lines = queries.shape[0], features.shape[0]
    inputs = (
        queries,
        weight.T,
        bias[None],
        jnp.stack([frame, patch]),
        time_offset.transpose(1, 2, 0),
        space_offset.transpose(0, 2, 3, 1),
        features,
        value_weight,
    )
    held = [pltpu.VMEM(x.shape, x.dtype) for x in inputs]
    held[4] = pltpu.VMEM((POINTS, rows), f32)
    held[5] = pltpu.VMEM((2, POINTS, rows), f32)
    place, *projected = pl.pallas_call(
        begin_kernel,
        out_shape=[jax.ShapeDtypeStruct((4 * POINTS, rows), f32)]
        + [jax.ShapeDtypeStruct((lines, AHD), bf16)] * PARTS,
        in_specs=[pl.BlockSpec(memory_space=pltpu.HBM)] * len(inputs),
        out_specs=vmem(1 + PARTS),
        scratch_shapes=held
        + [pltpu.VMEM((PARTS, lines, AHD), bf16), pltpu.SemaphoreType.DMA((len(inputs),))],
        name="begin",
        **params(12, 2 * lines * value_weight.size, 4 * MIB),
    )(*inputs)
    return place, projected


def hat(distance):
    return jnp.maximum(1.0 - jnp.abs(distance), 0.0)


def sample_kernel(frames, rows_each, place_ref, *refs):
    values, out_ref, spread, stacked = refs[:PARTS], refs[PARTS], refs[PARTS + 1], refs[PARTS + 2]
    count = place_ref.shape[1]
    block = frames * rows_each * GRID
    part = part_index()
    first = (time_index() * frames).astype(f32)
    cell = lax.broadcasted_iota(jnp.int32, (GRID, count), 0).astype(f32)
    frame_at = [place_ref[k : k + 1, :] for k in range(POINTS)]
    row_at = [place_ref[POINTS + k : POINTS + k + 1, :] for k in range(POINTS)]
    share = [place_ref[3 * POINTS + k : 3 * POINTS + k + 1, :] for k in range(POINTS)]
    column_hat = [
        hat(cell - place_ref[2 * POINTS + k : 2 * POINTS + k + 1, :]) for k in range(POINTS)
    ]
    frame_hat = [
        [share[k] * hat(first + float(f) - frame_at[k]) for k in range(POINTS)]
        for f in range(frames)
    ]
    for step in range(PARTS):
        source = lax.rem(part - step + PARTS, PARTS)
        top = source * rows_each
        row_hat = [
            [hat((top + r).astype(f32) - row_at[k]) for k in range(POINTS)]
            for r in range(rows_each)
        ]
        pieces = []
        for f in range(frames):
            for r in range(rows_each):
                total = (frame_hat[f][0] * row_hat[r][0]) * column_hat[0]
                for k in range(1, POINTS):
                    total = total + (frame_hat[f][k] * row_hat[r][k]) * column_hat[k]
                pieces.append(total)
        spread[step * block : (step + 1) * block, :] = jnp.concatenate(pieces, axis=0).astype(bf16)
        stacked[step * block : (step + 1) * block, :] = values[step][...]
    turned_values = stacked[...].T
    for lo in range(0, count, 256):
        out = dot(turned_values, spread[:, lo : lo + 256])
        out_ref[lo : lo + 256, :] = out.T.astype(out_ref.dtype)


def sample(values, place, frames, kind):
    rows, width = values[0].shape
    count = place.shape[1]
    rows_each = GRID // PARTS
    return pl.pallas_call(
        lambda *refs: sample_kernel(frames, rows_each, *refs),
        out_shape=jax.ShapeDtypeStruct((count, width), kind),
        in_specs=vmem(1 + PARTS),
        out_specs=pl.BlockSpec(memory_space=pltpu.VMEM),
        scratch_shapes=[
            pltpu.VMEM((PARTS * rows, count), bf16),
            pltpu.VMEM((PARTS * rows, width), bf16),
        ],
        name="sample_values",
        **params(10, 2 * PARTS * rows * width * count, 4 * PARTS * rows * width),
    )(place, *values)


def model_kernel(*refs):
    samples = refs[:PARTS]
    weights_ref, queries_ref, project_ref, gain_ref, out_ref = refs[PARTS:]
    width = project_ref.shape[0]
    mixed = queries_ref[...].astype(f32)
    for place in range(PARTS):
        mixed = mixed + dot(samples[place][...], weights_ref[gathered_source(place)])
    visual = lax.dot_general(
        mixed.astype(bf16),
        project_ref[...],
        (((1,), (1,)), ((), ())),
        preferred_element_type=f32,
    )
    squares = jnp.sum(visual * visual, axis=1, keepdims=True)
    high = squares.astype(bf16).astype(f32)
    middle = (squares - high).astype(bf16).astype(f32)
    low = squares - high - middle
    scaled = visual * gain_ref[...]
    out_ref[:, :width] = scaled.astype(bf16)
    extra = out_ref.shape[1] - width
    lane = lax.broadcasted_iota(jnp.int32, (scaled.shape[0], extra), 1)
    terms = jnp.where(lane == 0, high, jnp.where(lane == 1, middle, jnp.where(lane == 2, low, 0.0)))
    out_ref[:, width:] = terms.astype(bf16)


def model_columns(samples, weights, queries, project_weight, gain):
    rows, width = queries.shape[0], project_weight.shape[1]
    return pl.pallas_call(
        model_kernel,
        out_shape=jax.ShapeDtypeStruct((rows, width + 64), bf16),
        in_specs=vmem(PARTS + 4),
        out_specs=pl.BlockSpec(memory_space=pltpu.VMEM),
        name="model_columns",
        **params(8, 2 * rows * queries.shape[1] * (queries.shape[1] + width), 4 * MIB),
    )(*samples, weights, queries, project_weight.T, gain)


def turn(vectors, cosine, sine):
    return vectors * cosine + pltpu.roll(vectors, HD // 2, 1) * sine


def turned_product(width, blocks, weight_ref, bias_ref, cosine, sine):
    rows = blocks[0].shape[0]
    product = jnp.zeros((rows, weight_ref.shape[1]), f32)
    squares = jnp.zeros((rows, 1), f32)
    for place in range(PARTS):
        lines = pl.ds(pl.multiple_of(gathered_source(place) * width, 64), width)
        product = product + dot(blocks[place][:, :width], weight_ref[lines, :])
        terms = blocks[place][:, width:].astype(f32)
        squares = squares + jnp.sum(terms, axis=1, keepdims=True)
    scale = lax.rsqrt(squares / float(PARTS * width) + epsilon)
    product = product * scale + bias_ref[...]
    return [
        turn(product[:, lo : lo + HD], cosine[...], sine[...]).astype(bf16)
        for lo in range(0, product.shape[1], HD)
    ]


def query_kernel(width, *refs):
    out_ref = refs[-1]
    for head, vectors in enumerate(turned_product(width, refs[:PARTS], *refs[PARTS:-1])):
        out_ref[head] = vectors


def cache_kernel(width, *refs):
    refs[-1][...] = turned_product(width, refs[:PARTS], *refs[PARTS:-1])[0]


def head_states(kernel, shape, blocks, width, weight, bias, cosine, sine):
    return pl.pallas_call(
        lambda *refs: kernel(width, *refs),
        out_shape=jax.ShapeDtypeStruct(shape, bf16),
        in_specs=vmem(PARTS + 4),
        out_specs=pl.BlockSpec(memory_space=pltpu.VMEM),
        name="head_states",
        **params(8, 2 * blocks[0].shape[0] * weight.size, 2 * weight.size + 2 * MIB),
    )(*blocks, weight, bias, cosine, sine)


def attend_kernel(step, last, own_ref, other_ref, *refs):
    count = 1 if step == 0 or last else 2
    blocks = refs[:count]
    outs, (peak, total, mix) = refs[count + (3 if step else 0) : -3], refs[-3:]
    heads, rows, _ = own_ref.shape
    part, core = part_index(), lax.axis_index("mc")
    here, half = lax.axis_index("tz"), lax.axis_index("tx")
    factor = HD ** (-0.5) * 1.4426950408889634

    def update(slot, query_ref, head, used):
        query = query_ref[head]
        pieces = []
        for block in used:
            scores = (
                lax.dot_general(
                    query, block[:, :HD], (((1,), (1,)), ((), ())), preferred_element_type=f32
                )
                * factor
            )
            if step == 0:
                row = lax.broadcasted_iota(jnp.int32, scores.shape, 0) + half * rows
                column = lax.broadcasted_iota(jnp.int32, scores.shape, 1)
                column = jnp.where(column < rows, column + half * rows, column - half * rows)
                scores = jnp.where(column <= row, scores, masked)
            pieces += [scores[:, lo : lo + HD] for lo in range(0, scores.shape[1], HD)]
        top = pieces[0]
        for piece in pieces[1:]:
            top = jnp.maximum(top, piece)
        new = jnp.max(top, axis=1, keepdims=True)
        if step:
            old = peak[slot]
            new = jnp.maximum(old, new)
        else:
            new = jnp.broadcast_to(new, (rows, HD))
        weights = [jnp.exp2(piece - new) for piece in pieces]
        added = weights[0]
        for piece in weights[1:]:
            added = added + piece
        each = len(pieces) // len(used)
        mixed = None
        for k, block in enumerate(used):
            part_weights = jnp.concatenate(
                [piece.astype(bf16) for piece in weights[k * each : (k + 1) * each]], axis=1
            )
            product = dot(part_weights, block[:, HD:])
            mixed = product if mixed is None else mixed + product
        peak[slot] = new
        if step:
            shrink = jnp.exp2(old - new)
            total[slot] = total[slot] * shrink + added
            mix[slot] = mix[slot] * shrink + mixed
        else:
            total[slot] = added
            mix[slot] = mixed

    for side, query_ref in enumerate((own_ref, other_ref)):
        owner = part if side == 0 else part + 1 - 2 * core

        def one_head(head, _):
            group = lax.div(owner * heads + head, GROUP)
            mine = lax.rem(group, 2) == core
            slot = side * heads + head
            if step == 0:
                pl.when(mine)(lambda: update(slot, query_ref, head, blocks))
                return _
            up = mine & (here >= step)
            if count == 1:
                pl.when(up)(lambda: update(slot, query_ref, head, blocks))
            else:
                down = mine & (here + step >= RING)
                pl.when(up & down)(lambda: update(slot, query_ref, head, blocks))
                pl.when(up & jnp.logical_not(down))(
                    lambda: update(slot, query_ref, head, blocks[:1])
                )
                pl.when(down & jnp.logical_not(up))(
                    lambda: update(slot, query_ref, head, blocks[1:])
                )
            return _

        lax.fori_loop(0, heads, one_head, 0)
        if last:
            for head in range(heads):
                mine = lax.rem(lax.div(owner * heads + head, GROUP), 2) == core
                slot = side * heads + head
                share = 1.0 / jnp.sum(total[slot], axis=1, keepdims=True)
                outs[side][:, head * HD : (head + 1) * HD] = jnp.where(
                    mine, mix[slot] * share, 0.0
                ).astype(bf16)


def attend(step, last, own, other, blocks, state):
    heads, rows, _ = own.shape
    shape = jax.ShapeDtypeStruct((2 * heads, rows, HD), f32)
    results = [jax.ShapeDtypeStruct((rows, heads * HD), bf16)] * 2 if last else []
    first = 2 + len(blocks)
    outs = pl.pallas_call(
        lambda *refs: attend_kernel(step, last, *refs),
        out_shape=results + [shape] * 3,
        in_specs=vmem(first + len(state)),
        out_specs=vmem(len(results) + 3),
        input_output_aliases={first + k: len(results) + k for k in range(len(state))},
        name="attend",
        **params(16, 8 * heads * rows * 512 * HD * len(blocks), 4 * MIB),
    )(own, other, *blocks, *state)
    return outs[:2] if last else outs


def own_group(x):
    part = part_index()
    one = lax.ppermute(x, MP, [(0, 2), (2, 4), (4, 0), (1, 3), (3, 7)])
    two = lax.ppermute(x, MP, [(2, 6), (4, 2), (6, 4), (1, 5), (5, 3)])
    key = jnp.where(part == 0, x, jnp.where((part == 5) | (part == 6), two, one))
    value = jnp.where(part >= 5, x, jnp.where(part == 0, one, two))
    return jnp.concatenate([key, value], axis=1)


def local(
    features,
    queries,
    anchor_frame,
    anchor_patch,
    time_offset,
    space_offset,
    value_weight,
    point_weight,
    point_bias,
    output_weight,
    project_weight,
    norm_gain,
    query_weight,
    query_bias,
    cache_weight,
    cache_bias,
):
    part = part_index()
    frames, patches, feature_width = features.shape
    rows = queries.shape[0]
    model_width = project_weight.shape[1]

    weights = lax.all_gather(output_weight, MP)
    place, projected = begin(
        queries,
        point_weight,
        point_bias,
        anchor_frame,
        anchor_patch,
        time_offset,
        space_offset,
        features.reshape(frames * patches, feature_width),
        value_weight,
    )
    forward = [(i, i + 1) for i in range(15)]
    backward = [(i + 1, i) for i in range(15)]
    nearby = jnp.concatenate(
        [lax.ppermute(place, TM, forward), lax.ppermute(place, TM, backward)], axis=1
    )
    values = [projected[0]] + [
        lax.ppermute(projected[step], MP, turned(PARTS, step)) for step in range(1, PARTS)
    ]
    theirs = sample(values, nearby, frames, bf16)
    mine = sample(values, place, frames, f32)
    below = lax.ppermute(theirs[:rows], TM, backward)
    above = lax.ppermute(theirs[rows:], TM, forward)
    sampled = (mine + below.astype(f32) + above.astype(f32)).astype(bf16)
    samples = gather_blocks(sampled)

    columns = model_columns(samples, weights, queries, project_weight, norm_gain[None])
    blocks = gather_blocks(columns)

    positions = (time_index() * rows + jnp.arange(rows, dtype=jnp.int32)).astype(f32)
    frequency = rope_base ** (-2.0 * jnp.arange(HD // 2, dtype=f32) / HD)
    angles = positions[:, None] * frequency[None, :]
    cosine, sine = jnp.cos(angles), jnp.sin(angles)
    cosine = jnp.concatenate([cosine, cosine], axis=1)
    sine = jnp.concatenate([-sine, sine], axis=1)
    is_key = part < KVH
    own_cosine = jnp.where(is_key, cosine, 1.0)
    own_sine = jnp.where(is_key, sine, 0.0)
    key_value = head_states(
        cache_kernel,
        (rows, cache_weight.shape[1]),
        blocks,
        model_width,
        cache_weight,
        cache_bias[None],
        own_cosine,
        own_sine,
    )
    own = own_group(key_value)
    other = lax.ppermute(own, "tx", turned(2, 1))
    heads = query_weight.shape[1] // HD
    turned_queries = head_states(
        query_kernel,
        (heads, rows, HD),
        blocks,
        model_width,
        query_weight,
        query_bias[None],
        cosine,
        sine,
    )
    other_queries = lax.ppermute(turned_queries, "mc", turned(2, 1))

    up = down = jnp.concatenate([own, other], axis=0)
    state = ()
    for step in range(RING // 2 + 1):
        last = step == RING // 2
        blocks = [up] if step == 0 or last else [up, down]
        if not last:
            if step > 0:
                up, down, state = lax.optimization_barrier((up, down, state))
            pairs = [(i, i + 1) for i in range(step, RING - 1)]
            up = lax.ppermute(up, "tz", pairs)
            if step + 1 < RING // 2:
                down = lax.ppermute(down, "tz", turned(RING, -1))
        state = attend(step, last, turned_queries, other_queries, blocks, state)
    mixed, others = state
    others = lax.ppermute(others, "mc", turned(2, 1))
    attention = []
    for head in range(heads):
        mine = lax.rem((part * heads + head) // GROUP, 2) == lax.axis_index("mc")
        lanes = slice(head * HD, (head + 1) * HD)
        attention.append(jnp.where(mine, mixed[:, lanes], others[:, lanes]))
    attention = jnp.concatenate(attention, axis=1)
    return (attention, key_value)


def solution(mesh):
    finer = Mesh(
        mesh.devices.reshape(mesh.shape["dp"], RING, 2, 4, 2), ("dp", "tz", "tx", "my", "mc")
    )
    time = ("dp", *TM)
    placed = (
        P(time, MP, None),
        P(time, None),
        P(time),
        P(time),
        P(time, None, None),
        P(None, time, None, None),
        P(),
        P(),
        P(),
        P(MP, None),
        P(None, MP),
        P(MP),
        P(None, MP),
        P(MP),
        P(None, MP),
        P(MP),
    )
    return jax.shard_map(
        local,
        mesh=finer,
        in_specs=placed,
        out_specs=(P(time, MP), P(time, MP)),
        check_vma=False,
    )
```

```python
import jax
import jax.numpy as jnp
from jax import lax
from jax.experimental import pallas as pl
from jax.experimental.pallas import tpu as pltpu
from jax.sharding import Mesh
from jax.sharding import PartitionSpec as P

AH = 8
AHD = 128
POINTS = 4
GRID = 24
KVH = 4
HD = 128
GROUP = 7
PARTS = 8
RING = 8
TM = ("tz", "tx")
MP = ("my", "mc")

rope_base = 1000000.0
epsilon = 1e-06
masked = -1e30
MIB = 1 << 20

f32 = jnp.float32
bf16 = jnp.bfloat16


def part_index():
    return lax.axis_index("my") * 2 + lax.axis_index("mc")


def time_index():
    return lax.axis_index("tz") * 2 + lax.axis_index("tx")


def gathered_source(place):
    step, other = place // 2, place % 2
    row = lax.rem(lax.axis_index("my") - step + 4, 4)
    core = lax.axis_index("mc")
    return row * 2 + (1 - core if other else core)


def turned(size, step):
    return [(i, (i + step) % size) for i in range(size)]


def gather_blocks(x):
    columns = [x] + [lax.ppermute(x, "my", turned(4, step)) for step in (1, 2, 3)]
    blocks = []
    for block in columns:
        blocks += [block, lax.ppermute(block, "mc", turned(2, 1))]
    return blocks


def dot(a, b):
    return jnp.dot(a, b, preferred_element_type=f32)


def params(mib, flops=0, read=0):
    return dict(
        compiler_params=pltpu.CompilerParams(vmem_limit_bytes=mib * MIB),
        cost_estimate=pl.CostEstimate(flops=flops, bytes_accessed=read, transcendentals=0),
    )


def vmem(count):
    return [pl.BlockSpec(memory_space=pltpu.VMEM)] * count


def begin_kernel(*refs):
    inputs, place_ref, outs = refs[:9], refs[9], refs[10:14]
    arrived, (held, arriving) = refs[14:23], refs[23:]
    part = part_index()
    copies = []
    for k, (source, target) in enumerate(zip(inputs, arrived)):
        if k == 5:
            source = source.at[part]
        if k == 6:
            source = source.at[:, part]
        copies.append(pltpu.make_async_copy(source, target, arriving.at[k]))
    for copy in copies:
        copy.start()
    queries, point_weight, bias, frame, patch, time, space, features, value_weight = arrived
    for copy in copies[:7]:
        copy.wait()
    logits = lax.dot_general(
        point_weight[...], queries[...], (((1,), (1,)), ((), ())), preferred_element_type=f32
    )
    columns = AH * POINTS
    on_diagonal = lax.broadcasted_iota(jnp.int32, (columns, columns), 0) == (
        lax.broadcasted_iota(jnp.int32, (columns, columns), 1)
    )
    logits = logits + jnp.sum(jnp.where(on_diagonal, bias[...], 0.0), axis=1, keepdims=True)
    own = logits[:POINTS]
    for head in range(1, AH):
        own = jnp.where(part == head, logits[head * POINTS : (head + 1) * POINTS], own)
    share = jnp.exp(own - jnp.max(own, axis=0, keepdims=True))
    share = share / jnp.sum(share, axis=0, keepdims=True)
    patch = patch[...].astype(f32)
    row = jnp.floor((patch + 0.5) * (1.0 / GRID))
    place_ref[0:POINTS] = frame[...].astype(f32) + time[...]
    place_ref[POINTS : 2 * POINTS] = row + space[0]
    place_ref[2 * POINTS : 3 * POINTS] = (patch - row * GRID) + space[1]
    place_ref[3 * POINTS :] = share
    for copy in copies[7:]:
        copy.wait()
    for pair in range(PARTS // 2):
        both = dot(features[...], value_weight[:, pair * 256 : pair * 256 + 256]).astype(bf16)
        held[2 * pair] = both[:, :AHD]
        held[2 * pair + 1] = both[:, AHD:]
    chip = lax.axis_index("my")
    for step in range(4):
        first = 2 * lax.rem(chip + step, 4)
        outs[step][0] = held[first]
        outs[step][1] = held[first + 1]


def begin(queries, weight, bias, frame, patch, time_offset, space_offset, features, value_weight):
    rows, lines = queries.shape[0], features.shape[0]
    inputs = (
        queries,
        weight.T,
        bias[None],
        frame[None],
        patch[None],
        time_offset.transpose(1, 2, 0),
        space_offset.transpose(0, 2, 3, 1),
        features,
        value_weight,
    )
    held = [pltpu.VMEM(x.shape, x.dtype) for x in inputs]
    held[5] = pltpu.VMEM((POINTS, rows), f32)
    held[6] = pltpu.VMEM((2, POINTS, rows), f32)
    place, *projected = pl.pallas_call(
        begin_kernel,
        out_shape=[jax.ShapeDtypeStruct((4 * POINTS, rows), f32)]
        + [jax.ShapeDtypeStruct((2, lines, AHD), bf16)] * 4,
        in_specs=[pl.BlockSpec(memory_space=pltpu.HBM)] * len(inputs),
        out_specs=vmem(5),
        scratch_shapes=held
        + [pltpu.VMEM((PARTS, lines, AHD), bf16), pltpu.SemaphoreType.DMA((len(inputs),))],
        name="begin",
        **params(60, 2 * lines * value_weight.size, 4 * MIB),
    )(*inputs)
    return place, projected


def hat(distance):
    return jnp.maximum(1.0 - jnp.abs(distance), 0.0)


def sample_kernel(frames, rows_each, place_ref, *refs):
    values, out_ref, spread, stacked = refs[:PARTS], refs[PARTS], refs[PARTS + 1], refs[PARTS + 2]
    count = place_ref.shape[1]
    block = frames * rows_each * GRID
    core = lax.axis_index("mc")
    first = (time_index() * frames).astype(f32)
    cell = lax.broadcasted_iota(jnp.int32, (GRID, count), 0).astype(f32)
    frame_at = [place_ref[k : k + 1, :] for k in range(POINTS)]
    row_at = [place_ref[POINTS + k : POINTS + k + 1, :] for k in range(POINTS)]
    share = [place_ref[3 * POINTS + k : 3 * POINTS + k + 1, :] for k in range(POINTS)]
    column_hat = [
        hat(cell - place_ref[2 * POINTS + k : 2 * POINTS + k + 1, :]) for k in range(POINTS)
    ]
    frame_hat = [
        [share[k] * hat(first + float(f) - frame_at[k]) for k in range(POINTS)]
        for f in range(frames)
    ]
    for step in range(PARTS):
        top = gathered_source(step) * rows_each
        row_hat = [
            [hat((top + r).astype(f32) - row_at[k]) for k in range(POINTS)]
            for r in range(rows_each)
        ]
        pieces = []
        for f in range(frames):
            for r in range(rows_each):
                total = (frame_hat[f][0] * row_hat[r][0]) * column_hat[0]
                for k in range(1, POINTS):
                    total = total + (frame_hat[f][k] * row_hat[r][k]) * column_hat[k]
                pieces.append(total)
        spread[step * block : (step + 1) * block, :] = jnp.concatenate(pieces, axis=0).astype(bf16)
        stacked[step * block : (step + 1) * block, :] = values[step][core]
    turned_values = stacked[...].T
    for lo in range(0, count, 256):
        out = dot(turned_values, spread[:, lo : lo + 256])
        out_ref[lo : lo + 256, :] = out.T.astype(out_ref.dtype)


def sample(values, place, frames, kind):
    _, rows, width = values[0].shape
    count = place.shape[1]
    rows_each = GRID // PARTS
    return pl.pallas_call(
        lambda *refs: sample_kernel(frames, rows_each, *refs),
        out_shape=jax.ShapeDtypeStruct((count, width), kind),
        in_specs=vmem(1 + PARTS),
        out_specs=pl.BlockSpec(memory_space=pltpu.VMEM),
        scratch_shapes=[
            pltpu.VMEM((PARTS * rows, count), bf16),
            pltpu.VMEM((PARTS * rows, width), bf16),
        ],
        name="sample_values",
        **params(10, 2 * PARTS * rows * width * count, 4 * PARTS * rows * width),
    )(place, *values)


def model_kernel(*refs):
    samples, weights = refs[:PARTS], refs[PARTS : 2 * PARTS]
    queries_ref, project_ref, gain_ref, out_ref = refs[2 * PARTS :]
    width = project_ref.shape[0]
    mixed = queries_ref[...].astype(f32)
    for a, b in zip(samples, weights):
        mixed = mixed + dot(a[...], b[...])
    visual = lax.dot_general(
        mixed.astype(bf16),
        project_ref[...],
        (((1,), (1,)), ((), ())),
        preferred_element_type=f32,
    )
    squares = jnp.sum(visual * visual, axis=1, keepdims=True)
    high = squares.astype(bf16).astype(f32)
    middle = (squares - high).astype(bf16).astype(f32)
    low = squares - high - middle
    scaled = visual * gain_ref[...]
    out_ref[:, :width] = scaled.astype(bf16)
    extra = out_ref.shape[1] - width
    lane = lax.broadcasted_iota(jnp.int32, (scaled.shape[0], extra), 1)
    terms = jnp.where(lane == 0, high, jnp.where(lane == 1, middle, jnp.where(lane == 2, low, 0.0)))
    out_ref[:, width:] = terms.astype(bf16)


def model_columns(samples, weights, queries, project_weight, gain):
    rows, width = queries.shape[0], project_weight.shape[1]
    return pl.pallas_call(
        model_kernel,
        out_shape=jax.ShapeDtypeStruct((rows, width + 64), bf16),
        in_specs=vmem(2 * PARTS + 3),
        out_specs=pl.BlockSpec(memory_space=pltpu.VMEM),
        name="model_columns",
        **params(8, 2 * rows * queries.shape[1] * (queries.shape[1] + width), 4 * MIB),
    )(*samples, *weights, queries, project_weight.T, gain)


def turn(vectors, cosine, sine):
    return vectors * cosine + pltpu.roll(vectors, HD // 2, 1) * sine


def heads_kernel(width, *refs):
    inputs, (query_out, cache_out), arrived = refs[:14], refs[14:16], refs[16:30]
    arriving = refs[30]
    copies = [
        pltpu.make_async_copy(source, target, arriving.at[k])
        for k, (source, target) in enumerate(zip(inputs, arrived))
    ]
    for copy in copies:
        copy.start()
    cache_ref, cache_bias, cosine, sine = arrived[:4]
    blocks, (query_ref, query_bias) = arrived[4:12], arrived[12:]
    rows = blocks[0].shape[0]
    lines = [
        pl.ds(pl.multiple_of(gathered_source(place) * width, 64), width)
        for place in range(PARTS)
    ]
    squares = jnp.zeros((rows, 1), f32)
    cached = jnp.zeros((rows, cache_ref.shape[1]), f32)
    for copy in copies[:4]:
        copy.wait()
    for place in range(PARTS):
        copies[4 + place].wait()
        cached = cached + dot(blocks[place][:, :width], cache_ref[lines[place], :])
        terms = blocks[place][:, width:].astype(f32)
        squares = squares + jnp.sum(terms, axis=1, keepdims=True)
    scale = lax.rsqrt(squares / float(PARTS * width) + epsilon)
    cached = cached * scale + cache_bias[...]
    is_key = part_index() < KVH
    cache_out[...] = jnp.where(is_key, turn(cached, cosine[...], sine[...]), cached).astype(bf16)
    for copy in copies[12:]:
        copy.wait()
    queries = jnp.zeros((rows, query_ref.shape[1]), f32)
    for place in range(PARTS):
        queries = queries + dot(blocks[place][:, :width], query_ref[lines[place], :])
    queries = queries * scale + query_bias[...]
    for head in range(query_ref.shape[1] // HD):
        vectors = turn(queries[:, head * HD : (head + 1) * HD], cosine[...], sine[...])
        query_out[head] = vectors.astype(bf16)


def head_states(blocks, width, query_weight, cache_weight, query_bias, cache_bias, tables):
    rows = blocks[0].shape[0]
    inputs = (cache_weight, cache_bias, *tables, *blocks, query_weight, query_bias)
    return pl.pallas_call(
        lambda *refs: heads_kernel(width, *refs),
        out_shape=[
            jax.ShapeDtypeStruct((query_weight.shape[1] // HD, rows, HD), bf16),
            jax.ShapeDtypeStruct((rows, cache_weight.shape[1]), bf16),
        ],
        in_specs=[pl.BlockSpec(memory_space=pltpu.HBM)] * len(inputs),
        out_specs=vmem(2),
        scratch_shapes=[pltpu.VMEM(x.shape, x.dtype) for x in inputs]
        + [pltpu.SemaphoreType.DMA((len(inputs),))],
        name="head_states",
        **params(51, 2 * rows * (query_weight.size + cache_weight.size), 6 * MIB),
    )(*inputs)


def attend_kernel(step, last, own_ref, other_ref, *refs):
    count = 1 if step == 0 or last else 2
    blocks = refs[:count]
    outs, (peak, total, mix) = refs[count + (3 if step else 0) : -3], refs[-3:]
    heads, rows, _ = own_ref.shape
    part, core = part_index(), lax.axis_index("mc")
    here, half = lax.axis_index("tz"), lax.axis_index("tx")
    factor = HD ** (-0.5) * 1.4426950408889634

    def update(slot, query_ref, head, used):
        query = query_ref[head]
        pieces = []
        for block in used:
            scores = (
                lax.dot_general(
                    query, block[:, :HD], (((1,), (1,)), ((), ())), preferred_element_type=f32
                )
                * factor
            )
            if step == 0:
                row = lax.broadcasted_iota(jnp.int32, scores.shape, 0) + half * rows
                column = lax.broadcasted_iota(jnp.int32, scores.shape, 1)
                column = jnp.where(column < rows, column + half * rows, column - half * rows)
                scores = jnp.where(column <= row, scores, masked)
            pieces += [scores[:, lo : lo + HD] for lo in range(0, scores.shape[1], HD)]
        top = pieces[0]
        for piece in pieces[1:]:
            top = jnp.maximum(top, piece)
        new = jnp.max(top, axis=1, keepdims=True)
        if step:
            old = peak[slot]
            new = jnp.maximum(old, new)
        else:
            new = jnp.broadcast_to(new, (rows, HD))
        weights = [jnp.exp2(piece - new) for piece in pieces]
        added = weights[0]
        for piece in weights[1:]:
            added = added + piece
        each = len(pieces) // len(used)
        mixed = None
        for k, block in enumerate(used):
            part_weights = jnp.concatenate(
                [piece.astype(bf16) for piece in weights[k * each : (k + 1) * each]], axis=1
            )
            product = dot(part_weights, block[:, HD:])
            mixed = product if mixed is None else mixed + product
        peak[slot] = new
        if step:
            shrink = jnp.exp2(old - new)
            total[slot] = total[slot] * shrink + added
            mix[slot] = mix[slot] * shrink + mixed
        else:
            total[slot] = added
            mix[slot] = mixed

    for side, query_ref in enumerate((own_ref, other_ref)):
        owner = part if side == 0 else part + 1 - 2 * core

        def one_head(head, _):
            group = lax.div(owner * heads + head, GROUP)
            mine = lax.rem(group, 2) == core
            slot = side * heads + head
            if step == 0:
                pl.when(mine)(lambda: update(slot, query_ref, head, blocks))
                return _
            up = mine & (here >= step)
            if count == 1:
                pl.when(up)(lambda: update(slot, query_ref, head, blocks))
            else:
                down = mine & (here + step >= RING)
                pl.when(up & down)(lambda: update(slot, query_ref, head, blocks))
                pl.when(up & jnp.logical_not(down))(
                    lambda: update(slot, query_ref, head, blocks[:1])
                )
                pl.when(down & jnp.logical_not(up))(
                    lambda: update(slot, query_ref, head, blocks[1:])
                )
            return _

        lax.fori_loop(0, heads, one_head, 0)
        if last:
            for head in range(heads):
                mine = lax.rem(lax.div(owner * heads + head, GROUP), 2) == core
                slot = side * heads + head
                share = 1.0 / jnp.sum(total[slot], axis=1, keepdims=True)
                outs[side][:, head * HD : (head + 1) * HD] = jnp.where(
                    mine, mix[slot] * share, 0.0
                ).astype(bf16)


def attend(step, last, own, other, blocks, state):
    heads, rows, _ = own.shape
    shape = jax.ShapeDtypeStruct((2 * heads, rows, HD), f32)
    results = [jax.ShapeDtypeStruct((rows, heads * HD), bf16)] * 2 if last else []
    first = 2 + len(blocks)
    outs = pl.pallas_call(
        lambda *refs: attend_kernel(step, last, *refs),
        out_shape=results + [shape] * 3,
        in_specs=vmem(first + len(state)),
        out_specs=vmem(len(results) + 3),
        input_output_aliases={first + k: len(results) + k for k in range(len(state))},
        name="attend",
        **params(16, 8 * heads * rows * 512 * HD * len(blocks), 4 * MIB),
    )(own, other, *blocks, *state)
    return outs[:2] if last else outs


def own_group(x):
    part = part_index()
    one = lax.ppermute(x, MP, [(0, 2), (2, 4), (4, 0), (1, 3), (3, 7)])
    two = lax.ppermute(x, MP, [(2, 6), (4, 2), (6, 4), (1, 5), (5, 3)])
    key = jnp.where(part == 0, x, jnp.where((part == 5) | (part == 6), two, one))
    value = jnp.where(part >= 5, x, jnp.where(part == 0, one, two))
    return jnp.concatenate([key, value], axis=1)


def local(
    features,
    queries,
    anchor_frame,
    anchor_patch,
    time_offset,
    space_offset,
    value_weight,
    point_weight,
    point_bias,
    output_weight,
    project_weight,
    norm_gain,
    query_weight,
    query_bias,
    cache_weight,
    cache_bias,
):
    part = part_index()
    frames, patches, feature_width = features.shape
    rows = queries.shape[0]
    model_width = project_weight.shape[1]

    place, projected = begin(
        queries,
        point_weight,
        point_bias,
        anchor_frame,
        anchor_patch,
        time_offset,
        space_offset,
        features.reshape(frames * patches, feature_width),
        value_weight,
    )
    sibling = turned(2, 1)
    across = [(2 * z + 1, 2 * z + 2) for z in range(RING - 1)]
    across += [(target, source) for source, target in across]
    nearby = [lax.ppermute(place, TM, across), lax.ppermute(place, "tx", sibling)]
    columns = [projected[0]] + [
        lax.ppermute(projected[step], "my", turned(4, step)) for step in (1, 2, 3)
    ]
    values = []
    for block in columns:
        values += [block, lax.ppermute(block, "mc", turned(2, 1))]
    weight_columns = [output_weight] + [
        lax.ppermute(output_weight, "my", turned(4, step)) for step in (1, 2, 3)
    ]
    nearby, weight_columns = lax.optimization_barrier((nearby, weight_columns))
    weights = []
    for block in weight_columns:
        weights += [block, lax.ppermute(block, "mc", turned(2, 1))]

    theirs = sample(values, jnp.concatenate(nearby, axis=1), frames, bf16)
    mine = sample(values, place, frames, f32)
    far = lax.ppermute(theirs[:rows], TM, across)
    near = lax.ppermute(theirs[rows:], "tx", sibling)
    sampled = (mine + far.astype(f32) + near.astype(f32)).astype(bf16)
    samples = gather_blocks(sampled)

    columns = model_columns(samples, weights, queries, project_weight, norm_gain[None])
    blocks = gather_blocks(columns)

    positions = (time_index() * rows + jnp.arange(rows, dtype=jnp.int32)).astype(f32)
    frequency = rope_base ** (-2.0 * jnp.arange(HD // 2, dtype=f32) / HD)
    angles = positions[:, None] * frequency[None, :]
    cosine, sine = jnp.cos(angles), jnp.sin(angles)
    cosine = jnp.concatenate([cosine, cosine], axis=1)
    sine = jnp.concatenate([-sine, sine], axis=1)
    turned_queries, key_value = head_states(
        blocks,
        model_width,
        query_weight,
        cache_weight,
        query_bias[None],
        cache_bias[None],
        (cosine, sine),
    )
    own = own_group(key_value)
    other = lax.ppermute(own, "tx", turned(2, 1))
    heads = query_weight.shape[1] // HD
    other_queries = lax.ppermute(turned_queries, "mc", turned(2, 1))

    up = down = jnp.concatenate([own, other], axis=0)
    state = ()
    for step in range(RING // 2 + 1):
        last = step == RING // 2
        blocks = [up] if step == 0 or last else [up, down]
        if not last:
            if step > 0:
                up, down, state = lax.optimization_barrier((up, down, state))
            pairs = [(i, i + 1) for i in range(step, RING - 1)]
            up = lax.ppermute(up, "tz", pairs)
            if step + 1 < RING // 2:
                down = lax.ppermute(down, "tz", turned(RING, -1))
        state = attend(step, last, turned_queries, other_queries, blocks, state)
    mixed, others = state
    others = lax.ppermute(others, "mc", turned(2, 1))
    attention = []
    for head in range(heads):
        mine = lax.rem((part * heads + head) // GROUP, 2) == lax.axis_index("mc")
        lanes = slice(head * HD, (head + 1) * HD)
        attention.append(jnp.where(mine, mixed[:, lanes], others[:, lanes]))
    attention = jnp.concatenate(attention, axis=1)
    return (attention, key_value)


def solution(mesh):
    finer = Mesh(
        mesh.devices.reshape(mesh.shape["dp"], RING, 2, 4, 2), ("dp", "tz", "tx", "my", "mc")
    )
    time = ("dp", *TM)
    placed = (
        P(time, MP, None),
        P(time, None),
        P(time),
        P(time),
        P(time, None, None),
        P(None, time, None, None),
        P(),
        P(),
        P(),
        P(MP, None),
        P(None, MP),
        P(MP),
        P(None, MP),
        P(MP),
        P(None, MP),
        P(MP),
    )
    return jax.shard_map(
        local,
        mesh=finer,
        in_specs=placed,
        out_specs=(P(time, MP), P(time, MP)),
        check_vma=False,
    )
```

```python
import jax
import jax.numpy as jnp
from jax import lax
from jax.experimental import pallas as pl
from jax.experimental.pallas import tpu as pltpu
from jax.sharding import Mesh
from jax.sharding import PartitionSpec as P

AH = 8
AHD = 128
POINTS = 4
GRID = 24
KVH = 4
HD = 128
GROUP = 7
PARTS = 8
RING = 8
TM = ("tz", "tx")
MP = ("my", "mc")

rope_base = 1000000.0
epsilon = 1e-06
masked = -1e30
MIB = 1 << 20

f32 = jnp.float32
bf16 = jnp.bfloat16


def part_index():
    return lax.axis_index("my") * 2 + lax.axis_index("mc")


def time_index():
    return lax.axis_index("tz") * 2 + lax.axis_index("tx")


def gathered_source(place):
    step, other = place // 2, place % 2
    row = lax.rem(lax.axis_index("my") - step + 4, 4)
    core = lax.axis_index("mc")
    return row * 2 + (1 - core if other else core)


def turned(size, step):
    return [(i, (i + step) % size) for i in range(size)]


def gather_blocks(x):
    columns = [x] + [lax.ppermute(x, "my", turned(4, step)) for step in (1, 2, 3)]
    blocks = []
    for block in columns:
        blocks += [block, lax.ppermute(block, "mc", turned(2, 1))]
    return blocks


def dot(a, b):
    return jnp.dot(a, b, preferred_element_type=f32)


def params(mib, flops=0, read=0):
    return dict(
        compiler_params=pltpu.CompilerParams(vmem_limit_bytes=mib * MIB),
        cost_estimate=pl.CostEstimate(flops=flops, bytes_accessed=read, transcendentals=0),
    )


def vmem(count):
    return [pl.BlockSpec(memory_space=pltpu.VMEM)] * count


def begin_kernel(*refs):
    inputs, place_ref, outs = refs[:9], refs[9], refs[10:14]
    arrived, (held, arriving) = refs[14:23], refs[23:]
    part = part_index()
    copies = []
    for k, (source, target) in enumerate(zip(inputs, arrived)):
        if k == 5:
            source = source.at[part]
        if k == 6:
            source = source.at[:, part]
        copies.append(pltpu.make_async_copy(source, target, arriving.at[k]))
    for copy in copies:
        copy.start()
    queries, point_weight, bias, frame, patch, time, space, features, value_weight = arrived
    for copy in copies[:7]:
        copy.wait()
    logits = lax.dot_general(
        point_weight[...], queries[...], (((1,), (1,)), ((), ())), preferred_element_type=f32
    )
    columns = AH * POINTS
    on_diagonal = lax.broadcasted_iota(jnp.int32, (columns, columns), 0) == (
        lax.broadcasted_iota(jnp.int32, (columns, columns), 1)
    )
    logits = logits + jnp.sum(jnp.where(on_diagonal, bias[...], 0.0), axis=1, keepdims=True)
    own = logits[:POINTS]
    for head in range(1, AH):
        own = jnp.where(part == head, logits[head * POINTS : (head + 1) * POINTS], own)
    share = jnp.exp(own - jnp.max(own, axis=0, keepdims=True))
    share = share / jnp.sum(share, axis=0, keepdims=True)
    patch = patch[...].astype(f32)
    row = jnp.floor((patch + 0.5) * (1.0 / GRID))
    place_ref[0:POINTS] = frame[...].astype(f32) + time[...]
    place_ref[POINTS : 2 * POINTS] = row + space[0]
    place_ref[2 * POINTS : 3 * POINTS] = (patch - row * GRID) + space[1]
    place_ref[3 * POINTS :] = share
    for copy in copies[7:]:
        copy.wait()
    for pair in range(PARTS // 2):
        both = dot(features[...], value_weight[:, pair * 256 : pair * 256 + 256]).astype(bf16)
        held[2 * pair] = both[:, :AHD]
        held[2 * pair + 1] = both[:, AHD:]
    chip = lax.axis_index("my")
    for step in range(4):
        first = 2 * lax.rem(chip + step, 4)
        outs[step][0] = held[first]
        outs[step][1] = held[first + 1]


def begin(queries, weight, bias, frame, patch, time_offset, space_offset, features, value_weight):
    rows, lines = queries.shape[0], features.shape[0]
    inputs = (
        queries,
        weight.T,
        bias[None],
        frame[None],
        patch[None],
        time_offset.transpose(1, 2, 0),
        space_offset.transpose(0, 2, 3, 1),
        features,
        value_weight,
    )
    held = [pltpu.VMEM(x.shape, x.dtype) for x in inputs]
    held[5] = pltpu.VMEM((POINTS, rows), f32)
    held[6] = pltpu.VMEM((2, POINTS, rows), f32)
    place, *projected = pl.pallas_call(
        begin_kernel,
        out_shape=[jax.ShapeDtypeStruct((4 * POINTS, rows), f32)]
        + [jax.ShapeDtypeStruct((2, lines, AHD), bf16)] * 4,
        in_specs=[pl.BlockSpec(memory_space=pltpu.HBM)] * len(inputs),
        out_specs=vmem(5),
        scratch_shapes=held
        + [pltpu.VMEM((PARTS, lines, AHD), bf16), pltpu.SemaphoreType.DMA((len(inputs),))],
        name="begin",
        **params(60, 2 * lines * value_weight.size, 4 * MIB),
    )(*inputs)
    return place, projected


def hat(distance):
    return jnp.maximum(1.0 - jnp.abs(distance), 0.0)


def sample_kernel(frames, rows_each, place_ref, *refs):
    values, out_ref, spread, stacked = refs[:PARTS], refs[PARTS], refs[PARTS + 1], refs[PARTS + 2]
    count = place_ref.shape[1]
    block = frames * rows_each * GRID
    core = lax.axis_index("mc")
    first = (time_index() * frames).astype(f32)
    cell = lax.broadcasted_iota(jnp.int32, (GRID, count), 0).astype(f32)
    frame_at = [place_ref[k : k + 1, :] for k in range(POINTS)]
    row_at = [place_ref[POINTS + k : POINTS + k + 1, :] for k in range(POINTS)]
    share = [place_ref[3 * POINTS + k : 3 * POINTS + k + 1, :] for k in range(POINTS)]
    column_hat = [
        hat(cell - place_ref[2 * POINTS + k : 2 * POINTS + k + 1, :]) for k in range(POINTS)
    ]
    frame_hat = [
        [share[k] * hat(first + float(f) - frame_at[k]) for k in range(POINTS)]
        for f in range(frames)
    ]
    for step in range(PARTS):
        top = gathered_source(step) * rows_each
        row_hat = [
            [hat((top + r).astype(f32) - row_at[k]) for k in range(POINTS)]
            for r in range(rows_each)
        ]
        pieces = []
        for f in range(frames):
            for r in range(rows_each):
                total = (frame_hat[f][0] * row_hat[r][0]) * column_hat[0]
                for k in range(1, POINTS):
                    total = total + (frame_hat[f][k] * row_hat[r][k]) * column_hat[k]
                pieces.append(total)
        spread[step * block : (step + 1) * block, :] = jnp.concatenate(pieces, axis=0).astype(bf16)
        stacked[step * block : (step + 1) * block, :] = values[step][core]
    turned_values = stacked[...].T
    for lo in range(0, count, 256):
        out = dot(turned_values, spread[:, lo : lo + 256])
        out_ref[lo : lo + 256, :] = out.T.astype(out_ref.dtype)


def sample(values, place, frames, kind):
    _, rows, width = values[0].shape
    count = place.shape[1]
    rows_each = GRID // PARTS
    return pl.pallas_call(
        lambda *refs: sample_kernel(frames, rows_each, *refs),
        out_shape=jax.ShapeDtypeStruct((count, width), kind),
        in_specs=vmem(1 + PARTS),
        out_specs=pl.BlockSpec(memory_space=pltpu.VMEM),
        scratch_shapes=[
            pltpu.VMEM((PARTS * rows, count), bf16),
            pltpu.VMEM((PARTS * rows, width), bf16),
        ],
        name="sample_values",
        **params(10, 2 * PARTS * rows * width * count, 4 * PARTS * rows * width),
    )(place, *values)


def model_kernel(*refs):
    samples, weights = refs[:PARTS], refs[PARTS : PARTS + 2]
    queries_ref, project_ref, gain_ref, out_ref = refs[PARTS + 2 :]
    width = project_ref.shape[0]
    mixed = queries_ref[...].astype(f32)
    for place in range(PARTS):
        top = place // 2 * AHD
        mixed = mixed + dot(samples[place][...], weights[place % 2][top : top + AHD, :])
    visual = lax.dot_general(
        mixed.astype(bf16),
        project_ref[...],
        (((1,), (1,)), ((), ())),
        preferred_element_type=f32,
    )
    squares = jnp.sum(visual * visual, axis=1, keepdims=True)
    high = squares.astype(bf16).astype(f32)
    middle = (squares - high).astype(bf16).astype(f32)
    low = squares - high - middle
    scaled = visual * gain_ref[...]
    out_ref[:, :width] = scaled.astype(bf16)
    extra = out_ref.shape[1] - width
    lane = lax.broadcasted_iota(jnp.int32, (scaled.shape[0], extra), 1)
    terms = jnp.where(lane == 0, high, jnp.where(lane == 1, middle, jnp.where(lane == 2, low, 0.0)))
    out_ref[:, width:] = terms.astype(bf16)


def model_columns(samples, weights, queries, project_weight, gain):
    rows, width = queries.shape[0], project_weight.shape[1]
    return pl.pallas_call(
        model_kernel,
        out_shape=jax.ShapeDtypeStruct((rows, width + 64), bf16),
        in_specs=vmem(PARTS + 5),
        out_specs=pl.BlockSpec(memory_space=pltpu.VMEM),
        name="model_columns",
        **params(8, 2 * rows * queries.shape[1] * (queries.shape[1] + width), 4 * MIB),
    )(*samples, *weights, queries, project_weight.T, gain)


def turn(vectors, cosine, sine):
    return vectors * cosine + pltpu.roll(vectors, HD // 2, 1) * sine


def heads_kernel(width, *refs):
    inputs, (query_out, cache_out), arrived = refs[:14], refs[14:16], refs[16:30]
    arriving = refs[30]
    copies = [
        pltpu.make_async_copy(source, target, arriving.at[k])
        for k, (source, target) in enumerate(zip(inputs, arrived))
    ]
    for copy in copies:
        copy.start()
    cache_ref, cache_bias, cosine, sine = arrived[:4]
    blocks, (query_ref, query_bias) = arrived[4:12], arrived[12:]
    rows = blocks[0].shape[0]
    lines = [
        pl.ds(pl.multiple_of(gathered_source(place) * width, 64), width)
        for place in range(PARTS)
    ]
    squares = jnp.zeros((rows, 1), f32)
    cached = jnp.zeros((rows, cache_ref.shape[1]), f32)
    for copy in copies[:4]:
        copy.wait()
    for place in range(PARTS):
        copies[4 + place].wait()
        cached = cached + dot(blocks[place][:, :width], cache_ref[lines[place], :])
        terms = blocks[place][:, width:].astype(f32)
        squares = squares + jnp.sum(terms, axis=1, keepdims=True)
    scale = lax.rsqrt(squares / float(PARTS * width) + epsilon)
    cached = cached * scale + cache_bias[...]
    is_key = part_index() < KVH
    cache_out[...] = jnp.where(is_key, turn(cached, cosine[...], sine[...]), cached).astype(bf16)
    for copy in copies[12:]:
        copy.wait()
    queries = jnp.zeros((rows, query_ref.shape[1]), f32)
    for place in range(PARTS):
        queries = queries + dot(blocks[place][:, :width], query_ref[lines[place], :])
    queries = queries * scale + query_bias[...]
    for head in range(query_ref.shape[1] // HD):
        vectors = turn(queries[:, head * HD : (head + 1) * HD], cosine[...], sine[...])
        query_out[head] = vectors.astype(bf16)


def head_states(blocks, width, query_weight, cache_weight, query_bias, cache_bias, tables):
    rows = blocks[0].shape[0]
    inputs = (cache_weight, cache_bias, *tables, *blocks, query_weight, query_bias)
    return pl.pallas_call(
        lambda *refs: heads_kernel(width, *refs),
        out_shape=[
            jax.ShapeDtypeStruct((query_weight.shape[1] // HD, rows, HD), bf16),
            jax.ShapeDtypeStruct((rows, cache_weight.shape[1]), bf16),
        ],
        in_specs=[pl.BlockSpec(memory_space=pltpu.HBM)] * len(inputs),
        out_specs=vmem(2),
        scratch_shapes=[pltpu.VMEM(x.shape, x.dtype) for x in inputs]
        + [pltpu.SemaphoreType.DMA((len(inputs),))],
        name="head_states",
        **params(51, 2 * rows * (query_weight.size + cache_weight.size), 6 * MIB),
    )(*inputs)


def attend_kernel(step, last, own_ref, other_ref, *refs):
    count = 1 if step == 0 or last else 2
    blocks = refs[:count]
    outs, (peak, total, mix) = refs[count + (3 if step else 0) : -3], refs[-3:]
    heads, rows, _ = own_ref.shape
    part, core = part_index(), lax.axis_index("mc")
    here, half = lax.axis_index("tz"), lax.axis_index("tx")
    factor = HD ** (-0.5) * 1.4426950408889634

    def update(slot, query_ref, head, used):
        query = query_ref[head]
        pieces = []
        for block in used:
            scores = (
                lax.dot_general(
                    query, block[:, :HD], (((1,), (1,)), ((), ())), preferred_element_type=f32
                )
                * factor
            )
            if step == 0:
                row = lax.broadcasted_iota(jnp.int32, scores.shape, 0) + half * rows
                column = lax.broadcasted_iota(jnp.int32, scores.shape, 1)
                column = jnp.where(column < rows, column + half * rows, column - half * rows)
                scores = jnp.where(column <= row, scores, masked)
            pieces += [scores[:, lo : lo + HD] for lo in range(0, scores.shape[1], HD)]
        top = pieces[0]
        for piece in pieces[1:]:
            top = jnp.maximum(top, piece)
        new = jnp.max(top, axis=1, keepdims=True)
        if step:
            old = peak[slot]
            new = jnp.maximum(old, new)
        else:
            new = jnp.broadcast_to(new, (rows, HD))
        weights = [jnp.exp2(piece - new) for piece in pieces]
        added = weights[0]
        for piece in weights[1:]:
            added = added + piece
        each = len(pieces) // len(used)
        mixed = None
        for k, block in enumerate(used):
            part_weights = jnp.concatenate(
                [piece.astype(bf16) for piece in weights[k * each : (k + 1) * each]], axis=1
            )
            product = dot(part_weights, block[:, HD:])
            mixed = product if mixed is None else mixed + product
        peak[slot] = new
        if step:
            shrink = jnp.exp2(old - new)
            total[slot] = total[slot] * shrink + added
            mix[slot] = mix[slot] * shrink + mixed
        else:
            total[slot] = added
            mix[slot] = mixed

    for side, query_ref in enumerate((own_ref, other_ref)):
        owner = part if side == 0 else part + 1 - 2 * core

        def one_head(head, _):
            group = lax.div(owner * heads + head, GROUP)
            mine = lax.rem(group, 2) == core
            slot = side * heads + head
            if step == 0:
                pl.when(mine)(lambda: update(slot, query_ref, head, blocks))
                return _
            up = mine & (here >= step)
            if count == 1:
                pl.when(up)(lambda: update(slot, query_ref, head, blocks))
            else:
                down = mine & (here + step >= RING)
                pl.when(up & down)(lambda: update(slot, query_ref, head, blocks))
                pl.when(up & jnp.logical_not(down))(
                    lambda: update(slot, query_ref, head, blocks[:1])
                )
                pl.when(down & jnp.logical_not(up))(
                    lambda: update(slot, query_ref, head, blocks[1:])
                )
            return _

        lax.fori_loop(0, heads, one_head, 0)
        if last:
            for head in range(heads):
                mine = lax.rem(lax.div(owner * heads + head, GROUP), 2) == core
                slot = side * heads + head
                share = 1.0 / jnp.sum(total[slot], axis=1, keepdims=True)
                outs[side][:, head * HD : (head + 1) * HD] = jnp.where(
                    mine, mix[slot] * share, 0.0
                ).astype(bf16)


def attend(step, last, own, other, blocks, state):
    heads, rows, _ = own.shape
    shape = jax.ShapeDtypeStruct((2 * heads, rows, HD), f32)
    results = [jax.ShapeDtypeStruct((rows, heads * HD), bf16)] * 2 if last else []
    first = 2 + len(blocks)
    outs = pl.pallas_call(
        lambda *refs: attend_kernel(step, last, *refs),
        out_shape=results + [shape] * 3,
        in_specs=vmem(first + len(state)),
        out_specs=vmem(len(results) + 3),
        input_output_aliases={first + k: len(results) + k for k in range(len(state))},
        name="attend",
        **params(16, 8 * heads * rows * 512 * HD * len(blocks), 4 * MIB),
    )(own, other, *blocks, *state)
    return outs[:2] if last else outs


def own_group(x):
    part = part_index()
    blocks = [x] + [lax.ppermute(x, "my", turned(4, step)) for step in (1, 2, 3)]
    nearest = jnp.where((part == 5) | (part >= 6), blocks[2], blocks[1])
    key = jnp.where(part == 0, blocks[0], nearest)
    value = jnp.where(part == 0, blocks[2], jnp.where(part >= 5, blocks[0], blocks[3]))
    return jnp.concatenate([key, value], axis=1)


def local(
    features,
    queries,
    anchor_frame,
    anchor_patch,
    time_offset,
    space_offset,
    value_weight,
    point_weight,
    point_bias,
    output_weight,
    project_weight,
    norm_gain,
    query_weight,
    query_bias,
    cache_weight,
    cache_bias,
):
    part = part_index()
    frames, patches, feature_width = features.shape
    rows = queries.shape[0]
    model_width = project_weight.shape[1]

    place, projected = begin(
        queries,
        point_weight,
        point_bias,
        anchor_frame,
        anchor_patch,
        time_offset,
        space_offset,
        features.reshape(frames * patches, feature_width),
        value_weight,
    )
    sibling = turned(2, 1)
    across = [(2 * z + 1, 2 * z + 2) for z in range(RING - 1)]
    across += [(target, source) for source, target in across]
    nearby = [lax.ppermute(place, TM, across), lax.ppermute(place, "tx", sibling)]
    columns = [projected[0]] + [
        lax.ppermute(projected[step], "my", turned(4, step)) for step in (1, 2, 3)
    ]
    columns, nearby, output_weight = lax.optimization_barrier((columns, nearby, output_weight))
    values = []
    for block in columns:
        values += [block, lax.ppermute(block, "mc", turned(2, 1))]
    weight_columns = [output_weight] + [
        lax.ppermute(output_weight, "my", turned(4, step)) for step in (1, 2, 3)
    ]
    theirs = sample(values, jnp.concatenate(nearby, axis=1), frames, bf16)
    mine = sample(values, place, frames, f32)
    far = lax.ppermute(theirs[:rows], TM, across)
    near = lax.ppermute(theirs[rows:], "tx", sibling)
    far, near, mine, weight_columns = lax.optimization_barrier((far, near, mine, weight_columns))
    weights = jnp.concatenate(weight_columns, axis=0)
    weights = [weights, lax.ppermute(weights, "mc", turned(2, 1))]
    sampled = (mine + far.astype(f32) + near.astype(f32)).astype(bf16)
    sampled_columns = [sampled] + [
        lax.ppermute(sampled, "my", turned(4, step)) for step in (1, 2, 3)
    ]
    sampled_columns, weights = lax.optimization_barrier((sampled_columns, weights))
    samples = []
    for block in sampled_columns:
        samples += [block, lax.ppermute(block, "mc", turned(2, 1))]

    columns = model_columns(samples, weights, queries, project_weight, norm_gain[None])
    blocks = gather_blocks(columns)

    positions = (time_index() * rows + jnp.arange(rows, dtype=jnp.int32)).astype(f32)
    frequency = rope_base ** (-2.0 * jnp.arange(HD // 2, dtype=f32) / HD)
    angles = positions[:, None] * frequency[None, :]
    cosine, sine = jnp.cos(angles), jnp.sin(angles)
    cosine = jnp.concatenate([cosine, cosine], axis=1)
    sine = jnp.concatenate([-sine, sine], axis=1)
    turned_queries, key_value = head_states(
        blocks,
        model_width,
        query_weight,
        cache_weight,
        query_bias[None],
        cache_bias[None],
        (cosine, sine),
    )
    own = own_group(key_value)
    other = lax.ppermute(own, "tx", turned(2, 1))
    heads = query_weight.shape[1] // HD
    other_queries = lax.ppermute(turned_queries, "mc", turned(2, 1))

    up = down = jnp.concatenate([own, other], axis=0)
    state = ()
    for step in range(RING // 2 + 1):
        last = step == RING // 2
        blocks = [up] if step == 0 or last else [up, down]
        if not last:
            if step > 0:
                up, down, state = lax.optimization_barrier((up, down, state))
            pairs = [(i, i + 1) for i in range(step, RING - 1)]
            up = lax.ppermute(up, "tz", pairs)
            if step + 1 < RING // 2:
                down = lax.ppermute(down, "tz", turned(RING, -1))
        state = attend(step, last, turned_queries, other_queries, blocks, state)
    mixed, others = state
    others = lax.ppermute(others, "mc", turned(2, 1))
    attention = []
    for head in range(heads):
        mine = lax.rem((part * heads + head) // GROUP, 2) == lax.axis_index("mc")
        lanes = slice(head * HD, (head + 1) * HD)
        attention.append(jnp.where(mine, mixed[:, lanes], others[:, lanes]))
    attention = jnp.concatenate(attention, axis=1)
    return (attention, key_value)


def solution(mesh):
    finer = Mesh(
        mesh.devices.reshape(mesh.shape["dp"], RING, 2, 4, 2), ("dp", "tz", "tx", "my", "mc")
    )
    time = ("dp", *TM)
    placed = (
        P(time, MP, None),
        P(time, None),
        P(time),
        P(time),
        P(time, None, None),
        P(None, time, None, None),
        P(),
        P(),
        P(),
        P(MP, None),
        P(None, MP),
        P(MP),
        P(None, MP),
        P(MP),
        P(None, MP),
        P(MP),
    )
    return jax.shard_map(
        local,
        mesh=finer,
        in_specs=placed,
        out_specs=(P(time, MP), P(time, MP)),
        check_vma=False,
    )
```

```python
import jax
import jax.numpy as jnp
from jax import lax
from jax.experimental import pallas as pl
from jax.experimental.pallas import tpu as pltpu
from jax.sharding import Mesh
from jax.sharding import PartitionSpec as P

AH = 8
AHD = 128
POINTS = 4
GRID = 24
KVH = 4
HD = 128
GROUP = 7
PARTS = 8
RING = 8
TM = ("tz", "tx")
MP = ("my", "mc")

rope_base = 1000000.0
epsilon = 1e-06
masked = -1e30
MIB = 1 << 20

f32 = jnp.float32
bf16 = jnp.bfloat16


def part_index():
    return lax.axis_index("my") * 2 + lax.axis_index("mc")


def time_index():
    return lax.axis_index("tz") * 2 + lax.axis_index("tx")


def gathered_source(place):
    step, other = place // 2, place % 2
    row = lax.rem(lax.axis_index("my") - step + 4, 4)
    core = lax.axis_index("mc")
    return row * 2 + (1 - core if other else core)


def turned(size, step):
    return [(i, (i + step) % size) for i in range(size)]


def gather_blocks(x):
    columns = [x] + [lax.ppermute(x, "my", turned(4, step)) for step in (1, 2, 3)]
    blocks = []
    for block in columns:
        blocks += [block, lax.ppermute(block, "mc", turned(2, 1))]
    return blocks


def dot(a, b):
    return jnp.dot(a, b, preferred_element_type=f32)


def params(mib, flops=0, read=0):
    return dict(
        compiler_params=pltpu.CompilerParams(vmem_limit_bytes=mib * MIB),
        cost_estimate=pl.CostEstimate(flops=flops, bytes_accessed=read, transcendentals=0),
    )


def vmem(count):
    return [pl.BlockSpec(memory_space=pltpu.VMEM)] * count


def begin_kernel(*refs):
    inputs, place_ref, outs = refs[:9], refs[9], refs[10:14]
    arrived, (held, arriving) = refs[14:23], refs[23:]
    part = part_index()
    copies = []
    for k, (source, target) in enumerate(zip(inputs, arrived)):
        if k == 5:
            source = source.at[part]
        if k == 6:
            source = source.at[:, part]
        copies.append(pltpu.make_async_copy(source, target, arriving.at[k]))
    for copy in copies:
        copy.start()
    queries, point_weight, bias, frame, patch, time, space, features, value_weight = arrived
    for copy in copies[:7]:
        copy.wait()
    logits = lax.dot_general(
        point_weight[...], queries[...], (((1,), (1,)), ((), ())), preferred_element_type=f32
    )
    columns = AH * POINTS
    on_diagonal = lax.broadcasted_iota(jnp.int32, (columns, columns), 0) == (
        lax.broadcasted_iota(jnp.int32, (columns, columns), 1)
    )
    logits = logits + jnp.sum(jnp.where(on_diagonal, bias[...], 0.0), axis=1, keepdims=True)
    own = logits[:POINTS]
    for head in range(1, AH):
        own = jnp.where(part == head, logits[head * POINTS : (head + 1) * POINTS], own)
    share = jnp.exp(own - jnp.max(own, axis=0, keepdims=True))
    share = share / jnp.sum(share, axis=0, keepdims=True)
    patch = patch[...].astype(f32)
    row = jnp.floor((patch + 0.5) * (1.0 / GRID))
    place_ref[0:POINTS] = frame[...].astype(f32) + time[...]
    place_ref[POINTS : 2 * POINTS] = row + space[0]
    place_ref[2 * POINTS : 3 * POINTS] = (patch - row * GRID) + space[1]
    place_ref[3 * POINTS :] = share
    for copy in copies[7:]:
        copy.wait()
    for pair in range(PARTS // 2):
        both = dot(features[...], value_weight[:, pair * 256 : pair * 256 + 256]).astype(bf16)
        held[2 * pair] = both[:, :AHD]
        held[2 * pair + 1] = both[:, AHD:]
    chip = lax.axis_index("my")
    for step in range(4):
        first = 2 * lax.rem(chip + step, 4)
        outs[step][0] = held[first]
        outs[step][1] = held[first + 1]


def begin(queries, weight, bias, frame, patch, time_offset, space_offset, features, value_weight):
    rows, lines = queries.shape[0], features.shape[0]
    inputs = (
        queries,
        weight.T,
        bias[None],
        frame[None],
        patch[None],
        time_offset.transpose(1, 2, 0),
        space_offset.transpose(0, 2, 3, 1),
        features,
        value_weight,
    )
    held = [pltpu.VMEM(x.shape, x.dtype) for x in inputs]
    held[5] = pltpu.VMEM((POINTS, rows), f32)
    held[6] = pltpu.VMEM((2, POINTS, rows), f32)
    place, *projected = pl.pallas_call(
        begin_kernel,
        out_shape=[jax.ShapeDtypeStruct((4 * POINTS, rows), f32)]
        + [jax.ShapeDtypeStruct((2, lines, AHD), bf16)] * 4,
        in_specs=[pl.BlockSpec(memory_space=pltpu.HBM)] * len(inputs),
        out_specs=vmem(5),
        scratch_shapes=held
        + [pltpu.VMEM((PARTS, lines, AHD), bf16), pltpu.SemaphoreType.DMA((len(inputs),))],
        name="begin",
        **params(60, 2 * lines * value_weight.size, 4 * MIB),
    )(*inputs)
    return place, projected


def hat(distance):
    return jnp.maximum(1.0 - jnp.abs(distance), 0.0)


def sample_kernel(frames, rows_each, place_ref, *refs):
    values, outs, (spread, stacked) = refs[:PARTS], refs[PARTS:-2], refs[-2:]
    count = place_ref.shape[1]
    block = frames * rows_each * GRID
    core = lax.axis_index("mc")
    first = (time_index() * frames).astype(f32)
    cell = lax.broadcasted_iota(jnp.int32, (GRID, count), 0).astype(f32)
    frame_at = [place_ref[k : k + 1, :] for k in range(POINTS)]
    row_at = [place_ref[POINTS + k : POINTS + k + 1, :] for k in range(POINTS)]
    share = [place_ref[3 * POINTS + k : 3 * POINTS + k + 1, :] for k in range(POINTS)]
    column_hat = [
        hat(cell - place_ref[2 * POINTS + k : 2 * POINTS + k + 1, :]) for k in range(POINTS)
    ]
    frame_hat = [
        [share[k] * hat(first + float(f) - frame_at[k]) for k in range(POINTS)]
        for f in range(frames)
    ]
    for step in range(PARTS):
        top = gathered_source(step) * rows_each
        row_hat = [
            [hat((top + r).astype(f32) - row_at[k]) for k in range(POINTS)]
            for r in range(rows_each)
        ]
        pieces = []
        for f in range(frames):
            for r in range(rows_each):
                total = (frame_hat[f][0] * row_hat[r][0]) * column_hat[0]
                for k in range(1, POINTS):
                    total = total + (frame_hat[f][k] * row_hat[r][k]) * column_hat[k]
                pieces.append(total)
        spread[step * block : (step + 1) * block, :] = jnp.concatenate(pieces, axis=0).astype(bf16)
        stacked[step * block : (step + 1) * block, :] = values[step][core]
    turned_values = stacked[...].T
    rows = count // len(outs)
    for k, out_ref in enumerate(outs):
        out = dot(turned_values, spread[:, k * rows : (k + 1) * rows])
        out_ref[...] = out.T.astype(out_ref.dtype)


def sample(values, place, frames, kinds):
    _, rows, width = values[0].shape
    count = place.shape[1]
    rows_each = GRID // PARTS
    return pl.pallas_call(
        lambda *refs: sample_kernel(frames, rows_each, *refs),
        out_shape=[jax.ShapeDtypeStruct((count // len(kinds), width), kind) for kind in kinds],
        in_specs=vmem(1 + PARTS),
        out_specs=vmem(len(kinds)),
        scratch_shapes=[
            pltpu.VMEM((PARTS * rows, count), bf16),
            pltpu.VMEM((PARTS * rows, width), bf16),
        ],
        name="sample_values",
        **params(12, 2 * PARTS * rows * width * count, 4 * PARTS * rows * width),
    )(place, *values)


def model_kernel(*refs):
    samples, weights = refs[:PARTS], refs[PARTS : PARTS + 2]
    queries_ref, project_ref, gain_ref, out_ref = refs[PARTS + 2 :]
    width = project_ref.shape[0]
    mixed = queries_ref[...].astype(f32)
    for place in range(PARTS):
        top = place // 2 * AHD
        mixed = mixed + dot(samples[place][...], weights[place % 2][top : top + AHD, :])
    visual = lax.dot_general(
        mixed.astype(bf16),
        project_ref[...],
        (((1,), (1,)), ((), ())),
        preferred_element_type=f32,
    )
    squares = jnp.sum(visual * visual, axis=1, keepdims=True)
    high = squares.astype(bf16).astype(f32)
    middle = (squares - high).astype(bf16).astype(f32)
    low = squares - high - middle
    scaled = visual * gain_ref[...]
    out_ref[:, :width] = scaled.astype(bf16)
    extra = out_ref.shape[1] - width
    lane = lax.broadcasted_iota(jnp.int32, (scaled.shape[0], extra), 1)
    terms = jnp.where(lane == 0, high, jnp.where(lane == 1, middle, jnp.where(lane == 2, low, 0.0)))
    out_ref[:, width:] = terms.astype(bf16)


def model_columns(samples, weights, queries, project_weight, gain):
    rows, width = queries.shape[0], project_weight.shape[1]
    return pl.pallas_call(
        model_kernel,
        out_shape=jax.ShapeDtypeStruct((rows, width + 64), bf16),
        in_specs=vmem(PARTS + 5),
        out_specs=pl.BlockSpec(memory_space=pltpu.VMEM),
        name="model_columns",
        **params(8, 2 * rows * queries.shape[1] * (queries.shape[1] + width), 4 * MIB),
    )(*samples, *weights, queries, project_weight.T, gain)


def turn(vectors, cosine, sine):
    return vectors * cosine + pltpu.roll(vectors, HD // 2, 1) * sine


def heads_kernel(width, turned_part, *refs):
    inputs, out_ref, arrived, arriving = refs[:12], refs[12], refs[13:25], refs[25]
    copies = [
        pltpu.make_async_copy(source, target, arriving.at[k])
        for k, (source, target) in enumerate(zip(inputs, arrived))
    ]
    for copy in copies:
        copy.start()
    weight_ref, bias, cosine, sine = arrived[:4]
    blocks = arrived[4:]
    rows = blocks[0].shape[0]
    squares = jnp.zeros((rows, 1), f32)
    product = jnp.zeros((rows, weight_ref.shape[1]), f32)
    for copy in copies[:4]:
        copy.wait()
    for place in range(PARTS):
        copies[4 + place].wait()
        lines = pl.ds(pl.multiple_of(gathered_source(place) * width, 64), width)
        product = product + dot(blocks[place][:, :width], weight_ref[lines, :])
        terms = blocks[place][:, width:].astype(f32)
        squares = squares + jnp.sum(terms, axis=1, keepdims=True)
    scale = lax.rsqrt(squares / float(PARTS * width) + epsilon)
    product = product * scale + bias[...]
    for head in range(weight_ref.shape[1] // HD):
        plain = product[:, head * HD : (head + 1) * HD]
        vectors = turn(plain, cosine[...], sine[...])
        if turned_part is not None:
            vectors = jnp.where(part_index() < turned_part, vectors, plain)
        out_ref[head] = vectors.astype(bf16)


def head_states(blocks, width, weight, bias, tables, turned_part=None):
    rows = blocks[0].shape[0]
    inputs = (weight, bias[None], *tables, *blocks)
    return pl.pallas_call(
        lambda *refs: heads_kernel(width, turned_part, *refs),
        out_shape=jax.ShapeDtypeStruct((weight.shape[1] // HD, rows, HD), bf16),
        in_specs=[pl.BlockSpec(memory_space=pltpu.HBM)] * len(inputs),
        out_specs=pl.BlockSpec(memory_space=pltpu.VMEM),
        scratch_shapes=[pltpu.VMEM(x.shape, x.dtype) for x in inputs]
        + [pltpu.SemaphoreType.DMA((len(inputs),))],
        name="head_states",
        **params(51, 2 * rows * weight.size, 2 * MIB + 2 * weight.size),
    )(*inputs)


def attend_kernel(step, last, own_ref, other_ref, *refs):
    count = 1 if step == 0 or last else 2
    blocks = refs[:count]
    outs, (peak, total, mix) = refs[count + (3 if step else 0) : -3], refs[-3:]
    heads, rows, _ = own_ref.shape
    part, core = part_index(), lax.axis_index("mc")
    here, half = lax.axis_index("tz"), lax.axis_index("tx")
    factor = HD ** (-0.5) * 1.4426950408889634

    def update(slot, query_ref, head, used):
        query = query_ref[head]
        pieces = []
        for block in used:
            scores = (
                lax.dot_general(
                    query, block[:, :HD], (((1,), (1,)), ((), ())), preferred_element_type=f32
                )
                * factor
            )
            if step == 0:
                row = lax.broadcasted_iota(jnp.int32, scores.shape, 0) + half * rows
                column = lax.broadcasted_iota(jnp.int32, scores.shape, 1)
                column = jnp.where(column < rows, column + half * rows, column - half * rows)
                scores = jnp.where(column <= row, scores, masked)
            pieces += [scores[:, lo : lo + HD] for lo in range(0, scores.shape[1], HD)]
        top = pieces[0]
        for piece in pieces[1:]:
            top = jnp.maximum(top, piece)
        new = jnp.max(top, axis=1, keepdims=True)
        if step:
            old = peak[slot]
            new = jnp.maximum(old, new)
        else:
            new = jnp.broadcast_to(new, (rows, HD))
        weights = [jnp.exp2(piece - new) for piece in pieces]
        added = weights[0]
        for piece in weights[1:]:
            added = added + piece
        each = len(pieces) // len(used)
        mixed = None
        for k, block in enumerate(used):
            part_weights = jnp.concatenate(
                [piece.astype(bf16) for piece in weights[k * each : (k + 1) * each]], axis=1
            )
            product = dot(part_weights, block[:, HD:])
            mixed = product if mixed is None else mixed + product
        peak[slot] = new
        if step:
            shrink = jnp.exp2(old - new)
            total[slot] = total[slot] * shrink + added
            mix[slot] = mix[slot] * shrink + mixed
        else:
            total[slot] = added
            mix[slot] = mixed

    for side, query_ref in enumerate((own_ref, other_ref)):
        owner = part if side == 0 else part + 1 - 2 * core

        def one_head(head, _):
            group = lax.div(owner * heads + head, GROUP)
            mine = lax.rem(group, 2) == core
            slot = side * heads + head
            if step == 0:
                pl.when(mine)(lambda: update(slot, query_ref, head, blocks))
                return _
            up = mine & (here >= step)
            if count == 1:
                pl.when(up)(lambda: update(slot, query_ref, head, blocks))
            else:
                down = mine & (here + step >= RING)
                pl.when(up & down)(lambda: update(slot, query_ref, head, blocks))
                pl.when(up & jnp.logical_not(down))(
                    lambda: update(slot, query_ref, head, blocks[:1])
                )
                pl.when(down & jnp.logical_not(up))(
                    lambda: update(slot, query_ref, head, blocks[1:])
                )
            return _

        lax.fori_loop(0, heads, one_head, 0)
        if last:
            for head in range(heads):
                mine = lax.rem(lax.div(owner * heads + head, GROUP), 2) == core
                slot = side * heads + head
                share = 1.0 / jnp.sum(total[slot], axis=1, keepdims=True)
                outs[side][:, head * HD : (head + 1) * HD] = jnp.where(
                    mine, mix[slot] * share, 0.0
                ).astype(bf16)


def attend(step, last, own, other, blocks, state):
    heads, rows, _ = own.shape
    shape = jax.ShapeDtypeStruct((2 * heads, rows, HD), f32)
    results = [jax.ShapeDtypeStruct((rows, heads * HD), bf16)] * 2 if last else []
    first = 2 + len(blocks)
    outs = pl.pallas_call(
        lambda *refs: attend_kernel(step, last, *refs),
        out_shape=results + [shape] * 3,
        in_specs=vmem(first + len(state)),
        out_specs=vmem(len(results) + 3),
        input_output_aliases={first + k: len(results) + k for k in range(len(state))},
        name="attend",
        **params(16, 8 * heads * rows * 512 * HD * len(blocks), 4 * MIB),
    )(own, other, *blocks, *state)
    return outs[:2] if last else outs


def own_group(x, meanwhile):
    part = part_index()
    blocks = [x] + [lax.ppermute(x, "my", turned(4, step)) for step in (1, 2, 3)]
    blocks, meanwhile = lax.optimization_barrier((blocks, meanwhile))
    nearest = jnp.where((part == 5) | (part >= 6), blocks[2], blocks[1])
    key = jnp.where(part == 0, blocks[0], nearest)
    value = jnp.where(part == 0, blocks[2], jnp.where(part >= 5, blocks[0], blocks[3]))
    return jnp.concatenate([key, value], axis=1), meanwhile


def local(
    features,
    queries,
    anchor_frame,
    anchor_patch,
    time_offset,
    space_offset,
    value_weight,
    point_weight,
    point_bias,
    output_weight,
    project_weight,
    norm_gain,
    query_weight,
    query_bias,
    cache_weight,
    cache_bias,
):
    part = part_index()
    frames, patches, feature_width = features.shape
    rows = queries.shape[0]
    model_width = project_weight.shape[1]

    place, projected = begin(
        queries,
        point_weight,
        point_bias,
        anchor_frame,
        anchor_patch,
        time_offset,
        space_offset,
        features.reshape(frames * patches, feature_width),
        value_weight,
    )
    sibling = turned(2, 1)
    across = [(2 * z + 1, 2 * z + 2) for z in range(RING - 1)]
    across += [(target, source) for source, target in across]
    nearby = [lax.ppermute(place, TM, across), lax.ppermute(place, "tx", sibling)]
    columns = [projected[0]] + [
        lax.ppermute(projected[step], "my", turned(4, step)) for step in (1, 2, 3)
    ]
    columns, nearby, output_weight = lax.optimization_barrier((columns, nearby, output_weight))
    values = []
    for block in columns:
        values += [block, lax.ppermute(block, "mc", turned(2, 1))]
    weight_columns = [output_weight] + [
        lax.ppermute(output_weight, "my", turned(4, step)) for step in (1, 2, 3)
    ]
    places = jnp.concatenate([*nearby, place], axis=1)
    far, near, mine = sample(values, places, frames, (bf16, bf16, f32))
    far = lax.ppermute(far, TM, across)
    near = lax.ppermute(near, "tx", sibling)
    far, near, mine, weight_columns = lax.optimization_barrier((far, near, mine, weight_columns))
    weights = jnp.concatenate(weight_columns, axis=0)
    weights = [weights, lax.ppermute(weights, "mc", turned(2, 1))]
    sampled = (mine + far.astype(f32) + near.astype(f32)).astype(bf16)
    sampled_columns = [sampled] + [
        lax.ppermute(sampled, "my", turned(4, step)) for step in (1, 2, 3)
    ]
    sampled_columns, weights = lax.optimization_barrier((sampled_columns, weights))
    samples = []
    for block in sampled_columns:
        samples += [block, lax.ppermute(block, "mc", turned(2, 1))]

    columns = model_columns(samples, weights, queries, project_weight, norm_gain[None])
    blocks = gather_blocks(columns)

    positions = (time_index() * rows + jnp.arange(rows, dtype=jnp.int32)).astype(f32)
    frequency = rope_base ** (-2.0 * jnp.arange(HD // 2, dtype=f32) / HD)
    angles = positions[:, None] * frequency[None, :]
    cosine, sine = jnp.cos(angles), jnp.sin(angles)
    cosine = jnp.concatenate([cosine, cosine], axis=1)
    sine = jnp.concatenate([-sine, sine], axis=1)
    tables = (cosine, sine)
    key_value = head_states(blocks, model_width, cache_weight, cache_bias, tables, KVH)[0]
    turned_queries = head_states(blocks, model_width, query_weight, query_bias, tables)
    own, turned_queries = own_group(key_value, turned_queries)
    other = lax.ppermute(own, "tx", turned(2, 1))
    heads = query_weight.shape[1] // HD
    other_queries = lax.ppermute(turned_queries, "mc", turned(2, 1))
    other, other_queries = lax.optimization_barrier((other, other_queries))

    up = down = jnp.concatenate([own, other], axis=0)
    state = ()
    for step in range(RING // 2 + 1):
        last = step == RING // 2
        blocks = [up] if step == 0 or last else [up, down]
        if not last:
            if step > 0:
                up, down, state = lax.optimization_barrier((up, down, state))
            pairs = [(i, i + 1) for i in range(step, RING - 1)]
            up = lax.ppermute(up, "tz", pairs)
            if step + 1 < RING // 2:
                down = lax.ppermute(down, "tz", turned(RING, -1))
        state = attend(step, last, turned_queries, other_queries, blocks, state)
    mixed, others = state
    others = lax.ppermute(others, "mc", turned(2, 1))
    attention = []
    for head in range(heads):
        mine = lax.rem((part * heads + head) // GROUP, 2) == lax.axis_index("mc")
        lanes = slice(head * HD, (head + 1) * HD)
        attention.append(jnp.where(mine, mixed[:, lanes], others[:, lanes]))
    attention = jnp.concatenate(attention, axis=1)
    return (attention, key_value)


def solution(mesh):
    finer = Mesh(
        mesh.devices.reshape(mesh.shape["dp"], RING, 2, 4, 2), ("dp", "tz", "tx", "my", "mc")
    )
    time = ("dp", *TM)
    placed = (
        P(time, MP, None),
        P(time, None),
        P(time),
        P(time),
        P(time, None, None),
        P(None, time, None, None),
        P(),
        P(),
        P(),
        P(MP, None),
        P(None, MP),
        P(MP),
        P(None, MP),
        P(MP),
        P(None, MP),
        P(MP),
    )
    return jax.shard_map(
        local,
        mesh=finer,
        in_specs=placed,
        out_specs=(P(time, MP), P(time, MP)),
        check_vma=False,
    )
```

```python
import jax
import jax.numpy as jnp
from jax import lax
from jax.experimental import pallas as pl
from jax.experimental.pallas import tpu as pltpu
from jax.sharding import Mesh
from jax.sharding import PartitionSpec as P

AH = 8
AHD = 128
POINTS = 4
GRID = 24
KVH = 4
HD = 128
GROUP = 7
PARTS = 8
RING = 8
TM = ("tz", "tx")
MP = ("my", "mc")

rope_base = 1000000.0
epsilon = 1e-06
masked = -1e30
MIB = 1 << 20

f32 = jnp.float32
bf16 = jnp.bfloat16


def part_index():
    return lax.axis_index("my") * 2 + lax.axis_index("mc")


def time_index():
    return lax.axis_index("tz") * 2 + lax.axis_index("tx")


def gathered_source(place):
    step, other = place // 2, place % 2
    row = lax.rem(lax.axis_index("my") - step + 4, 4)
    core = lax.axis_index("mc")
    return row * 2 + (1 - core if other else core)


def turned(size, step):
    return [(i, (i + step) % size) for i in range(size)]


def gather_blocks(x):
    columns = [x] + [lax.ppermute(x, "my", turned(4, step)) for step in (1, 2, 3)]
    blocks = []
    for block in columns:
        blocks += [block, lax.ppermute(block, "mc", turned(2, 1))]
    return blocks


def dot(a, b):
    return jnp.dot(a, b, preferred_element_type=f32)


def params(mib, flops=0, read=0):
    return dict(
        compiler_params=pltpu.CompilerParams(vmem_limit_bytes=mib * MIB),
        cost_estimate=pl.CostEstimate(flops=flops, bytes_accessed=read, transcendentals=0),
    )


def vmem(count):
    return [pl.BlockSpec(memory_space=pltpu.VMEM)] * count


def begin_kernel(*refs):
    inputs, place_ref, outs = refs[:9], refs[9], refs[10:14]
    arrived, (held, arriving) = refs[14:23], refs[23:]
    part = part_index()
    copies = []
    for k, (source, target) in enumerate(zip(inputs[:8], arrived)):
        if k == 5:
            source = source.at[part]
        if k == 6:
            source = source.at[:, part]
        copies.append(pltpu.make_async_copy(source, target, arriving.at[k]))
    pairs = [slice(lo, lo + 2 * AHD) for lo in range(0, AH * AHD, 2 * AHD)]
    for k, lanes in enumerate(pairs):
        copies.append(
            pltpu.make_async_copy(
                inputs[8].at[:, lanes], arrived[8].at[:, lanes], arriving.at[8 + k]
            )
        )
    for copy in copies:
        copy.start()
    queries, point_weight, bias, frame, patch, time, space, features, value_weight = arrived
    for copy in copies[:7]:
        copy.wait()
    logits = lax.dot_general(
        point_weight[...], queries[...], (((1,), (1,)), ((), ())), preferred_element_type=f32
    )
    columns = AH * POINTS
    on_diagonal = lax.broadcasted_iota(jnp.int32, (columns, columns), 0) == (
        lax.broadcasted_iota(jnp.int32, (columns, columns), 1)
    )
    logits = logits + jnp.sum(jnp.where(on_diagonal, bias[...], 0.0), axis=1, keepdims=True)
    own = logits[:POINTS]
    for head in range(1, AH):
        own = jnp.where(part == head, logits[head * POINTS : (head + 1) * POINTS], own)
    share = jnp.exp(own - jnp.max(own, axis=0, keepdims=True))
    share = share / jnp.sum(share, axis=0, keepdims=True)
    patch = patch[...].astype(f32)
    row = jnp.floor((patch + 0.5) * (1.0 / GRID))
    place_ref[0:POINTS] = frame[...].astype(f32) + time[...]
    place_ref[POINTS : 2 * POINTS] = row + space[0]
    place_ref[2 * POINTS : 3 * POINTS] = (patch - row * GRID) + space[1]
    place_ref[3 * POINTS :] = share
    copies[7].wait()
    for pair, lanes in enumerate(pairs):
        copies[8 + pair].wait()
        both = dot(features[...], value_weight[:, lanes]).astype(bf16)
        held[2 * pair] = both[:, :AHD]
        held[2 * pair + 1] = both[:, AHD:]
    chip = lax.axis_index("my")
    for step in range(4):
        first = 2 * lax.rem(chip + step, 4)
        outs[step][0] = held[first]
        outs[step][1] = held[first + 1]


def begin(queries, weight, bias, frame, patch, time_offset, space_offset, features, value_weight):
    rows, lines = queries.shape[0], features.shape[0]
    inputs = (
        queries,
        weight.T,
        bias[None],
        frame[None],
        patch[None],
        time_offset.transpose(1, 2, 0),
        space_offset.transpose(0, 2, 3, 1),
        features,
        value_weight,
    )
    held = [pltpu.VMEM(x.shape, x.dtype) for x in inputs]
    held[5] = pltpu.VMEM((POINTS, rows), f32)
    held[6] = pltpu.VMEM((2, POINTS, rows), f32)
    place, *projected = pl.pallas_call(
        begin_kernel,
        out_shape=[jax.ShapeDtypeStruct((4 * POINTS, rows), f32)]
        + [jax.ShapeDtypeStruct((2, lines, AHD), bf16)] * 4,
        in_specs=[pl.BlockSpec(memory_space=pltpu.HBM)] * len(inputs),
        out_specs=vmem(5),
        scratch_shapes=held
        + [pltpu.VMEM((PARTS, lines, AHD), bf16), pltpu.SemaphoreType.DMA((12,))],
        name="begin",
        **params(60, 2 * lines * value_weight.size, 4 * MIB),
    )(*inputs)
    return place, projected


def hat(distance):
    return jnp.maximum(1.0 - jnp.abs(distance), 0.0)


def sample_kernel(frames, rows_each, place_ref, *refs):
    values, outs, (spread, stacked) = refs[:PARTS], refs[PARTS:-2], refs[-2:]
    count = place_ref.shape[1]
    block = frames * rows_each * GRID
    core = lax.axis_index("mc")
    first = (time_index() * frames).astype(f32)
    cell = lax.broadcasted_iota(jnp.int32, (GRID, count), 0).astype(f32)
    frame_at = [place_ref[k : k + 1, :] for k in range(POINTS)]
    row_at = [place_ref[POINTS + k : POINTS + k + 1, :] for k in range(POINTS)]
    share = [place_ref[3 * POINTS + k : 3 * POINTS + k + 1, :] for k in range(POINTS)]
    column_hat = [
        hat(cell - place_ref[2 * POINTS + k : 2 * POINTS + k + 1, :]) for k in range(POINTS)
    ]
    frame_hat = [
        [share[k] * hat(first + float(f) - frame_at[k]) for k in range(POINTS)]
        for f in range(frames)
    ]
    for step in range(PARTS):
        top = gathered_source(step) * rows_each
        row_hat = [
            [hat((top + r).astype(f32) - row_at[k]) for k in range(POINTS)]
            for r in range(rows_each)
        ]
        pieces = []
        for f in range(frames):
            for r in range(rows_each):
                total = (frame_hat[f][0] * row_hat[r][0]) * column_hat[0]
                for k in range(1, POINTS):
                    total = total + (frame_hat[f][k] * row_hat[r][k]) * column_hat[k]
                pieces.append(total)
        spread[step * block : (step + 1) * block, :] = jnp.concatenate(pieces, axis=0).astype(bf16)
        stacked[step * block : (step + 1) * block, :] = values[step][core]
    turned_values = stacked[...].T
    rows = count // len(outs)
    for k, out_ref in enumerate(outs):
        out = dot(turned_values, spread[:, k * rows : (k + 1) * rows])
        out_ref[...] = out.T.astype(out_ref.dtype)


def sample(values, place, frames, kinds):
    _, rows, width = values[0].shape
    count = place.shape[1]
    rows_each = GRID // PARTS
    return pl.pallas_call(
        lambda *refs: sample_kernel(frames, rows_each, *refs),
        out_shape=[jax.ShapeDtypeStruct((count // len(kinds), width), kind) for kind in kinds],
        in_specs=vmem(1 + PARTS),
        out_specs=vmem(len(kinds)),
        scratch_shapes=[
            pltpu.VMEM((PARTS * rows, count), bf16),
            pltpu.VMEM((PARTS * rows, width), bf16),
        ],
        name="sample_values",
        **params(12, 2 * PARTS * rows * width * count, 4 * PARTS * rows * width),
    )(place, *values)


def model_kernel(*refs):
    samples, weights = refs[:PARTS], refs[PARTS : PARTS + 2]
    queries_ref, project_ref, gain_ref, out_ref = refs[PARTS + 2 :]
    width = project_ref.shape[0]
    mixed = queries_ref[...].astype(f32)
    for place in range(PARTS):
        top = place // 2 * AHD
        mixed = mixed + dot(samples[place][...], weights[place % 2][top : top + AHD, :])
    visual = lax.dot_general(
        mixed.astype(bf16),
        project_ref[...],
        (((1,), (1,)), ((), ())),
        preferred_element_type=f32,
    )
    squares = jnp.sum(visual * visual, axis=1, keepdims=True)
    high = squares.astype(bf16).astype(f32)
    middle = (squares - high).astype(bf16).astype(f32)
    low = squares - high - middle
    scaled = visual * gain_ref[...]
    out_ref[:, :width] = scaled.astype(bf16)
    extra = out_ref.shape[1] - width
    lane = lax.broadcasted_iota(jnp.int32, (scaled.shape[0], extra), 1)
    terms = jnp.where(lane == 0, high, jnp.where(lane == 1, middle, jnp.where(lane == 2, low, 0.0)))
    out_ref[:, width:] = terms.astype(bf16)


def model_columns(samples, weights, queries, project_weight, gain):
    rows, width = queries.shape[0], project_weight.shape[1]
    return pl.pallas_call(
        model_kernel,
        out_shape=jax.ShapeDtypeStruct((rows, width + 64), bf16),
        in_specs=vmem(PARTS + 5),
        out_specs=pl.BlockSpec(memory_space=pltpu.VMEM),
        name="model_columns",
        **params(8, 2 * rows * queries.shape[1] * (queries.shape[1] + width), 4 * MIB),
    )(*samples, *weights, queries, project_weight.T, gain)


def turn(vectors, cosine, sine):
    return vectors * cosine + pltpu.roll(vectors, HD // 2, 1) * sine


def heads_kernel(width, turned_part, weight_hbm, bias, cosine, sine, *refs):
    blocks, (out_ref, weight_ref, arriving) = refs[:PARTS], refs[PARTS:]
    copies = []
    for place in range(PARTS):
        lines = pl.ds(pl.multiple_of(gathered_source(place) * width, 64), width)
        copies.append(
            pltpu.make_async_copy(
                weight_hbm.at[lines, :], weight_ref.at[place], arriving.at[place]
            )
        )
        copies[place].start()
    rows = blocks[0].shape[0]
    squares = jnp.zeros((rows, blocks[0].shape[1] - width), f32)
    for block in blocks:
        squares = squares + block[:, width:].astype(f32)
    scale = jnp.sum(squares, axis=1, keepdims=True) / float(PARTS * width)
    scale = lax.rsqrt(scale + epsilon)
    product = jnp.zeros((rows, weight_ref.shape[2]), f32)
    for place in range(PARTS):
        copies[place].wait()
        product = product + dot(blocks[place][:, :width], weight_ref[place])
    product = product * scale + bias[...]
    for head in range(weight_ref.shape[2] // HD):
        plain = product[:, head * HD : (head + 1) * HD]
        vectors = turn(plain, cosine[...], sine[...])
        if turned_part is not None:
            vectors = jnp.where(part_index() < turned_part, vectors, plain)
        out_ref[head] = vectors.astype(bf16)


def head_states(blocks, width, weight, bias, tables, turned_part=None):
    rows = blocks[0].shape[0]
    specs = vmem(4 + PARTS)
    specs[0] = pl.BlockSpec(memory_space=pltpu.HBM)
    return pl.pallas_call(
        lambda *refs: heads_kernel(width, turned_part, *refs),
        out_shape=jax.ShapeDtypeStruct((weight.shape[1] // HD, rows, HD), bf16),
        in_specs=specs,
        out_specs=pl.BlockSpec(memory_space=pltpu.VMEM),
        scratch_shapes=[
            pltpu.VMEM((PARTS, width, weight.shape[1]), bf16),
            pltpu.SemaphoreType.DMA((PARTS,)),
        ],
        name="head_states",
        **params(51, 2 * rows * weight.size, 2 * MIB + 2 * weight.size),
    )(weight, bias[None], *tables, *blocks)


def attend_kernel(step, last, own_ref, other_ref, *refs):
    count = 1 if step == 0 or last else 2
    blocks = refs[:count]
    outs, (peak, total, mix) = refs[count + (3 if step else 0) : -3], refs[-3:]
    heads, rows, _ = own_ref.shape
    part, core = part_index(), lax.axis_index("mc")
    here, half = lax.axis_index("tz"), lax.axis_index("tx")
    factor = HD ** (-0.5) * 1.4426950408889634

    def update(slot, query_ref, head, used):
        query = query_ref[head]
        pieces = []
        for block in used:
            scores = (
                lax.dot_general(
                    query, block[:, :HD], (((1,), (1,)), ((), ())), preferred_element_type=f32
                )
                * factor
            )
            if step == 0:
                row = lax.broadcasted_iota(jnp.int32, scores.shape, 0) + half * rows
                column = lax.broadcasted_iota(jnp.int32, scores.shape, 1)
                column = jnp.where(column < rows, column + half * rows, column - half * rows)
                scores = jnp.where(column <= row, scores, masked)
            pieces += [scores[:, lo : lo + HD] for lo in range(0, scores.shape[1], HD)]
        top = pieces[0]
        for piece in pieces[1:]:
            top = jnp.maximum(top, piece)
        new = jnp.max(top, axis=1, keepdims=True)
        if step:
            old = peak[slot]
            new = jnp.maximum(old, new)
        else:
            new = jnp.broadcast_to(new, (rows, HD))
        weights = [jnp.exp2(piece - new) for piece in pieces]
        added = weights[0]
        for piece in weights[1:]:
            added = added + piece
        each = len(pieces) // len(used)
        mixed = None
        for k, block in enumerate(used):
            part_weights = jnp.concatenate(
                [piece.astype(bf16) for piece in weights[k * each : (k + 1) * each]], axis=1
            )
            product = dot(part_weights, block[:, HD:])
            mixed = product if mixed is None else mixed + product
        peak[slot] = new
        if step:
            shrink = jnp.exp2(old - new)
            total[slot] = total[slot] * shrink + added
            mix[slot] = mix[slot] * shrink + mixed
        else:
            total[slot] = added
            mix[slot] = mixed

    for side, query_ref in enumerate((own_ref, other_ref)):
        owner = part if side == 0 else part + 1 - 2 * core

        def one_head(head, _):
            group = lax.div(owner * heads + head, GROUP)
            mine = lax.rem(group, 2) == core
            slot = side * heads + head
            if step == 0:
                pl.when(mine)(lambda: update(slot, query_ref, head, blocks))
                return _
            up = mine & (here >= step)
            if count == 1:
                pl.when(up)(lambda: update(slot, query_ref, head, blocks))
            else:
                down = mine & (here + step >= RING)
                pl.when(up & down)(lambda: update(slot, query_ref, head, blocks))
                pl.when(up & jnp.logical_not(down))(
                    lambda: update(slot, query_ref, head, blocks[:1])
                )
                pl.when(down & jnp.logical_not(up))(
                    lambda: update(slot, query_ref, head, blocks[1:])
                )
            return _

        lax.fori_loop(0, heads, one_head, 0)
        if last:
            for head in range(heads):
                mine = lax.rem(lax.div(owner * heads + head, GROUP), 2) == core
                slot = side * heads + head
                share = 1.0 / jnp.sum(total[slot], axis=1, keepdims=True)
                outs[side][:, head * HD : (head + 1) * HD] = jnp.where(
                    mine, mix[slot] * share, 0.0
                ).astype(bf16)


def attend(step, last, own, other, blocks, state):
    heads, rows, _ = own.shape
    shape = jax.ShapeDtypeStruct((2 * heads, rows, HD), f32)
    results = [jax.ShapeDtypeStruct((rows, heads * HD), bf16)] * 2 if last else []
    first = 2 + len(blocks)
    outs = pl.pallas_call(
        lambda *refs: attend_kernel(step, last, *refs),
        out_shape=results + [shape] * 3,
        in_specs=vmem(first + len(state)),
        out_specs=vmem(len(results) + 3),
        input_output_aliases={first + k: len(results) + k for k in range(len(state))},
        name="attend",
        **params(16, 8 * heads * rows * 512 * HD * len(blocks), 4 * MIB),
    )(own, other, *blocks, *state)
    return outs[:2] if last else outs


def own_group(x, meanwhile):
    part = part_index()
    blocks = [x] + [lax.ppermute(x, "my", turned(4, step)) for step in (1, 2, 3)]
    blocks, meanwhile = lax.optimization_barrier((blocks, meanwhile))
    nearest = jnp.where((part == 5) | (part >= 6), blocks[2], blocks[1])
    key = jnp.where(part == 0, blocks[0], nearest)
    value = jnp.where(part == 0, blocks[2], jnp.where(part >= 5, blocks[0], blocks[3]))
    return jnp.concatenate([key, value], axis=1), meanwhile


def local(
    features,
    queries,
    anchor_frame,
    anchor_patch,
    time_offset,
    space_offset,
    value_weight,
    point_weight,
    point_bias,
    output_weight,
    project_weight,
    norm_gain,
    query_weight,
    query_bias,
    cache_weight,
    cache_bias,
):
    part = part_index()
    frames, patches, feature_width = features.shape
    rows = queries.shape[0]
    model_width = project_weight.shape[1]

    place, projected = begin(
        queries,
        point_weight,
        point_bias,
        anchor_frame,
        anchor_patch,
        time_offset,
        space_offset,
        features.reshape(frames * patches, feature_width),
        value_weight,
    )
    sibling = turned(2, 1)
    across = [(2 * z + 1, 2 * z + 2) for z in range(RING - 1)]
    across += [(target, source) for source, target in across]
    nearby = [lax.ppermute(place, TM, across), lax.ppermute(place, "tx", sibling)]
    columns = [projected[0]] + [
        lax.ppermute(projected[step], "my", turned(4, step)) for step in (1, 2, 3)
    ]
    columns, nearby, output_weight = lax.optimization_barrier((columns, nearby, output_weight))
    values = []
    for block in columns:
        values += [block, lax.ppermute(block, "mc", turned(2, 1))]
    weight_columns = [output_weight] + [
        lax.ppermute(output_weight, "my", turned(4, step)) for step in (1, 2, 3)
    ]
    far, near = sample(values, jnp.concatenate(nearby, axis=1), frames, (bf16, bf16))
    (mine,) = sample(values, place, frames, (f32,))
    far = lax.ppermute(far, TM, across)
    near = lax.ppermute(near, "tx", sibling)
    far, near, mine, weight_columns = lax.optimization_barrier((far, near, mine, weight_columns))
    weights = jnp.concatenate(weight_columns, axis=0)
    weights = [weights, lax.ppermute(weights, "mc", turned(2, 1))]
    sampled = (mine + far.astype(f32) + near.astype(f32)).astype(bf16)
    sampled_columns = [sampled] + [
        lax.ppermute(sampled, "my", turned(4, step)) for step in (1, 2, 3)
    ]
    sampled_columns, weights = lax.optimization_barrier((sampled_columns, weights))
    samples = []
    for block in sampled_columns:
        samples += [block, lax.ppermute(block, "mc", turned(2, 1))]

    columns = model_columns(samples, weights, queries, project_weight, norm_gain[None])
    blocks = gather_blocks(columns)

    positions = (time_index() * rows + jnp.arange(rows, dtype=jnp.int32)).astype(f32)
    frequency = rope_base ** (-2.0 * jnp.arange(HD // 2, dtype=f32) / HD)
    angles = positions[:, None] * frequency[None, :]
    cosine, sine = jnp.cos(angles), jnp.sin(angles)
    cosine = jnp.concatenate([cosine, cosine], axis=1)
    sine = jnp.concatenate([-sine, sine], axis=1)
    tables = (cosine, sine)
    key_value = head_states(blocks, model_width, cache_weight, cache_bias, tables, KVH)[0]
    turned_queries = head_states(blocks, model_width, query_weight, query_bias, tables)
    own, turned_queries = own_group(key_value, turned_queries)
    other = lax.ppermute(own, "tx", turned(2, 1))
    heads = query_weight.shape[1] // HD
    other_queries = lax.ppermute(turned_queries, "mc", turned(2, 1))
    other, other_queries = lax.optimization_barrier((other, other_queries))

    up = down = jnp.concatenate([own, other], axis=0)
    state = ()
    for step in range(RING // 2 + 1):
        last = step == RING // 2
        blocks = [up] if step == 0 or last else [up, down]
        if not last:
            if step > 0:
                up, down, state = lax.optimization_barrier((up, down, state))
            pairs = [(i, i + 1) for i in range(step, RING - 1)]
            up = lax.ppermute(up, "tz", pairs)
            if step + 1 < RING // 2:
                down = lax.ppermute(down, "tz", turned(RING, -1))
        state = attend(step, last, turned_queries, other_queries, blocks, state)
    mixed, others = state
    others = lax.ppermute(others, "mc", turned(2, 1))
    attention = []
    for head in range(heads):
        mine = lax.rem((part * heads + head) // GROUP, 2) == lax.axis_index("mc")
        lanes = slice(head * HD, (head + 1) * HD)
        attention.append(jnp.where(mine, mixed[:, lanes], others[:, lanes]))
    attention = jnp.concatenate(attention, axis=1)
    return (attention, key_value)


def solution(mesh):
    finer = Mesh(
        mesh.devices.reshape(mesh.shape["dp"], RING, 2, 4, 2), ("dp", "tz", "tx", "my", "mc")
    )
    time = ("dp", *TM)
    placed = (
        P(time, MP, None),
        P(time, None),
        P(time),
        P(time),
        P(time, None, None),
        P(None, time, None, None),
        P(),
        P(),
        P(),
        P(MP, None),
        P(None, MP),
        P(MP),
        P(None, MP),
        P(MP),
        P(None, MP),
        P(MP),
    )
    return jax.shard_map(
        local,
        mesh=finer,
        in_specs=placed,
        out_specs=(P(time, MP), P(time, MP)),
        check_vma=False,
    )
```

```python
import jax
import jax.numpy as jnp
from jax import lax
from jax.experimental import pallas as pl
from jax.experimental.pallas import tpu as pltpu
from jax.sharding import Mesh
from jax.sharding import PartitionSpec as P

AH = 8
AHD = 128
POINTS = 4
GRID = 24
KVH = 4
HD = 128
GROUP = 7
PARTS = 8
RING = 8
TM = ("tz", "tx")
MP = ("my", "mc")

rope_base = 1000000.0
epsilon = 1e-06
masked = -1e30
MIB = 1 << 20

f32 = jnp.float32
bf16 = jnp.bfloat16


def part_index():
    return lax.axis_index("my") * 2 + lax.axis_index("mc")


def time_index():
    return lax.axis_index("tz") * 2 + lax.axis_index("tx")


def gathered_source(place):
    step, other = place // 2, place % 2
    row = lax.rem(lax.axis_index("my") - step + 4, 4)
    core = lax.axis_index("mc")
    return row * 2 + (1 - core if other else core)


def turned(size, step):
    return [(i, (i + step) % size) for i in range(size)]


def gather_blocks(x):
    columns = [x] + [lax.ppermute(x, "my", turned(4, step)) for step in (1, 2, 3)]
    blocks = []
    for block in columns:
        blocks += [block, lax.ppermute(block, "mc", turned(2, 1))]
    return blocks


def dot(a, b):
    return jnp.dot(a, b, preferred_element_type=f32)


def params(mib, flops=0, read=0):
    return dict(
        compiler_params=pltpu.CompilerParams(vmem_limit_bytes=mib * MIB),
        cost_estimate=pl.CostEstimate(flops=flops, bytes_accessed=read, transcendentals=0),
    )


def vmem(count):
    return [pl.BlockSpec(memory_space=pltpu.VMEM)] * count


def begin_kernel(*refs):
    inputs, place_ref, outs = refs[:9], refs[9], refs[10:14]
    arrived, (held, arriving) = refs[14:23], refs[23:]
    part = part_index()
    copies = []
    for k, (source, target) in enumerate(zip(inputs, arrived)):
        if k == 5:
            source = source.at[part]
        if k == 6:
            source = source.at[:, part]
        copies.append(pltpu.make_async_copy(source, target, arriving.at[k]))
    for copy in copies:
        copy.start()
    queries, point_weight, bias, frame, patch, time, space, features, value_weight = arrived
    for copy in copies[:7]:
        copy.wait()
    logits = lax.dot_general(
        point_weight[...], queries[...], (((1,), (1,)), ((), ())), preferred_element_type=f32
    )
    columns = AH * POINTS
    on_diagonal = lax.broadcasted_iota(jnp.int32, (columns, columns), 0) == (
        lax.broadcasted_iota(jnp.int32, (columns, columns), 1)
    )
    logits = logits + jnp.sum(jnp.where(on_diagonal, bias[...], 0.0), axis=1, keepdims=True)
    own = logits[:POINTS]
    for head in range(1, AH):
        own = jnp.where(part == head, logits[head * POINTS : (head + 1) * POINTS], own)
    share = jnp.exp(own - jnp.max(own, axis=0, keepdims=True))
    share = share / jnp.sum(share, axis=0, keepdims=True)
    patch = patch[...].astype(f32)
    row = jnp.floor((patch + 0.5) * (1.0 / GRID))
    place_ref[0:POINTS] = frame[...].astype(f32) + time[...]
    place_ref[POINTS : 2 * POINTS] = row + space[0]
    place_ref[2 * POINTS : 3 * POINTS] = (patch - row * GRID) + space[1]
    place_ref[3 * POINTS :] = share
    for copy in copies[7:]:
        copy.wait()
    for pair in range(PARTS // 2):
        both = dot(features[...], value_weight[:, pair * 256 : pair * 256 + 256]).astype(bf16)
        held[2 * pair] = both[:, :AHD]
        held[2 * pair + 1] = both[:, AHD:]
    chip = lax.axis_index("my")
    for step in range(4):
        first = 2 * lax.rem(chip + step, 4)
        outs[step][0] = held[first]
        outs[step][1] = held[first + 1]


def begin(queries, weight, bias, frame, patch, time_offset, space_offset, features, value_weight):
    rows, lines = queries.shape[0], features.shape[0]
    inputs = (
        queries,
        weight.T,
        bias[None],
        frame[None],
        patch[None],
        time_offset.transpose(1, 2, 0),
        space_offset.transpose(0, 2, 3, 1),
        features,
        value_weight,
    )
    held = [pltpu.VMEM(x.shape, x.dtype) for x in inputs]
    held[5] = pltpu.VMEM((POINTS, rows), f32)
    held[6] = pltpu.VMEM((2, POINTS, rows), f32)
    place, *projected = pl.pallas_call(
        begin_kernel,
        out_shape=[jax.ShapeDtypeStruct((4 * POINTS, rows), f32)]
        + [jax.ShapeDtypeStruct((2, lines, AHD), bf16)] * 4,
        in_specs=[pl.BlockSpec(memory_space=pltpu.HBM)] * len(inputs),
        out_specs=vmem(5),
        scratch_shapes=held
        + [pltpu.VMEM((PARTS, lines, AHD), bf16), pltpu.SemaphoreType.DMA((len(inputs),))],
        name="begin",
        **params(60, 2 * lines * value_weight.size, 4 * MIB),
    )(*inputs)
    return place, projected


def hat(distance):
    return jnp.maximum(1.0 - jnp.abs(distance), 0.0)


def sample_kernel(frames, rows_each, place_ref, *refs):
    values, outs, (spread, stacked) = refs[:PARTS], refs[PARTS:-2], refs[-2:]
    count = place_ref.shape[1]
    block = frames * rows_each * GRID
    core = lax.axis_index("mc")
    first = (time_index() * frames).astype(f32)
    cell = lax.broadcasted_iota(jnp.int32, (GRID, count), 0).astype(f32)
    frame_at = [place_ref[k : k + 1, :] for k in range(POINTS)]
    row_at = [place_ref[POINTS + k : POINTS + k + 1, :] for k in range(POINTS)]
    share = [place_ref[3 * POINTS + k : 3 * POINTS + k + 1, :] for k in range(POINTS)]
    column_hat = [
        hat(cell - place_ref[2 * POINTS + k : 2 * POINTS + k + 1, :]) for k in range(POINTS)
    ]
    frame_hat = [
        [share[k] * hat(first + float(f) - frame_at[k]) for k in range(POINTS)]
        for f in range(frames)
    ]
    for step in range(PARTS):
        top = gathered_source(step) * rows_each
        row_hat = [
            [hat((top + r).astype(f32) - row_at[k]) for k in range(POINTS)]
            for r in range(rows_each)
        ]
        pieces = []
        for f in range(frames):
            for r in range(rows_each):
                total = (frame_hat[f][0] * row_hat[r][0]) * column_hat[0]
                for k in range(1, POINTS):
                    total = total + (frame_hat[f][k] * row_hat[r][k]) * column_hat[k]
                pieces.append(total)
        spread[step * block : (step + 1) * block, :] = jnp.concatenate(pieces, axis=0).astype(bf16)
        stacked[step * block : (step + 1) * block, :] = values[step][core]
    turned_values = stacked[...].T
    rows = count // len(outs)
    for k, out_ref in enumerate(outs):
        out = dot(turned_values, spread[:, k * rows : (k + 1) * rows])
        out_ref[...] = out.T.astype(out_ref.dtype)


def sample(values, place, frames, kinds):
    _, rows, width = values[0].shape
    count = place.shape[1]
    rows_each = GRID // PARTS
    return pl.pallas_call(
        lambda *refs: sample_kernel(frames, rows_each, *refs),
        out_shape=[jax.ShapeDtypeStruct((count // len(kinds), width), kind) for kind in kinds],
        in_specs=vmem(1 + PARTS),
        out_specs=vmem(len(kinds)),
        scratch_shapes=[
            pltpu.VMEM((PARTS * rows, count), bf16),
            pltpu.VMEM((PARTS * rows, width), bf16),
        ],
        name="sample_values",
        **params(12, 2 * PARTS * rows * width * count, 4 * PARTS * rows * width),
    )(place, *values)


def model_kernel(*refs):
    samples, weights = refs[:PARTS], refs[PARTS : PARTS + 2]
    queries_ref, project_ref, gain_ref, out_ref = refs[PARTS + 2 :]
    width = project_ref.shape[0]
    mixed = queries_ref[...].astype(f32)
    for place in range(PARTS):
        top = place // 2 * AHD
        mixed = mixed + dot(samples[place][...], weights[place % 2][top : top + AHD, :])
    visual = lax.dot_general(
        mixed.astype(bf16),
        project_ref[...],
        (((1,), (1,)), ((), ())),
        preferred_element_type=f32,
    )
    squares = jnp.sum(visual * visual, axis=1, keepdims=True)
    high = squares.astype(bf16).astype(f32)
    middle = (squares - high).astype(bf16).astype(f32)
    low = squares - high - middle
    scaled = visual * gain_ref[...]
    out_ref[:, :width] = scaled.astype(bf16)
    extra = out_ref.shape[1] - width
    lane = lax.broadcasted_iota(jnp.int32, (scaled.shape[0], extra), 1)
    terms = jnp.where(lane == 0, high, jnp.where(lane == 1, middle, jnp.where(lane == 2, low, 0.0)))
    out_ref[:, width:] = terms.astype(bf16)


def model_columns(samples, weights, queries, project_weight, gain):
    rows, width = queries.shape[0], project_weight.shape[1]
    return pl.pallas_call(
        model_kernel,
        out_shape=jax.ShapeDtypeStruct((rows, width + 64), bf16),
        in_specs=vmem(PARTS + 5),
        out_specs=pl.BlockSpec(memory_space=pltpu.VMEM),
        name="model_columns",
        **params(8, 2 * rows * queries.shape[1] * (queries.shape[1] + width), 4 * MIB),
    )(*samples, *weights, queries, project_weight.T, gain)


def turn(vectors, cosine, sine):
    return vectors * cosine + pltpu.roll(vectors, HD // 2, 1) * sine


def heads_kernel(width, turned_part, weight_ref, bias, cosine, sine, *refs):
    blocks, out_ref = refs[:PARTS], refs[PARTS]
    rows = blocks[0].shape[0]
    squares = jnp.zeros((rows, blocks[0].shape[1] - width), f32)
    for block in blocks:
        squares = squares + block[:, width:].astype(f32)
    scale = jnp.sum(squares, axis=1, keepdims=True) / float(PARTS * width)
    scale = lax.rsqrt(scale + epsilon)
    product = jnp.zeros((rows, weight_ref.shape[1]), f32)
    for place in range(PARTS):
        lines = pl.ds(pl.multiple_of(gathered_source(place) * width, 64), width)
        product = product + dot(blocks[place][:, :width], weight_ref[lines, :])
    product = product * scale + bias[...]
    for head in range(weight_ref.shape[1] // HD):
        plain = product[:, head * HD : (head + 1) * HD]
        vectors = turn(plain, cosine[...], sine[...])
        if turned_part is not None:
            vectors = jnp.where(part_index() < turned_part, vectors, plain)
        out_ref[head] = vectors.astype(bf16)


def head_states(blocks, width, weight, bias, tables, grant, turned_part=None):
    rows = blocks[0].shape[0]
    return pl.pallas_call(
        lambda *refs: heads_kernel(width, turned_part, *refs),
        out_shape=jax.ShapeDtypeStruct((weight.shape[1] // HD, rows, HD), bf16),
        in_specs=vmem(4 + PARTS),
        out_specs=pl.BlockSpec(memory_space=pltpu.VMEM),
        name="head_states",
        **params(grant, 2 * rows * weight.size, 2 * MIB + 2 * weight.size),
    )(weight, bias[None], *tables, *blocks)


def attend_kernel(step, last, own_ref, other_ref, *refs):
    count = 1 if step == 0 or last else 2
    blocks = refs[:count]
    outs, (peak, total, mix) = refs[count + (3 if step else 0) : -3], refs[-3:]
    heads, rows, _ = own_ref.shape
    part, core = part_index(), lax.axis_index("mc")
    here, half = lax.axis_index("tz"), lax.axis_index("tx")
    factor = HD ** (-0.5) * 1.4426950408889634

    def update(slot, query_ref, head, used):
        query = query_ref[head]
        pieces = []
        for block in used:
            scores = (
                lax.dot_general(
                    query, block[:, :HD], (((1,), (1,)), ((), ())), preferred_element_type=f32
                )
                * factor
            )
            if step == 0:
                row = lax.broadcasted_iota(jnp.int32, scores.shape, 0) + half * rows
                column = lax.broadcasted_iota(jnp.int32, scores.shape, 1)
                column = jnp.where(column < rows, column + half * rows, column - half * rows)
                scores = jnp.where(column <= row, scores, masked)
            pieces += [scores[:, lo : lo + HD] for lo in range(0, scores.shape[1], HD)]
        top = pieces[0]
        for piece in pieces[1:]:
            top = jnp.maximum(top, piece)
        new = jnp.max(top, axis=1, keepdims=True)
        if step:
            old = peak[slot]
            new = jnp.maximum(old, new)
        else:
            new = jnp.broadcast_to(new, (rows, HD))
        weights = [jnp.exp2(piece - new) for piece in pieces]
        added = weights[0]
        for piece in weights[1:]:
            added = added + piece
        each = len(pieces) // len(used)
        mixed = None
        for k, block in enumerate(used):
            part_weights = jnp.concatenate(
                [piece.astype(bf16) for piece in weights[k * each : (k + 1) * each]], axis=1
            )
            product = dot(part_weights, block[:, HD:])
            mixed = product if mixed is None else mixed + product
        peak[slot] = new
        if step:
            shrink = jnp.exp2(old - new)
            total[slot] = total[slot] * shrink + added
            mix[slot] = mix[slot] * shrink + mixed
        else:
            total[slot] = added
            mix[slot] = mixed

    for side, query_ref in enumerate((own_ref, other_ref)):
        owner = part if side == 0 else part + 1 - 2 * core

        def one_head(head, _):
            group = lax.div(owner * heads + head, GROUP)
            mine = lax.rem(group, 2) == core
            slot = side * heads + head
            if step == 0:
                pl.when(mine)(lambda: update(slot, query_ref, head, blocks))
                return _
            up = mine & (here >= step)
            if count == 1:
                pl.when(up)(lambda: update(slot, query_ref, head, blocks))
            else:
                down = mine & (here + step >= RING)
                pl.when(up & down)(lambda: update(slot, query_ref, head, blocks))
                pl.when(up & jnp.logical_not(down))(
                    lambda: update(slot, query_ref, head, blocks[:1])
                )
                pl.when(down & jnp.logical_not(up))(
                    lambda: update(slot, query_ref, head, blocks[1:])
                )
            return _

        lax.fori_loop(0, heads, one_head, 0)
        if last:
            for head in range(heads):
                mine = lax.rem(lax.div(owner * heads + head, GROUP), 2) == core
                slot = side * heads + head
                share = 1.0 / jnp.sum(total[slot], axis=1, keepdims=True)
                outs[side][:, head * HD : (head + 1) * HD] = jnp.where(
                    mine, mix[slot] * share, 0.0
                ).astype(bf16)


def attend(step, last, own, other, blocks, state):
    heads, rows, _ = own.shape
    shape = jax.ShapeDtypeStruct((2 * heads, rows, HD), f32)
    results = [jax.ShapeDtypeStruct((rows, heads * HD), bf16)] * 2 if last else []
    first = 2 + len(blocks)
    outs = pl.pallas_call(
        lambda *refs: attend_kernel(step, last, *refs),
        out_shape=results + [shape] * 3,
        in_specs=vmem(first + len(state)),
        out_specs=vmem(len(results) + 3),
        input_output_aliases={first + k: len(results) + k for k in range(len(state))},
        name="attend",
        **params(16, 8 * heads * rows * 512 * HD * len(blocks), 4 * MIB),
    )(own, other, *blocks, *state)
    return outs[:2] if last else outs


def own_group(x, meanwhile):
    part = part_index()
    blocks = [x] + [lax.ppermute(x, "my", turned(4, step)) for step in (1, 2, 3)]
    blocks, meanwhile = lax.optimization_barrier((blocks, meanwhile))
    nearest = jnp.where((part == 5) | (part >= 6), blocks[2], blocks[1])
    key = jnp.where(part == 0, blocks[0], nearest)
    value = jnp.where(part == 0, blocks[2], jnp.where(part >= 5, blocks[0], blocks[3]))
    return jnp.concatenate([key, value], axis=1), meanwhile


def local(
    features,
    queries,
    anchor_frame,
    anchor_patch,
    time_offset,
    space_offset,
    value_weight,
    point_weight,
    point_bias,
    output_weight,
    project_weight,
    norm_gain,
    query_weight,
    query_bias,
    cache_weight,
    cache_bias,
):
    part = part_index()
    frames, patches, feature_width = features.shape
    rows = queries.shape[0]
    model_width = project_weight.shape[1]

    place, projected = begin(
        queries,
        point_weight,
        point_bias,
        anchor_frame,
        anchor_patch,
        time_offset,
        space_offset,
        features.reshape(frames * patches, feature_width),
        value_weight,
    )
    sibling = turned(2, 1)
    across = [(2 * z + 1, 2 * z + 2) for z in range(RING - 1)]
    across += [(target, source) for source, target in across]
    nearby = [lax.ppermute(place, TM, across), lax.ppermute(place, "tx", sibling)]
    columns = [projected[0]] + [
        lax.ppermute(projected[step], "my", turned(4, step)) for step in (1, 2, 3)
    ]
    columns, output_weight = lax.optimization_barrier((columns, output_weight))
    columns[0], nearby = lax.optimization_barrier((columns[0], nearby))
    values = []
    for block in columns:
        values += [block, lax.ppermute(block, "mc", turned(2, 1))]
    weight_columns = [output_weight] + [
        lax.ppermute(output_weight, "my", turned(4, step)) for step in (1, 2, 3)
    ]
    far, near = sample(values, jnp.concatenate(nearby, axis=1), frames, (bf16, bf16))
    (mine,) = sample(values, place, frames, (f32,))
    far = lax.ppermute(far, TM, across)
    near = lax.ppermute(near, "tx", sibling)
    far, near, mine, weight_columns = lax.optimization_barrier((far, near, mine, weight_columns))
    weights = jnp.concatenate(weight_columns, axis=0)
    weights = [weights, lax.ppermute(weights, "mc", turned(2, 1))]
    sampled = (mine + far.astype(f32) + near.astype(f32)).astype(bf16)
    sampled_columns = [sampled] + [
        lax.ppermute(sampled, "my", turned(4, step)) for step in (1, 2, 3)
    ]
    sampled_columns, weights = lax.optimization_barrier((sampled_columns, weights))
    samples = []
    for block in sampled_columns:
        samples += [block, lax.ppermute(block, "mc", turned(2, 1))]

    columns = model_columns(samples, weights, queries, project_weight, norm_gain[None])
    blocks = gather_blocks(columns)

    positions = (time_index() * rows + jnp.arange(rows, dtype=jnp.int32)).astype(f32)
    frequency = rope_base ** (-2.0 * jnp.arange(HD // 2, dtype=f32) / HD)
    angles = positions[:, None] * frequency[None, :]
    cosine, sine = jnp.cos(angles), jnp.sin(angles)
    cosine = jnp.concatenate([cosine, cosine], axis=1)
    sine = jnp.concatenate([-sine, sine], axis=1)
    tables = (cosine, sine)
    key_value = head_states(blocks, model_width, cache_weight, cache_bias, tables, 44, KVH)[0]
    turned_queries = head_states(blocks, model_width, query_weight, query_bias, tables, 44)
    own, turned_queries = own_group(key_value, turned_queries)
    other = lax.ppermute(own, "tx", turned(2, 1))
    heads = query_weight.shape[1] // HD
    other_queries = lax.ppermute(turned_queries, "mc", turned(2, 1))
    other, other_queries = lax.optimization_barrier((other, other_queries))

    up = down = jnp.concatenate([own, other], axis=0)
    state = ()
    for step in range(RING // 2 + 1):
        last = step == RING // 2
        blocks = [up] if step == 0 or last else [up, down]
        if not last:
            if step > 0:
                up, down, state = lax.optimization_barrier((up, down, state))
            pairs = [(i, i + 1) for i in range(step, RING - 1)]
            up = lax.ppermute(up, "tz", pairs)
            if step + 1 < RING // 2:
                down = lax.ppermute(down, "tz", turned(RING, -1))
        state = attend(step, last, turned_queries, other_queries, blocks, state)
    mixed, others = state
    others = lax.ppermute(others, "mc", turned(2, 1))
    attention = []
    for head in range(heads):
        mine = lax.rem((part * heads + head) // GROUP, 2) == lax.axis_index("mc")
        lanes = slice(head * HD, (head + 1) * HD)
        attention.append(jnp.where(mine, mixed[:, lanes], others[:, lanes]))
    attention = jnp.concatenate(attention, axis=1)
    return (attention, key_value)


def solution(mesh):
    finer = Mesh(
        mesh.devices.reshape(mesh.shape["dp"], RING, 2, 4, 2), ("dp", "tz", "tx", "my", "mc")
    )
    time = ("dp", *TM)
    placed = (
        P(time, MP, None),
        P(time, None),
        P(time),
        P(time),
        P(time, None, None),
        P(None, time, None, None),
        P(),
        P(),
        P(),
        P(MP, None),
        P(None, MP),
        P(MP),
        P(None, MP),
        P(MP),
        P(None, MP),
        P(MP),
    )
    return jax.shard_map(
        local,
        mesh=finer,
        in_specs=placed,
        out_specs=(P(time, MP), P(time, MP)),
        check_vma=False,
    )
```

```python
import jax
import jax.numpy as jnp
from jax import lax
from jax.experimental import pallas as pl
from jax.experimental.pallas import tpu as pltpu
from jax.sharding import Mesh
from jax.sharding import PartitionSpec as P

AH = 8
AHD = 128
POINTS = 4
GRID = 24
KVH = 4
HD = 128
GROUP = 7
PARTS = 8
RING = 8
TM = ("tz", "tx")
MP = ("my", "mc")

rope_base = 1000000.0
epsilon = 1e-06
masked = -1e30
MIB = 1 << 20

f32 = jnp.float32
bf16 = jnp.bfloat16


def part_index():
    return lax.axis_index("my") * 2 + lax.axis_index("mc")


def time_index():
    return lax.axis_index("tz") * 2 + lax.axis_index("tx")


def gathered_source(place):
    step, other = place // 2, place % 2
    row = lax.rem(lax.axis_index("my") - step + 4, 4)
    core = lax.axis_index("mc")
    return row * 2 + (1 - core if other else core)


def turned(size, step):
    return [(i, (i + step) % size) for i in range(size)]


def gather_blocks(x):
    columns = [x] + [lax.ppermute(x, "my", turned(4, step)) for step in (1, 2, 3)]
    blocks = []
    for block in columns:
        blocks += [block, lax.ppermute(block, "mc", turned(2, 1))]
    return blocks


def dot(a, b):
    return jnp.dot(a, b, preferred_element_type=f32)


def params(mib, flops=0, read=0):
    return dict(
        compiler_params=pltpu.CompilerParams(vmem_limit_bytes=mib * MIB),
        cost_estimate=pl.CostEstimate(flops=flops, bytes_accessed=read, transcendentals=0),
    )


def vmem(count):
    return [pl.BlockSpec(memory_space=pltpu.VMEM)] * count


def begin_kernel(*refs):
    inputs, place_ref, outs = refs[:9], refs[9], refs[10:14]
    arrived, (held, arriving) = refs[14:23], refs[23:]
    part = part_index()
    copies = []
    for k, (source, target) in enumerate(zip(inputs, arrived)):
        if k == 5:
            source = source.at[part]
        if k == 6:
            source = source.at[:, part]
        copies.append(pltpu.make_async_copy(source, target, arriving.at[k]))
    for copy in copies:
        copy.start()
    queries, point_weight, bias, frame, patch, time, space, features, value_weight = arrived
    for copy in copies[:7]:
        copy.wait()
    logits = lax.dot_general(
        point_weight[...], queries[...], (((1,), (1,)), ((), ())), preferred_element_type=f32
    )
    columns = AH * POINTS
    on_diagonal = lax.broadcasted_iota(jnp.int32, (columns, columns), 0) == (
        lax.broadcasted_iota(jnp.int32, (columns, columns), 1)
    )
    logits = logits + jnp.sum(jnp.where(on_diagonal, bias[...], 0.0), axis=1, keepdims=True)
    own = logits[:POINTS]
    for head in range(1, AH):
        own = jnp.where(part == head, logits[head * POINTS : (head + 1) * POINTS], own)
    share = jnp.exp(own - jnp.max(own, axis=0, keepdims=True))
    share = share / jnp.sum(share, axis=0, keepdims=True)
    patch = patch[...].astype(f32)
    row = jnp.floor((patch + 0.5) * (1.0 / GRID))
    place_ref[0:POINTS] = frame[...].astype(f32) + time[...]
    place_ref[POINTS : 2 * POINTS] = row + space[0]
    place_ref[2 * POINTS : 3 * POINTS] = (patch - row * GRID) + space[1]
    place_ref[3 * POINTS :] = share
    for copy in copies[7:]:
        copy.wait()
    for pair in range(PARTS // 2):
        both = dot(features[...], value_weight[:, pair * 256 : pair * 256 + 256]).astype(bf16)
        held[2 * pair] = both[:, :AHD]
        held[2 * pair + 1] = both[:, AHD:]
    chip = lax.axis_index("my")
    for step in range(4):
        first = 2 * lax.rem(chip + step, 4)
        outs[step][0] = held[first]
        outs[step][1] = held[first + 1]


def begin(queries, weight, bias, frame, patch, time_offset, space_offset, features, value_weight):
    rows, lines = queries.shape[0], features.shape[0]
    inputs = (
        queries,
        weight.T,
        bias[None],
        frame[None],
        patch[None],
        time_offset.transpose(1, 2, 0),
        space_offset.transpose(0, 2, 3, 1),
        features,
        value_weight,
    )
    held = [pltpu.VMEM(x.shape, x.dtype) for x in inputs]
    held[5] = pltpu.VMEM((POINTS, rows), f32)
    held[6] = pltpu.VMEM((2, POINTS, rows), f32)
    place, *projected = pl.pallas_call(
        begin_kernel,
        out_shape=[jax.ShapeDtypeStruct((4 * POINTS, rows), f32)]
        + [jax.ShapeDtypeStruct((2, lines, AHD), bf16)] * 4,
        in_specs=[pl.BlockSpec(memory_space=pltpu.HBM)] * len(inputs),
        out_specs=vmem(5),
        scratch_shapes=held
        + [pltpu.VMEM((PARTS, lines, AHD), bf16), pltpu.SemaphoreType.DMA((len(inputs),))],
        name="begin",
        **params(60, 2 * lines * value_weight.size, 4 * MIB),
    )(*inputs)
    return place, projected


def hat(distance):
    return jnp.maximum(1.0 - jnp.abs(distance), 0.0)


def sample_kernel(frames, rows_each, place_ref, *refs):
    values, outs, (spread, stacked) = refs[:PARTS], refs[PARTS:-2], refs[-2:]
    count = place_ref.shape[1]
    block = frames * rows_each * GRID
    core = lax.axis_index("mc")
    first = (time_index() * frames).astype(f32)
    cell = lax.broadcasted_iota(jnp.int32, (GRID, count), 0).astype(f32)
    frame_at = [place_ref[k : k + 1, :] for k in range(POINTS)]
    row_at = [place_ref[POINTS + k : POINTS + k + 1, :] for k in range(POINTS)]
    share = [place_ref[3 * POINTS + k : 3 * POINTS + k + 1, :] for k in range(POINTS)]
    column_hat = [
        hat(cell - place_ref[2 * POINTS + k : 2 * POINTS + k + 1, :]) for k in range(POINTS)
    ]
    frame_hat = [
        [share[k] * hat(first + float(f) - frame_at[k]) for k in range(POINTS)]
        for f in range(frames)
    ]
    for step in range(PARTS):
        top = gathered_source(step) * rows_each
        row_hat = [
            [hat((top + r).astype(f32) - row_at[k]) for k in range(POINTS)]
            for r in range(rows_each)
        ]
        pieces = []
        for f in range(frames):
            for r in range(rows_each):
                total = (frame_hat[f][0] * row_hat[r][0]) * column_hat[0]
                for k in range(1, POINTS):
                    total = total + (frame_hat[f][k] * row_hat[r][k]) * column_hat[k]
                pieces.append(total)
        spread[step * block : (step + 1) * block, :] = jnp.concatenate(pieces, axis=0).astype(bf16)
        stacked[step * block : (step + 1) * block, :] = values[step][core]
    turned_values = stacked[...].T
    rows = count // len(outs)
    for k, out_ref in enumerate(outs):
        out = dot(turned_values, spread[:, k * rows : (k + 1) * rows])
        out_ref[...] = out.T.astype(out_ref.dtype)


def sample(values, place, frames, kinds):
    _, rows, width = values[0].shape
    count = place.shape[1]
    rows_each = GRID // PARTS
    return pl.pallas_call(
        lambda *refs: sample_kernel(frames, rows_each, *refs),
        out_shape=[jax.ShapeDtypeStruct((count // len(kinds), width), kind) for kind in kinds],
        in_specs=vmem(1 + PARTS),
        out_specs=vmem(len(kinds)),
        scratch_shapes=[
            pltpu.VMEM((PARTS * rows, count), bf16),
            pltpu.VMEM((PARTS * rows, width), bf16),
        ],
        name="sample_values",
        **params(12, 2 * PARTS * rows * width * count, 4 * PARTS * rows * width),
    )(place, *values)


def model_kernel(*refs):
    samples, weights = refs[:PARTS], refs[PARTS : PARTS + 2]
    queries_ref, project_ref, gain_ref, out_ref = refs[PARTS + 2 :]
    width = project_ref.shape[0]
    mixed = queries_ref[...].astype(f32)
    for place in range(PARTS):
        top = place // 2 * AHD
        mixed = mixed + dot(samples[place][...], weights[place % 2][top : top + AHD, :])
    visual = lax.dot_general(
        mixed.astype(bf16),
        project_ref[...],
        (((1,), (1,)), ((), ())),
        preferred_element_type=f32,
    )
    squares = jnp.sum(visual * visual, axis=1, keepdims=True)
    high = squares.astype(bf16).astype(f32)
    middle = (squares - high).astype(bf16).astype(f32)
    low = squares - high - middle
    scaled = visual * gain_ref[...]
    out_ref[:, :width] = scaled.astype(bf16)
    extra = out_ref.shape[1] - width
    lane = lax.broadcasted_iota(jnp.int32, (scaled.shape[0], extra), 1)
    terms = jnp.where(lane == 0, high, jnp.where(lane == 1, middle, jnp.where(lane == 2, low, 0.0)))
    out_ref[:, width:] = terms.astype(bf16)


def model_columns(samples, weights, queries, project_weight, gain):
    rows, width = queries.shape[0], project_weight.shape[1]
    return pl.pallas_call(
        model_kernel,
        out_shape=jax.ShapeDtypeStruct((rows, width + 64), bf16),
        in_specs=vmem(PARTS + 5),
        out_specs=pl.BlockSpec(memory_space=pltpu.VMEM),
        name="model_columns",
        **params(8, 2 * rows * queries.shape[1] * (queries.shape[1] + width), 4 * MIB),
    )(*samples, *weights, queries, project_weight.T, gain)


def turn(vectors, cosine, sine):
    return vectors * cosine + pltpu.roll(vectors, HD // 2, 1) * sine


def heads_kernel(width, turned_part, weight_ref, bias, cosine, sine, *refs):
    blocks, out_ref = refs[:PARTS], refs[PARTS]
    rows = blocks[0].shape[0]
    squares = jnp.zeros((rows, blocks[0].shape[1] - width), f32)
    for block in blocks:
        squares = squares + block[:, width:].astype(f32)
    scale = jnp.sum(squares, axis=1, keepdims=True) / float(PARTS * width)
    scale = lax.rsqrt(scale + epsilon)
    product = jnp.zeros((rows, weight_ref.shape[1]), f32)
    for place in range(PARTS):
        lines = pl.ds(pl.multiple_of(gathered_source(place) * width, 64), width)
        product = product + dot(blocks[place][:, :width], weight_ref[lines, :])
    product = product * scale + bias[...]
    for head in range(weight_ref.shape[1] // HD):
        plain = product[:, head * HD : (head + 1) * HD]
        vectors = turn(plain, cosine[...], sine[...])
        if turned_part is not None:
            vectors = jnp.where(part_index() < turned_part, vectors, plain)
        out_ref[head] = vectors.astype(bf16)


def head_states(blocks, width, weight, bias, tables, grant, turned_part=None):
    rows = blocks[0].shape[0]
    return pl.pallas_call(
        lambda *refs: heads_kernel(width, turned_part, *refs),
        out_shape=jax.ShapeDtypeStruct((weight.shape[1] // HD, rows, HD), bf16),
        in_specs=vmem(4 + PARTS),
        out_specs=pl.BlockSpec(memory_space=pltpu.VMEM),
        name="head_states",
        **params(grant, 2 * rows * weight.size, 2 * MIB + 2 * weight.size),
    )(weight, bias[None], *tables, *blocks)


def attend_kernel(step, last, own_ref, other_ref, *refs):
    count = 1 if step == 0 or last else 2
    blocks = refs[:count]
    outs, (peak, total, mix) = refs[count + (3 if step else 0) : -3], refs[-3:]
    heads, rows, _ = own_ref.shape
    part, core = part_index(), lax.axis_index("mc")
    here, half = lax.axis_index("tz"), lax.axis_index("tx")
    factor = HD ** (-0.5) * 1.4426950408889634

    def update(slot, query_ref, head, used):
        query = query_ref[head]
        pieces = []
        for block in used:
            scores = (
                lax.dot_general(
                    query, block[:, :HD], (((1,), (1,)), ((), ())), preferred_element_type=f32
                )
                * factor
            )
            if step == 0:
                row = lax.broadcasted_iota(jnp.int32, scores.shape, 0) + half * rows
                column = lax.broadcasted_iota(jnp.int32, scores.shape, 1)
                column = jnp.where(column < rows, column + half * rows, column - half * rows)
                scores = jnp.where(column <= row, scores, masked)
            pieces += [scores[:, lo : lo + HD] for lo in range(0, scores.shape[1], HD)]
        top = pieces[0]
        for piece in pieces[1:]:
            top = jnp.maximum(top, piece)
        new = jnp.max(top, axis=1, keepdims=True)
        if step:
            old = peak[slot]
            new = jnp.maximum(old, new)
        else:
            new = jnp.broadcast_to(new, (rows, HD))
        weights = [jnp.exp2(piece - new) for piece in pieces]
        added = weights[0]
        for piece in weights[1:]:
            added = added + piece
        each = len(pieces) // len(used)
        mixed = None
        for k, block in enumerate(used):
            part_weights = jnp.concatenate(
                [piece.astype(bf16) for piece in weights[k * each : (k + 1) * each]], axis=1
            )
            product = dot(part_weights, block[:, HD:])
            mixed = product if mixed is None else mixed + product
        peak[slot] = new
        if step:
            shrink = jnp.exp2(old - new)
            total[slot] = total[slot] * shrink + added
            mix[slot] = mix[slot] * shrink + mixed
        else:
            total[slot] = added
            mix[slot] = mixed

    for side, query_ref in enumerate((own_ref, other_ref)):
        owner = part if side == 0 else part + 1 - 2 * core

        def one_head(head, _):
            group = lax.div(owner * heads + head, GROUP)
            mine = lax.rem(group, 2) == core
            slot = side * heads + head
            if step == 0:
                pl.when(mine)(lambda: update(slot, query_ref, head, blocks))
                return _
            up = mine & (here >= step)
            if count == 1:
                pl.when(up)(lambda: update(slot, query_ref, head, blocks))
            else:
                down = mine & (here + step >= RING)
                pl.when(up & down)(lambda: update(slot, query_ref, head, blocks))
                pl.when(up & jnp.logical_not(down))(
                    lambda: update(slot, query_ref, head, blocks[:1])
                )
                pl.when(down & jnp.logical_not(up))(
                    lambda: update(slot, query_ref, head, blocks[1:])
                )
            return _

        lax.fori_loop(0, heads, one_head, 0)
        if last:
            for head in range(heads):
                mine = lax.rem(lax.div(owner * heads + head, GROUP), 2) == core
                slot = side * heads + head
                share = 1.0 / jnp.sum(total[slot], axis=1, keepdims=True)
                outs[side][:, head * HD : (head + 1) * HD] = jnp.where(
                    mine, mix[slot] * share, 0.0
                ).astype(bf16)


def attend(step, last, own, other, blocks, state):
    heads, rows, _ = own.shape
    shape = jax.ShapeDtypeStruct((2 * heads, rows, HD), f32)
    results = [jax.ShapeDtypeStruct((rows, heads * HD), bf16)] * 2 if last else []
    first = 2 + len(blocks)
    outs = pl.pallas_call(
        lambda *refs: attend_kernel(step, last, *refs),
        out_shape=results + [shape] * 3,
        in_specs=vmem(first + len(state)),
        out_specs=vmem(len(results) + 3),
        input_output_aliases={first + k: len(results) + k for k in range(len(state))},
        name="attend",
        **params(16, 8 * heads * rows * 512 * HD * len(blocks), 4 * MIB),
    )(own, other, *blocks, *state)
    return outs[:2] if last else outs


def own_group(x, meanwhile):
    part = part_index()
    blocks = [x] + [lax.ppermute(x, "my", turned(4, step)) for step in (1, 2, 3)]
    blocks, meanwhile = lax.optimization_barrier((blocks, meanwhile))
    nearest = jnp.where((part == 5) | (part >= 6), blocks[2], blocks[1])
    key = jnp.where(part == 0, blocks[0], nearest)
    value = jnp.where(part == 0, blocks[2], jnp.where(part >= 5, blocks[0], blocks[3]))
    return jnp.concatenate([key, value], axis=1), meanwhile


def local(
    features,
    queries,
    anchor_frame,
    anchor_patch,
    time_offset,
    space_offset,
    value_weight,
    point_weight,
    point_bias,
    output_weight,
    project_weight,
    norm_gain,
    query_weight,
    query_bias,
    cache_weight,
    cache_bias,
):
    part = part_index()
    frames, patches, feature_width = features.shape
    rows = queries.shape[0]
    model_width = project_weight.shape[1]

    place, projected = begin(
        queries,
        point_weight,
        point_bias,
        anchor_frame,
        anchor_patch,
        time_offset,
        space_offset,
        features.reshape(frames * patches, feature_width),
        value_weight,
    )
    sibling = turned(2, 1)
    across = [(2 * z + 1, 2 * z + 2) for z in range(RING - 1)]
    across += [(target, source) for source, target in across]
    nearby = [lax.ppermute(place, TM, across), lax.ppermute(place, "tx", sibling)]
    columns = [projected[0]] + [
        lax.ppermute(projected[step], "my", turned(4, step)) for step in (1, 2, 3)
    ]
    columns, output_weight = lax.optimization_barrier((columns, output_weight))
    columns[0], nearby = lax.optimization_barrier((columns[0], nearby))
    values = []
    for block in columns:
        values += [block, lax.ppermute(block, "mc", turned(2, 1))]
    weight_columns = [output_weight] + [
        lax.ppermute(output_weight, "my", turned(4, step)) for step in (1, 2, 3)
    ]
    far, near = sample(values, jnp.concatenate(nearby, axis=1), frames, (bf16, bf16))
    (mine,) = sample(values, place, frames, (f32,))
    far = lax.ppermute(far, TM, across)
    near = lax.ppermute(near, "tx", sibling)
    far, near, mine, weight_columns = lax.optimization_barrier((far, near, mine, weight_columns))
    weights = jnp.concatenate(weight_columns, axis=0)
    weights = [weights, lax.ppermute(weights, "mc", turned(2, 1))]
    sampled = (mine + far.astype(f32) + near.astype(f32)).astype(bf16)
    sampled_columns = [sampled] + [
        lax.ppermute(sampled, "my", turned(4, step)) for step in (1, 2, 3)
    ]
    sampled_columns, weights = lax.optimization_barrier((sampled_columns, weights))
    samples = []
    for block in sampled_columns:
        samples += [block, lax.ppermute(block, "mc", turned(2, 1))]

    columns = model_columns(samples, weights, queries, project_weight, norm_gain[None])
    blocks = gather_blocks(columns)

    positions = (time_index() * rows + jnp.arange(rows, dtype=jnp.int32)).astype(f32)
    frequency = rope_base ** (-2.0 * jnp.arange(HD // 2, dtype=f32) / HD)
    angles = positions[:, None] * frequency[None, :]
    cosine, sine = jnp.cos(angles), jnp.sin(angles)
    cosine = jnp.concatenate([cosine, cosine], axis=1)
    sine = jnp.concatenate([-sine, sine], axis=1)
    tables = (cosine, sine)
    key_value = head_states(blocks, model_width, cache_weight, cache_bias, tables, 44, KVH)[0]
    turned_queries = head_states(blocks, model_width, query_weight, query_bias, tables, 44)
    own, turned_queries = own_group(key_value, turned_queries)
    other = lax.ppermute(own, "tx", turned(2, 1))
    heads = query_weight.shape[1] // HD
    other_queries = lax.ppermute(turned_queries, "mc", turned(2, 1))

    up = down = jnp.concatenate([own, other], axis=0)
    state = ()
    for step in range(RING // 2 + 1):
        last = step == RING // 2
        blocks = [up] if step == 0 or last else [up, down]
        if not last:
            if step > 0:
                up, down, state = lax.optimization_barrier((up, down, state))
            pairs = [(i, i + 1) for i in range(step, RING - 1)]
            up = lax.ppermute(up, "tz", pairs)
            if step + 1 < RING // 2:
                down = lax.ppermute(down, "tz", turned(RING, -1))
        state = attend(step, last, turned_queries, other_queries, blocks, state)
    mixed, others = state
    others = lax.ppermute(others, "mc", turned(2, 1))
    attention = []
    for head in range(heads):
        mine = lax.rem((part * heads + head) // GROUP, 2) == lax.axis_index("mc")
        lanes = slice(head * HD, (head + 1) * HD)
        attention.append(jnp.where(mine, mixed[:, lanes], others[:, lanes]))
    attention = jnp.concatenate(attention, axis=1)
    return (attention, key_value)


def solution(mesh):
    finer = Mesh(
        mesh.devices.reshape(mesh.shape["dp"], RING, 2, 4, 2), ("dp", "tz", "tx", "my", "mc")
    )
    time = ("dp", *TM)
    placed = (
        P(time, MP, None),
        P(time, None),
        P(time),
        P(time),
        P(time, None, None),
        P(None, time, None, None),
        P(),
        P(),
        P(),
        P(MP, None),
        P(None, MP),
        P(MP),
        P(None, MP),
        P(MP),
        P(None, MP),
        P(MP),
    )
    return jax.shard_map(
        local,
        mesh=finer,
        in_specs=placed,
        out_specs=(P(time, MP), P(time, MP)),
        check_vma=False,
    )
```

```python
import jax
import jax.numpy as jnp
from jax import lax
from jax.experimental import pallas as pl
from jax.experimental.pallas import tpu as pltpu
from jax.sharding import Mesh
from jax.sharding import PartitionSpec as P

AH = 8
AHD = 128
POINTS = 4
GRID = 24
KVH = 4
HD = 128
GROUP = 7
PARTS = 8
RING = 8
TM = ("tz", "tx")
MP = ("my", "mc")

rope_base = 1000000.0
epsilon = 1e-06
masked = -1e30
MIB = 1 << 20

f32 = jnp.float32
bf16 = jnp.bfloat16


def part_index():
    return lax.axis_index("my") * 2 + lax.axis_index("mc")


def time_index():
    return lax.axis_index("tz") * 2 + lax.axis_index("tx")


def gathered_source(place):
    step, other = place // 2, place % 2
    row = lax.rem(lax.axis_index("my") - step + 4, 4)
    core = lax.axis_index("mc")
    return row * 2 + (1 - core if other else core)


def turned(size, step):
    return [(i, (i + step) % size) for i in range(size)]


def gather_blocks(x):
    columns = [x] + [lax.ppermute(x, "my", turned(4, step)) for step in (1, 2, 3)]
    blocks = []
    for block in columns:
        blocks += [block, lax.ppermute(block, "mc", turned(2, 1))]
    return blocks


def dot(a, b):
    return jnp.dot(a, b, preferred_element_type=f32)


def params(mib, flops=0, read=0):
    return dict(
        compiler_params=pltpu.CompilerParams(vmem_limit_bytes=mib * MIB),
        cost_estimate=pl.CostEstimate(flops=flops, bytes_accessed=read, transcendentals=0),
    )


def vmem(count):
    return [pl.BlockSpec(memory_space=pltpu.VMEM)] * count


def begin_kernel(*refs):
    inputs, place_ref, outs = refs[:9], refs[9], refs[10:14]
    arrived, (held, arriving) = refs[14:23], refs[23:]
    part = part_index()
    copies = []
    for k, (source, target) in enumerate(zip(inputs, arrived)):
        if k == 5:
            source = source.at[part]
        if k == 6:
            source = source.at[:, part]
        copies.append(pltpu.make_async_copy(source, target, arriving.at[k]))
    for copy in copies:
        copy.start()
    queries, point_weight, bias, frame, patch, time, space, features, value_weight = arrived
    for copy in copies[:7]:
        copy.wait()
    logits = lax.dot_general(
        point_weight[...], queries[...], (((1,), (1,)), ((), ())), preferred_element_type=f32
    )
    columns = AH * POINTS
    on_diagonal = lax.broadcasted_iota(jnp.int32, (columns, columns), 0) == (
        lax.broadcasted_iota(jnp.int32, (columns, columns), 1)
    )
    logits = logits + jnp.sum(jnp.where(on_diagonal, bias[...], 0.0), axis=1, keepdims=True)
    own = logits[:POINTS]
    for head in range(1, AH):
        own = jnp.where(part == head, logits[head * POINTS : (head + 1) * POINTS], own)
    share = jnp.exp(own - jnp.max(own, axis=0, keepdims=True))
    share = share / jnp.sum(share, axis=0, keepdims=True)
    patch = patch[...].astype(f32)
    row = jnp.floor((patch + 0.5) * (1.0 / GRID))
    place_ref[0:POINTS] = frame[...].astype(f32) + time[...]
    place_ref[POINTS : 2 * POINTS] = row + space[0]
    place_ref[2 * POINTS : 3 * POINTS] = (patch - row * GRID) + space[1]
    place_ref[3 * POINTS :] = share
    for copy in copies[7:]:
        copy.wait()
    for pair in range(PARTS // 2):
        both = dot(features[...], value_weight[:, pair * 256 : pair * 256 + 256]).astype(bf16)
        held[2 * pair] = both[:, :AHD]
        held[2 * pair + 1] = both[:, AHD:]
    chip = lax.axis_index("my")
    for step in range(4):
        first = 2 * lax.rem(chip + step, 4)
        outs[step][0] = held[first]
        outs[step][1] = held[first + 1]


def begin(queries, weight, bias, frame, patch, time_offset, space_offset, features, value_weight):
    rows, lines = queries.shape[0], features.shape[0]
    inputs = (
        queries,
        weight.T,
        bias[None],
        frame[None],
        patch[None],
        time_offset.transpose(1, 2, 0),
        space_offset.transpose(0, 2, 3, 1),
        features,
        value_weight,
    )
    held = [pltpu.VMEM(x.shape, x.dtype) for x in inputs]
    held[5] = pltpu.VMEM((POINTS, rows), f32)
    held[6] = pltpu.VMEM((2, POINTS, rows), f32)
    place, *projected = pl.pallas_call(
        begin_kernel,
        out_shape=[jax.ShapeDtypeStruct((4 * POINTS, rows), f32)]
        + [jax.ShapeDtypeStruct((2, lines, AHD), bf16)] * 4,
        in_specs=[pl.BlockSpec(memory_space=pltpu.HBM)] * len(inputs),
        out_specs=vmem(5),
        scratch_shapes=held
        + [pltpu.VMEM((PARTS, lines, AHD), bf16), pltpu.SemaphoreType.DMA((len(inputs),))],
        name="begin",
        **params(60, 2 * lines * value_weight.size, 4 * MIB),
    )(*inputs)
    return place, projected


def hat(distance):
    return jnp.maximum(1.0 - jnp.abs(distance), 0.0)


def sample_kernel(frames, rows_each, place_ref, *refs):
    values, outs, (spread, stacked) = refs[:PARTS], refs[PARTS:-2], refs[-2:]
    count = place_ref.shape[1]
    block = frames * rows_each * GRID
    core = lax.axis_index("mc")
    first = (time_index() * frames).astype(f32)
    cell = lax.broadcasted_iota(jnp.int32, (GRID, count), 0).astype(f32)
    frame_at = [place_ref[k : k + 1, :] for k in range(POINTS)]
    row_at = [place_ref[POINTS + k : POINTS + k + 1, :] for k in range(POINTS)]
    share = [place_ref[3 * POINTS + k : 3 * POINTS + k + 1, :] for k in range(POINTS)]
    column_hat = [
        hat(cell - place_ref[2 * POINTS + k : 2 * POINTS + k + 1, :]) for k in range(POINTS)
    ]
    frame_hat = [
        [share[k] * hat(first + float(f) - frame_at[k]) for k in range(POINTS)]
        for f in range(frames)
    ]
    for step in range(PARTS):
        top = gathered_source(step) * rows_each
        row_hat = [
            [hat((top + r).astype(f32) - row_at[k]) for k in range(POINTS)]
            for r in range(rows_each)
        ]
        pieces = []
        for f in range(frames):
            for r in range(rows_each):
                total = (frame_hat[f][0] * row_hat[r][0]) * column_hat[0]
                for k in range(1, POINTS):
                    total = total + (frame_hat[f][k] * row_hat[r][k]) * column_hat[k]
                pieces.append(total)
        spread[step * block : (step + 1) * block, :] = jnp.concatenate(pieces, axis=0).astype(bf16)
        stacked[step * block : (step + 1) * block, :] = values[step][core]
    turned_values = stacked[...].T
    rows = count // len(outs)
    for k, out_ref in enumerate(outs):
        out = dot(turned_values, spread[:, k * rows : (k + 1) * rows])
        out_ref[...] = out.T.astype(out_ref.dtype)


def sample(values, place, frames, kinds):
    _, rows, width = values[0].shape
    count = place.shape[1]
    rows_each = GRID // PARTS
    return pl.pallas_call(
        lambda *refs: sample_kernel(frames, rows_each, *refs),
        out_shape=[jax.ShapeDtypeStruct((count // len(kinds), width), kind) for kind in kinds],
        in_specs=vmem(1 + PARTS),
        out_specs=vmem(len(kinds)),
        scratch_shapes=[
            pltpu.VMEM((PARTS * rows, count), bf16),
            pltpu.VMEM((PARTS * rows, width), bf16),
        ],
        name="sample_values",
        **params(12, 2 * PARTS * rows * width * count, 4 * PARTS * rows * width),
    )(place, *values)


def model_kernel(*refs):
    samples, weights = refs[:PARTS], refs[PARTS : PARTS + 2]
    queries_ref, project_ref, gain_ref, out_ref = refs[PARTS + 2 :]
    width = project_ref.shape[0]
    mixed = queries_ref[...].astype(f32)
    for place in range(PARTS):
        top = place // 2 * AHD
        mixed = mixed + dot(samples[place][...], weights[place % 2][top : top + AHD, :])
    visual = lax.dot_general(
        mixed.astype(bf16),
        project_ref[...],
        (((1,), (1,)), ((), ())),
        preferred_element_type=f32,
    )
    squares = jnp.sum(visual * visual, axis=1, keepdims=True)
    high = squares.astype(bf16).astype(f32)
    middle = (squares - high).astype(bf16).astype(f32)
    low = squares - high - middle
    scaled = visual * gain_ref[...]
    out_ref[:, :width] = scaled.astype(bf16)
    extra = out_ref.shape[1] - width
    lane = lax.broadcasted_iota(jnp.int32, (scaled.shape[0], extra), 1)
    terms = jnp.where(lane == 0, high, jnp.where(lane == 1, middle, jnp.where(lane == 2, low, 0.0)))
    out_ref[:, width:] = terms.astype(bf16)


def model_columns(samples, weights, queries, project_weight, gain):
    rows, width = queries.shape[0], project_weight.shape[1]
    return pl.pallas_call(
        model_kernel,
        out_shape=jax.ShapeDtypeStruct((rows, width + 64), bf16),
        in_specs=vmem(PARTS + 5),
        out_specs=pl.BlockSpec(memory_space=pltpu.VMEM),
        name="model_columns",
        **params(8, 2 * rows * queries.shape[1] * (queries.shape[1] + width), 4 * MIB),
    )(*samples, *weights, queries, project_weight.T, gain)


def turn(vectors, cosine, sine):
    return vectors * cosine + pltpu.roll(vectors, HD // 2, 1) * sine


def heads_kernel(width, turned_part, weight_ref, bias, cosine, sine, *refs):
    blocks, out_ref = refs[:PARTS], refs[PARTS]
    rows = blocks[0].shape[0]
    squares = jnp.zeros((rows, blocks[0].shape[1] - width), f32)
    for block in blocks:
        squares = squares + block[:, width:].astype(f32)
    scale = jnp.sum(squares, axis=1, keepdims=True) / float(PARTS * width)
    scale = lax.rsqrt(scale + epsilon)
    product = jnp.zeros((rows, weight_ref.shape[1]), f32)
    for place in range(PARTS):
        lines = pl.ds(pl.multiple_of(gathered_source(place) * width, 64), width)
        product = product + dot(blocks[place][:, :width], weight_ref[lines, :])
    product = product * scale + bias[...]
    for head in range(weight_ref.shape[1] // HD):
        plain = product[:, head * HD : (head + 1) * HD]
        vectors = turn(plain, cosine[...], sine[...])
        if turned_part is not None:
            vectors = jnp.where(part_index() < turned_part, vectors, plain)
        out_ref[head] = vectors.astype(bf16)


def head_states(blocks, width, weight, bias, tables, grant, turned_part=None):
    rows = blocks[0].shape[0]
    return pl.pallas_call(
        lambda *refs: heads_kernel(width, turned_part, *refs),
        out_shape=jax.ShapeDtypeStruct((weight.shape[1] // HD, rows, HD), bf16),
        in_specs=vmem(4 + PARTS),
        out_specs=pl.BlockSpec(memory_space=pltpu.VMEM),
        name="head_states",
        **params(grant, 2 * rows * weight.size, 2 * MIB + 2 * weight.size),
    )(weight, bias[None], *tables, *blocks)


def attend_kernel(step, last, own_ref, other_ref, *refs):
    count = 1 if step == 0 or last else 2
    blocks = refs[:count]
    outs, (peak, total, mix) = refs[count + (3 if step else 0) : -3], refs[-3:]
    heads, rows, _ = own_ref.shape
    part, core = part_index(), lax.axis_index("mc")
    here, half = lax.axis_index("tz"), lax.axis_index("tx")
    factor = HD ** (-0.5) * 1.4426950408889634

    def update(slot, query_ref, head, used):
        query = query_ref[head]
        pieces = []
        for block in used:
            scores = (
                lax.dot_general(
                    query, block[:, :HD], (((1,), (1,)), ((), ())), preferred_element_type=f32
                )
                * factor
            )
            if step == 0:
                row = lax.broadcasted_iota(jnp.int32, scores.shape, 0) + half * rows
                column = lax.broadcasted_iota(jnp.int32, scores.shape, 1)
                column = jnp.where(column < rows, column + half * rows, column - half * rows)
                scores = jnp.where(column <= row, scores, masked)
            pieces += [scores[:, lo : lo + HD] for lo in range(0, scores.shape[1], HD)]
        top = pieces[0]
        for piece in pieces[1:]:
            top = jnp.maximum(top, piece)
        new = jnp.max(top, axis=1, keepdims=True)
        if step:
            old = peak[slot]
            new = jnp.maximum(old, new)
        else:
            new = jnp.broadcast_to(new, (rows, HD))
        weights = [jnp.exp2(piece - new) for piece in pieces]
        added = weights[0]
        for piece in weights[1:]:
            added = added + piece
        each = len(pieces) // len(used)
        mixed = None
        for k, block in enumerate(used):
            part_weights = jnp.concatenate(
                [piece.astype(bf16) for piece in weights[k * each : (k + 1) * each]], axis=1
            )
            product = dot(part_weights, block[:, HD:])
            mixed = product if mixed is None else mixed + product
        peak[slot] = new
        if step:
            shrink = jnp.exp2(old - new)
            total[slot] = total[slot] * shrink + added
            mix[slot] = mix[slot] * shrink + mixed
        else:
            total[slot] = added
            mix[slot] = mixed

    for side, query_ref in enumerate((own_ref, other_ref)):
        owner = part if side == 0 else part + 1 - 2 * core

        def one_head(head, _):
            group = lax.div(owner * heads + head, GROUP)
            mine = lax.rem(group, 2) == core
            slot = side * heads + head
            if step == 0:
                pl.when(mine)(lambda: update(slot, query_ref, head, blocks))
                return _
            up = mine & (here >= step)
            if count == 1:
                pl.when(up)(lambda: update(slot, query_ref, head, blocks))
            else:
                down = mine & (here + step >= RING)
                pl.when(up & down)(lambda: update(slot, query_ref, head, blocks))
                pl.when(up & jnp.logical_not(down))(
                    lambda: update(slot, query_ref, head, blocks[:1])
                )
                pl.when(down & jnp.logical_not(up))(
                    lambda: update(slot, query_ref, head, blocks[1:])
                )
            return _

        lax.fori_loop(0, heads, one_head, 0)
        if last:
            for head in range(heads):
                mine = lax.rem(lax.div(owner * heads + head, GROUP), 2) == core
                slot = side * heads + head
                share = 1.0 / jnp.sum(total[slot], axis=1, keepdims=True)
                outs[side][:, head * HD : (head + 1) * HD] = jnp.where(
                    mine, mix[slot] * share, 0.0
                ).astype(bf16)


def attend(step, last, own, other, blocks, state):
    heads, rows, _ = own.shape
    shape = jax.ShapeDtypeStruct((2 * heads, rows, HD), f32)
    results = [jax.ShapeDtypeStruct((rows, heads * HD), bf16)] * 2 if last else []
    first = 2 + len(blocks)
    outs = pl.pallas_call(
        lambda *refs: attend_kernel(step, last, *refs),
        out_shape=results + [shape] * 3,
        in_specs=vmem(first + len(state)),
        out_specs=vmem(len(results) + 3),
        input_output_aliases={first + k: len(results) + k for k in range(len(state))},
        name="attend",
        **params(16, 8 * heads * rows * 512 * HD * len(blocks), 4 * MIB),
    )(own, other, *blocks, *state)
    return outs[:2] if last else outs


def own_group(x, meanwhile):
    part = part_index()
    blocks = [x] + [lax.ppermute(x, "my", turned(4, step)) for step in (1, 2, 3)]
    blocks, meanwhile = lax.optimization_barrier((blocks, meanwhile))
    nearest = jnp.where((part == 5) | (part >= 6), blocks[2], blocks[1])
    key = jnp.where(part == 0, blocks[0], nearest)
    value = jnp.where(part == 0, blocks[2], jnp.where(part >= 5, blocks[0], blocks[3]))
    return jnp.concatenate([key, value], axis=1), meanwhile


def local(
    features,
    queries,
    anchor_frame,
    anchor_patch,
    time_offset,
    space_offset,
    value_weight,
    point_weight,
    point_bias,
    output_weight,
    project_weight,
    norm_gain,
    query_weight,
    query_bias,
    cache_weight,
    cache_bias,
):
    part = part_index()
    frames, patches, feature_width = features.shape
    rows = queries.shape[0]
    model_width = project_weight.shape[1]

    place, projected = begin(
        queries,
        point_weight,
        point_bias,
        anchor_frame,
        anchor_patch,
        time_offset,
        space_offset,
        features.reshape(frames * patches, feature_width),
        value_weight,
    )
    sibling = turned(2, 1)
    across = [(2 * z + 1, 2 * z + 2) for z in range(RING - 1)]
    across += [(target, source) for source, target in across]
    nearby = [lax.ppermute(place, TM, across), lax.ppermute(place, "tx", sibling)]
    columns = [projected[0]] + [
        lax.ppermute(projected[step], "my", turned(4, step)) for step in (1, 2, 3)
    ]
    columns, output_weight = lax.optimization_barrier((columns, output_weight))
    columns[0], nearby = lax.optimization_barrier((columns[0], nearby))
    values = []
    for block in columns:
        values += [block, lax.ppermute(block, "mc", turned(2, 1))]
    weight_columns = [output_weight] + [
        lax.ppermute(output_weight, "my", turned(4, step)) for step in (1, 2, 3)
    ]
    far, near = sample(values, jnp.concatenate(nearby, axis=1), frames, (bf16, bf16))
    (mine,) = sample(values, place, frames, (f32,))
    far = lax.ppermute(far, TM, across)
    near = lax.ppermute(near, "tx", sibling)
    far, near, mine, weight_columns = lax.optimization_barrier((far, near, mine, weight_columns))
    weights = jnp.concatenate(weight_columns, axis=0)
    weights = [weights, lax.ppermute(weights, "mc", turned(2, 1))]
    sampled = (mine + far.astype(f32) + near.astype(f32)).astype(bf16)
    sampled_columns = [sampled] + [
        lax.ppermute(sampled, "my", turned(4, step)) for step in (1, 2, 3)
    ]
    sampled_columns, weights = lax.optimization_barrier((sampled_columns, weights))
    samples = []
    for block in sampled_columns:
        samples += [block, lax.ppermute(block, "mc", turned(2, 1))]

    columns = model_columns(samples, weights, queries, project_weight, norm_gain[None])
    blocks = gather_blocks(columns)

    positions = (time_index() * rows + jnp.arange(rows, dtype=jnp.int32)).astype(f32)
    frequency = rope_base ** (-2.0 * jnp.arange(HD // 2, dtype=f32) / HD)
    angles = positions[:, None] * frequency[None, :]
    cosine, sine = jnp.cos(angles), jnp.sin(angles)
    cosine = jnp.concatenate([cosine, cosine], axis=1)
    sine = jnp.concatenate([-sine, sine], axis=1)
    tables = (cosine, sine)
    key_value = head_states(blocks, model_width, cache_weight, cache_bias, tables, 44, KVH)[0]
    turned_queries = head_states(blocks, model_width, query_weight, query_bias, tables, 44)
    own, turned_queries = own_group(key_value, turned_queries)
    other = lax.ppermute(own, "tx", turned(2, 1))
    heads = query_weight.shape[1] // HD
    other_queries = lax.ppermute(turned_queries, "mc", turned(2, 1))

    up = down = jnp.concatenate([own, other], axis=0)
    state = ()
    for step in range(RING // 2 + 1):
        last = step == RING // 2
        blocks = [up] if step == 0 or last else [up, down]
        if not last:
            if step > 0:
                up, down, state = lax.optimization_barrier((up, down, state))
            pairs = [(i, i + 1) for i in range(step, RING - 1)]
            up = lax.ppermute(up, "tz", pairs)
            if step + 1 < RING // 2:
                pairs = [((o - step) % RING, (o - step - 1) % RING) for o in range(RING // 2 - 1)]
                down = lax.ppermute(down, "tz", pairs)
        state = attend(step, last, turned_queries, other_queries, blocks, state)
    mixed, others = state
    others = lax.ppermute(others, "mc", turned(2, 1))
    attention = []
    for head in range(heads):
        mine = lax.rem((part * heads + head) // GROUP, 2) == lax.axis_index("mc")
        lanes = slice(head * HD, (head + 1) * HD)
        attention.append(jnp.where(mine, mixed[:, lanes], others[:, lanes]))
    attention = jnp.concatenate(attention, axis=1)
    return (attention, key_value)


def solution(mesh):
    finer = Mesh(
        mesh.devices.reshape(mesh.shape["dp"], RING, 2, 4, 2), ("dp", "tz", "tx", "my", "mc")
    )
    time = ("dp", *TM)
    placed = (
        P(time, MP, None),
        P(time, None),
        P(time),
        P(time),
        P(time, None, None),
        P(None, time, None, None),
        P(),
        P(),
        P(),
        P(MP, None),
        P(None, MP),
        P(MP),
        P(None, MP),
        P(MP),
        P(None, MP),
        P(MP),
    )
    return jax.shard_map(
        local,
        mesh=finer,
        in_specs=placed,
        out_specs=(P(time, MP), P(time, MP)),
        check_vma=False,
    )
```
